32 devices in a mesh: ens: 2 (over x), lon: 8 (over z, y), lat: 2 (over core).
Axes of the slice: x: 2, y: 2, z: 4, core: 2. Of those that a mesh axis runs over, the one named last changes fastest.
Arguments:
- stream: float32 [6, 4, 24, 96, 512], P('ens', None, 'lat', 'lon'), parts along dimension 0, may hold values from -6 to 6
- region_ids: int32 [8, 24, 96], P('ens', 'lat', 'lon'), parts along dimension 0, may hold values from 0 to 2, as said below
- qkv_weight: bfloat16 [2, 512, 1536], replicated, may hold values from -0.25 to 0.25
- out_weight: bfloat16 [2, 512, 512], replicated, may hold values from -0.25 to 0.25
- up_weight: bfloat16 [2, 512, 2048], replicated, may hold values from -0.25 to 0.25
- down_weight: bfloat16 [2, 2048, 512], replicated, may hold values from -0.125 to 0.125
- norm_gain: float32 [2, 2, 512], replicated, may hold values from 0.5 to 1.5
- norm_bias: float32 [2, 2, 512], replicated, may hold values from -2 to 2
- logit_scale: float32 [2, 8], replicated, may hold values from 2 to 12
Outputs:
- mixed: float32 [6, 4, 24, 96, 512], P('ens', None, 'lat', 'lon'), parts along dimension 0
The draws below stay inside these ranges and needn't reach their ends.
There are 2 independent parts, one for each index of `ens`. The reference program is written for one: setup_inputs(seed, part) draws one part's arguments, and reference() takes and returns one part's arrays. A program takes and returns all parts, laid end to end along the dimension named above; an argument that names none is the same for every part. Nothing has to cross between parts.
Inputs may be any that keep to these rules, and one draw needn't show every extreme that they name: `region_ids`: within each window of the rolled frame the ids depend only on the longitude column: they are 0, 1, 2 in three contiguous runs of columns, each run one column or more, the same over all levels and latitude rows of the window.
All inputs are finite; a program needn't handle non-finite values.
Results may differ from the reference program's by a relative error of at most 0.008.
Values may be sent and summed in bfloat16 or wider, within the bound.
A program may use at most 128 MiB of HBM per device.

```python
import math
import jax
import jax.numpy as jnp
from jax import lax

D = 512
HEADS = 8
FF = 2048
SAMPLES = 3
LEVELS = 4
WIN_LAT = 6
WIN_LON = 12
LAT = 24
LON = 96


def draw_region_ids(key, part):
    lat_blocks = LAT // WIN_LAT
    lon_blocks = LON // WIN_LON
    first_key, second_key = jax.random.split(jax.random.fold_in(key, 11))
    first_cut = jax.random.randint(first_key, (lat_blocks, lon_blocks), 1, WIN_LON // 2 + 1)
    second_cut = jax.random.randint(second_key, (lat_blocks, lon_blocks), WIN_LON // 2 + 1, WIN_LON)
    inside = jnp.arange(WIN_LON, dtype=jnp.int32)
    ids = (inside[None, None, :] >= first_cut[..., None]).astype(jnp.int32) + (inside[None, None, :] >= second_cut[..., None]).astype(jnp.int32)
    grid = jnp.broadcast_to(ids[:, None, :, :], (lat_blocks, WIN_LAT, lon_blocks, WIN_LON)).reshape(LAT, LON)
    return jnp.broadcast_to(grid[None], (LEVELS, LAT, LON)).astype(jnp.int32)


def block_scale(key, shape, pieces, least, high):
    level = 1.0
    for axis_at, shards_of in pieces:
        draws = jax.random.uniform(jax.random.fold_in(jax.random.fold_in(key, 6), axis_at), (shards_of,), jnp.float32, least / len(pieces), high / len(pieces))
        level = level * jnp.repeat(jnp.exp(draws), shape[axis_at] // shards_of).reshape((-1,) + (1,) * (len(shape) - 1 - axis_at))
    return level


def scatter_about(stream_key, extent, scale, limit, pieces=(), kind=jnp.bfloat16):
    values = jax.random.normal(stream_key, extent, jnp.float32) * scale
    if len(pieces) > 0:
        values = block_scale(stream_key, extent, pieces, -0.22, 0.18) * values
    return jnp.clip(values, min=-limit, max=limit).astype(kind)


def setup_inputs(seed: int = 0, part: int = 0) -> dict:
    seeds = jax.random.split(jax.random.key(seed), 10)
    own_keys = jax.random.split(jax.random.fold_in(seeds[9], part), 10)
    return {
        "stream": scatter_about(own_keys[0], (SAMPLES, LEVELS, LAT, LON, D), 1.0, 6.0, ((2, 2), (3, 8)), jnp.float32),
        "region_ids": draw_region_ids(jax.random.fold_in(jax.random.fold_in(seeds[9], part), 71), part),
        "qkv_weight": scatter_about(seeds[2], (2, D, 3 * D), D ** -0.5, 0.25),
        "out_weight": scatter_about(seeds[3], (2, D, D), D ** -0.5, 0.25),
        "up_weight": scatter_about(seeds[4], (2, D, FF), D ** -0.5, 0.25),
        "down_weight": scatter_about(seeds[5], (2, FF, D), FF ** -0.5, 0.125),
        "norm_gain": jnp.clip(1.0 + 0.1 * jax.random.normal(seeds[6], (2, 2, D), jnp.float32), 0.5, 1.5),
        "norm_bias": scatter_about(seeds[7], (2, 2, D), 0.3, 2.0, (), jnp.float32),
        "logit_scale": jnp.clip(jnp.exp(jax.random.uniform(seeds[8], (2, HEADS), jnp.float32, math.log(2.0), math.log(12.0))), 2.0, 12.0),
    }


highest = lax.Precision.HIGHEST

def norm_rows(values, gain_row, bias_row):
    average = lax.optimization_barrier(jnp.mean(values, -1, keepdims=True))
    centred = values - average
    spread = lax.optimization_barrier(jnp.mean(centred * centred, -1, keepdims=True))
    return centred / jnp.sqrt(spread + 1e-05) * gain_row + bias_row

def to_windows(grid):
    sample_count, level_count, lat_rows, lon_cols, channels = grid.shape
    blocks = grid.reshape(sample_count, level_count, lat_rows // WIN_LAT, WIN_LAT, lon_cols // WIN_LON, WIN_LON, channels)
    blocks = blocks.transpose(0, 2, 4, 1, 3, 5, 6)
    return blocks.reshape(-1, level_count * WIN_LAT * WIN_LON, channels)

def from_windows(blocks, sample_count, level_count, lat_rows, lon_cols):
    channels = blocks.shape[-1]
    grid = blocks.reshape(sample_count, lat_rows // WIN_LAT, lon_cols // WIN_LON, level_count, WIN_LAT, WIN_LON, channels)
    grid = grid.transpose(0, 3, 1, 4, 2, 5, 6)
    return grid.reshape(sample_count, level_count, lat_rows, lon_cols, channels)

def attend(triple, region_key, scale_row, head_count):
    win_tokens, three_width = triple.shape
    width = three_width // 3
    head_dim = width // head_count
    parts = triple.reshape(win_tokens, 3, head_count, head_dim).astype(jnp.float32)
    query = parts[:, 0]
    key_part = parts[:, 1]
    values = parts[:, 2]
    query_unit = query / jnp.sqrt(lax.optimization_barrier(jnp.sum(query * query, -1, keepdims=True)) + 1e-06)
    key_unit = key_part / jnp.sqrt(lax.optimization_barrier(jnp.sum(key_part * key_part, -1, keepdims=True)) + 1e-06)
    scores = jnp.einsum('ihd,jhd->hij', query_unit, key_unit, precision=highest)
    scores = scores * scale_row[:, None, None]
    weights = jnp.exp(scores)
    if region_key is not None:
        allowed = region_key[:, None] == region_key[None, :]
        weights = jnp.where(allowed[None], weights, jnp.zeros_like(weights))
    shares = (weights / lax.optimization_barrier(jnp.sum(weights, -1, keepdims=True))).astype(jnp.bfloat16)
    result = jnp.einsum('hij,jhd->ihd', shares.astype(jnp.float32), values, precision=highest)
    return result.reshape(win_tokens, width).astype(jnp.bfloat16)

def swin_layer(stream, layer_index, region_key, qkv_weight, out_weight, up_weight, down_weight, norm_gain, norm_bias, logit_scale):
    sample_count, level_count, lat_rows, lon_cols, width = stream.shape
    operand = stream.astype(jnp.bfloat16)
    if region_key is not None:
        operand = jnp.roll(operand, (-(WIN_LAT // 2), -(WIN_LON // 2)), axis=(2, 3))
    triple = jnp.dot(operand.reshape(-1, width), qkv_weight[layer_index], preferred_element_type=jnp.float32)
    triple = triple.astype(jnp.bfloat16).reshape(sample_count, level_count, lat_rows, lon_cols, 3 * width)
    blocks = to_windows(triple)
    scale_row = logit_scale[layer_index]
    head_count = scale_row.shape[0]
    if region_key is not None:
        full_key = jnp.broadcast_to(region_key[None], (sample_count,) + region_key.shape)
        key_blocks = to_windows(full_key[..., None])[..., 0]

        def masked_group(pair):
            return attend(pair[0], pair[1], scale_row, head_count)
        result = lax.map(masked_group, (blocks, key_blocks))
    else:

        def plain_group(group):
            return attend(group, None, scale_row, head_count)
        result = lax.map(plain_group, blocks)
    attended = from_windows(result, sample_count, level_count, lat_rows, lon_cols)
    if region_key is not None:
        attended = jnp.roll(attended, (WIN_LAT // 2, WIN_LON // 2), axis=(2, 3))
    projected = jnp.dot(attended.reshape(-1, width), out_weight[layer_index], preferred_element_type=jnp.float32)
    after = stream.reshape(-1, width) + norm_rows(projected, norm_gain[layer_index, 0], norm_bias[layer_index, 0])
    hidden = jax.nn.gelu(jnp.dot(after.astype(jnp.bfloat16), up_weight[layer_index], preferred_element_type=jnp.float32))
    hidden = hidden.astype(jnp.bfloat16)
    mlp_out = jnp.dot(hidden, down_weight[layer_index], preferred_element_type=jnp.float32)
    after = after + norm_rows(mlp_out, norm_gain[layer_index, 1], norm_bias[layer_index, 1])
    return after.reshape(sample_count, level_count, lat_rows, lon_cols, width)

def reference(stream, region_ids, qkv_weight, out_weight, up_weight, down_weight, norm_gain, norm_bias, logit_scale):
    lat_rows = stream.shape[2]
    position = jnp.arange(lat_rows, dtype=jnp.int32)
    band = (position >= lat_rows - WIN_LAT).astype(jnp.int32) + (position >= lat_rows - WIN_LAT // 2).astype(jnp.int32)
    region_key = region_ids * 3 + band[None, :, None]
    first = swin_layer(stream, 0, None, qkv_weight, out_weight, up_weight, down_weight, norm_gain, norm_bias, logit_scale)
    return swin_layer(first, 1, region_key, qkv_weight, out_weight, up_weight, down_weight, norm_gain, norm_bias, logit_scale)
```

```python
import functools

import jax
import jax.numpy as jnp
from jax import lax
from jax.experimental import pallas as pl
from jax.experimental.pallas import tpu as pltpu
from jax.sharding import PartitionSpec as P

WIN_LAT = 6
WIN_LON = 12
HALF_LAT = WIN_LAT // 2
HALF_LON = WIN_LON // 2
LOG2E = 1.4426950408889634
VMEM_LIMIT = 60 * 1024 * 1024

f32 = jnp.float32
bf16 = jnp.bfloat16


MESH = pl.DeviceIdType.MESH


def mm(a, b):
    return jnp.dot(a, b, preferred_element_type=f32)


def attend_window(operand, qkv_weight, scale_row, bias_ref, head_dim, store):
    tokens, width = operand.shape
    group = 4 * head_dim
    pair = 2 * head_dim
    rest = pair // 4
    main = tokens - rest
    last = (((1,), (1,)), ((), ()))
    query = mm(operand, qkv_weight[:, :width])
    key = mm(operand, qkv_weight[:, width : 2 * width])
    value = mm(operand, qkv_weight[:, 2 * width :]).astype(bf16)
    d0 = lax.broadcasted_iota(jnp.int32, (group, group), 0)
    d1 = lax.broadcasted_iota(jnp.int32, (group, group), 1)
    same_head = lax.shift_right_logical(d0, head_dim.bit_length() - 1) == lax.shift_right_logical(
        d1, head_dim.bit_length() - 1
    )
    same_head = same_head.astype(f32).astype(bf16)

    def lanes(rows, cols, at, size):
        lane = lax.broadcasted_iota(jnp.int32, (rows, cols), 1)
        return ((lane >= at) & (lane < at + size)).astype(f32).astype(bf16)

    first_b = lanes(tokens, pair, 0, head_dim)
    second_b = lanes(tokens, pair, head_dim, head_dim)
    first = lax.broadcasted_iota(jnp.int32, (tokens, pair), 1) < head_dim

    def unit(part, scale):
        rounded = part.astype(bf16)
        inv = lax.rsqrt(mm(rounded * rounded, same_head) + 1e-06)
        if scale is not None:
            inv = inv * scale
        return (part * inv).astype(bf16)

    for g in range(width // group):
        at = g * group
        q = unit(query[:, at : at + group], scale_row[:, at : at + group])
        k = unit(key[:, at : at + group], None)
        v = value[:, at : at + group]
        k_rest = jnp.concatenate(
            [k[main:] * lanes(rest, group, h * head_dim, head_dim) for h in range(4)], axis=0
        )
        rest_score = lax.dot_general(q, k_rest, last, preferred_element_type=f32)
        if bias_ref is not None:
            rest_score = rest_score + bias_ref[:, main:]
        rest_weights = jnp.exp2(rest_score).astype(bf16)
        columns = []
        for h in range(4):
            side = h % 2
            own, other = (first_b, second_b)[side][:rest], (second_b, first_b)[side][:rest]
            v_rest = v[main:, (h // 2) * pair : (h // 2 + 1) * pair] * own + other
            zero = jnp.zeros_like(v_rest)
            columns.append(jnp.concatenate([v_rest if i == h else zero for i in range(4)], axis=0))
        rest_out = mm(rest_weights, jnp.concatenate(columns, axis=1))
        shares = []
        for h in range(4):
            cut = slice((h // 2) * pair, (h // 2 + 1) * pair)
            own = (first_b, second_b)[h % 2][:main]
            score = lax.dot_general(q[:, cut], k[:main, cut] * own, last, preferred_element_type=f32)
            if bias_ref is not None:
                score = score + bias_ref[:, :main]
            shares.append(jnp.exp2(score).astype(bf16))
        for p in range(2):
            cut = slice(p * pair, (p + 1) * pair)
            v_pair = v[:main, cut]
            both = []
            for side, (own, other) in enumerate(((first_b, second_b), (second_b, first_b))):
                h = 2 * p + side
                both.append(
                    mm(shares[h], v_pair * own[:main] + other[:main]) + rest_out[:, h * pair : (h + 1) * pair]
                )
            result = jnp.where(first, both[0], both[1])
            total = pltpu.roll(jnp.where(first, both[1], both[0]), head_dim, 1)
            store(slice(at + p * pair, at + (p + 1) * pair), (result / total).astype(bf16))


def scale_lanes(scale_ref, layer, width, heads):
    lane = lax.broadcasted_iota(jnp.int32, (1, width), 1)
    row = jnp.zeros((1, width), f32)
    for h in range(heads):
        row = jnp.where(lane >= h * (width // heads), scale_ref[layer, h] * LOG2E, row)
    return row


def norm_rows(values, gain_row, bias_row):
    average = jnp.mean(values, -1, keepdims=True)
    centred = values - average
    spread = jnp.mean(centred * centred, -1, keepdims=True)
    return centred * (lax.rsqrt(spread + 1e-05)) * gain_row + bias_row


def gelu_twice(x):
    c = 0.7978845608028654
    x = x.astype(bf16)
    one = jnp.ones((), bf16)
    inner = x * (jnp.asarray(c, bf16) + jnp.asarray(c * 0.044715, bf16) * (x * x))
    return x * (one + jnp.tanh(inner))


def finish_window(x, attended, out_weight, up_ref, down_ref, gain, bias):
    after = x + norm_rows(mm(attended, out_weight), gain[0:1], bias[0:1])
    after_b = after.astype(bf16)
    ff = up_ref.shape[1]
    step = min(512, ff)
    total = None
    for at in range(0, ff, step):
        hidden = gelu_twice(mm(after_b, up_ref[:, at : at + step]))
        part = mm(hidden, down_ref[at : at + step, :])
        total = part if total is None else total + part
    return after + norm_rows(0.5 * total, gain[1:2], bias[1:2])


def window_keys(ids_ref, j, cols, main, rest, levels, base, lat_total):
    run = HALF_LON * levels
    quarter = HALF_LAT * run
    shape = (1, cols)
    at = lax.broadcasted_iota(jnp.int32, shape, 1)
    t = jnp.where(at < main, at, main + ((at - main) & (rest - 1))).astype(f32)

    def cut(value, by):
        return jnp.floor((value + 0.5) * (1.0 / by))

    q = cut(t, quarter)
    half = cut(q, 2)
    block = q - 2 * half
    inside = t - quarter * q
    r = cut(inside, run)
    column = half * HALF_LON + cut(inside - run * r, levels)
    row = base + block * HALF_LAT + r
    key = jnp.zeros(shape, f32)
    ids = ids_ref[j * WIN_LAT, 0:1, :].astype(f32)
    for c in range(WIN_LON):
        key = jnp.where(column == c, ids[:, c : c + 1], key)
    band = jnp.where(row >= lat_total - WIN_LAT, 1.0, 0.0) + jnp.where(row >= lat_total - HALF_LAT, 1.0, 0.0)
    return key * 3 + band


def kernel(lat_size, x_hbm, ids_ref, qkv_hbm, out_hbm, up_hbm, down_hbm, gain_ref, bias_ref, scale_ref,
           y_hbm, x_s, first_s, op_s, att_s, send_s, send_own, back_s, back_own, mask_s, win_f, win_b,
           scale_s, qkv_s, out_s, up_s, down_s, w_sem, x_sem, y_sem, send1, recv1, send2, recv2):
    samples, lat_rows, lon_cols, levels, width = x_s.shape
    wins = lat_rows // WIN_LAT
    blocks = 2 * wins
    run = HALF_LON * levels
    quarter = HALF_LAT * run
    last_block = blocks - 1

    loads = [
        [
            pltpu.make_async_copy(src.at[layer], dst.at[layer], w_sem.at[layer, k])
            for k, (src, dst) in enumerate(
                ((qkv_hbm, qkv_s), (out_hbm, out_s), (up_hbm, up_s), (down_hbm, down_s))
            )
        ]
        for layer in range(2)
    ]

    def x_load(s):
        return pltpu.make_async_copy(x_hbm.at[s], x_s.at[s], x_sem.at[s])

    x_load(0).start()
    for copy in loads[0]:
        copy.start()
    for s in range(1, samples):
        x_load(s).start()
    for copy in loads[1]:
        copy.start()

    lon, lat = lax.axis_index("lon"), lax.axis_index("lat")
    lon_size = lax.axis_size("lon")
    west = lax.rem(lon + lon_size - 1, lon_size)
    east = lax.rem(lon + 1, lon_size)
    before = lax.rem(lat + lat_size - 1, lat_size)
    after = lax.rem(lat + 1, lat_size)

    barrier = pltpu.get_barrier_semaphore()
    peers = ((west, lat), (west, before), (lon, before), (lon, after), (east, lat), (east, after))
    for to_lon, to_lat in peers:
        pl.semaphore_signal(barrier, inc=1, device_id={"lon": to_lon, "lat": to_lat}, device_id_type=MESH)

    heads = scale_ref.shape[1]
    head_dim = width // heads
    rest = head_dim // 2
    tokens = 4 * quarter
    for layer in range(2):
        scale_s[layer : layer + 1, :] = scale_lanes(scale_ref, layer, width, heads)

    lat_total = lat_size * lat_rows
    cols = tokens + 3 * rest
    for j in range(wins):
        base = (lat * lat_rows + j * WIN_LAT).astype(f32)
        key = window_keys(ids_ref, j, cols, tokens - rest, rest, levels, base, lat_total)
        kinds = lax.broadcasted_iota(jnp.int32, (16, cols), 0).astype(f32)
        member = (kinds == key).astype(f32).astype(bf16)
        same = lax.dot_general(member[:, :tokens], member, (((0,), (0,)), ((), ())), preferred_element_type=f32)
        mask_s[j] = (same - 1.0) * 1e30

    def remote(src, dst, send, recv, to_lon, to_lat):
        return pltpu.make_async_remote_copy(
            src_ref=src, dst_ref=dst, send_sem=send, recv_sem=recv,
            device_id={"lon": to_lon, "lat": to_lat}, device_id_type=MESH,
        )

    def ahead(s, k):
        if k == 0:
            return remote(send_s.at[s, pl.ds(1, 1)], op_s.at[s, 1, pl.ds(0, 1)], send1.at[s, k], recv1.at[s, k], west, lat)
        if k == 1:
            return remote(send_s.at[s, pl.ds(0, 1)], op_s.at[s, 1, pl.ds(last_block, 1)], send1.at[s, k], recv1.at[s, k], west, before)
        if k == 2:
            return remote(send_own.at[s], op_s.at[s, 0, pl.ds(last_block, 1)], send1.at[s, k], recv1.at[s, k], lon, before)
        j = k - 2
        return remote(send_s.at[s, pl.ds(2 * j, 2)], op_s.at[s, 1, pl.ds(2 * j - 1, 2)], send1.at[s, k], recv1.at[s, k], west, lat)

    def back(s, k):
        if k == 0:
            return remote(back_s.at[s, pl.ds(last_block - 1, 1)], att_s.at[s, 0, pl.ds(last_block, 1)], send2.at[s, k], recv2.at[s, k], east, lat)
        if k == 1:
            return remote(back_s.at[s, pl.ds(last_block, 1)], att_s.at[s, 0, pl.ds(0, 1)], send2.at[s, k], recv2.at[s, k], east, after)
        if k == 2:
            return remote(back_own.at[s], att_s.at[s, 1, pl.ds(0, 1)], send2.at[s, k], recv2.at[s, k], lon, after)
        j = k - 3
        return remote(back_s.at[s, pl.ds(2 * j, 2)], att_s.at[s, 0, pl.ds(2 * j + 1, 2)], send2.at[s, k], recv2.at[s, k], east, lat)

    copies = 3 + wins - 1

    def store(cut, value):
        win_b[:, cut] = value

    def layer_first(i, carry):
        s, j = lax.div(i, wins), lax.rem(i, wins)

        @pl.when(j == 0)
        def _():
            x_load(s).wait()

        @pl.when(i == 0)
        def _():
            loads[0][0].wait()

        for half in range(2):
            for block in range(2):
                for r in range(HALF_LAT):
                    row = (half * 2 + block) * quarter + r * run
                    part = x_s[s, j * WIN_LAT + block * HALF_LAT + r, half * HALF_LON : (half + 1) * HALF_LON]
                    first_s[i, row : row + run, :] = part.reshape(run, width)
        attend_window(first_s[i].astype(bf16), qkv_s.at[0], scale_s[0:1, :], None, head_dim, store)

        @pl.when(i == 0)
        def _():
            for copy in loads[0][1:]:
                copy.wait()

        first_s[i] = finish_window(first_s[i], win_b[...], out_s[0], up_s.at[0], down_s.at[0], gain_ref[0], bias_ref[0])

        def block_of(q):
            return first_s[i, q * quarter : (q + 1) * quarter, :].astype(bf16)

        @pl.when(i == 0)
        def _():
            pl.semaphore_wait(barrier, len(peers))

        send_s[s, 2 * j] = block_of(0)
        send_s[s, 2 * j + 1] = block_of(1)
        op_s[s, 0, 2 * j] = block_of(3)

        @pl.when(j == 0)
        def _():
            send_own[s, 0] = block_of(2)
            for k in range(3):
                ahead(s, k).start()

        for jj in range(1, wins):

            @pl.when(j == jj)
            def _():
                op_s[s, 0, 2 * jj - 1] = block_of(2)
                ahead(s, 2 + jj).start()

        return carry

    def shifted_attention(i, carry):
        s, j = lax.div(i, wins), lax.rem(i, wins)

        @pl.when(j == 0)
        def _():
            for k in range(copies):
                ahead(s, k).wait_recv()

        @pl.when(i == 0)
        def _():
            loads[1][0].wait()

        for half in range(2):
            for block in range(2):
                row = (half * 2 + block) * quarter
                win_f[row : row + quarter, :] = op_s[s, half, 2 * j + block].astype(f32)
        attend_window(win_f[...].astype(bf16), qkv_s.at[1], scale_s[1:2, :], mask_s.at[j], head_dim, store)
        win_f[...] = win_b[...].astype(f32)

        def block_of(q):
            return win_f[q * quarter : (q + 1) * quarter, :].astype(bf16)

        att_s[s, 1, 2 * j + 1] = block_of(0)
        back_s[s, 2 * j] = block_of(2)
        back_s[s, 2 * j + 1] = block_of(3)

        @pl.when(j == wins - 1)
        def _():
            back_own[s, 0] = block_of(1)
            for k in range(3):
                back(s, k).start()

        for jj in range(wins - 1):

            @pl.when(j == jj)
            def _():
                att_s[s, 1, 2 * jj + 2] = block_of(1)
                back(s, 3 + jj).start()

        return carry

    def y_copy(s, j):
        rows = pl.ds(j * WIN_LAT, WIN_LAT)
        return pltpu.make_async_copy(x_s.at[s, rows], y_hbm.at[s, rows], y_sem.at[s, j])

    def layer_last(i, carry):
        s, j = lax.div(i, wins), lax.rem(i, wins)

        @pl.when(j == 0)
        def _():
            for k in range(copies):
                back(s, k).wait_recv()

        @pl.when(i == 0)
        def _():
            for copy in loads[1][1:]:
                copy.wait()

        for half in range(2):
            for block in range(2):
                row = (half * 2 + block) * quarter
                win_f[row : row + quarter, :] = att_s[s, half, 2 * j + block].astype(f32)
        win_f[...] = finish_window(
            first_s[i], win_f[...].astype(bf16), out_s[1], up_s.at[1], down_s.at[1], gain_ref[1], bias_ref[1]
        )
        for half in range(2):
            for block in range(2):
                for r in range(HALF_LAT):
                    row = (half * 2 + block) * quarter + r * run
                    x_s[s, j * WIN_LAT + block * HALF_LAT + r, half * HALF_LON : (half + 1) * HALF_LON] = win_f[
                        row : row + run, :
                    ].reshape(HALF_LON, levels, width)
        y_copy(s, j).start()
        return carry

    def stage(k, carry):
        for lag, step in enumerate((layer_first, shifted_attention, layer_last)):
            s = k - lag

            @pl.when((s >= 0) & (s < samples))
            def _():
                lax.fori_loop(s * wins, (s + 1) * wins, step, 0)

        return carry

    lax.fori_loop(0, samples + 2, stage, 0)

    def drain(s, carry):
        for k in range(copies):
            ahead(s, k).wait_send()
            back(s, k).wait_send()
        for j in range(wins):
            y_copy(s, j).wait()
        return carry

    lax.fori_loop(0, samples, drain, 0)


def local(stream, region_ids, qkv_weight, out_weight, up_weight, down_weight, norm_gain, norm_bias, logit_scale):
    samples, levels, lat_rows, lon_cols, width = stream.shape
    assert lon_cols == WIN_LON
    wins = lat_rows // WIN_LAT
    blocks = 2 * wins
    quarter = levels * HALF_LAT * HALF_LON
    tokens = 4 * quarter
    copies = 3 + wins - 1
    x = stream.transpose(0, 2, 3, 1, 4)
    ids = region_ids.transpose(1, 0, 2)
    hbm = pl.BlockSpec(memory_space=pl.ANY)
    vmem = pl.BlockSpec(memory_space=pltpu.VMEM)
    smem = pl.BlockSpec(memory_space=pltpu.SMEM)
    sem = pltpu.SemaphoreType.DMA
    y = pl.pallas_call(
        functools.partial(kernel, lax.axis_size("lat")),
        in_specs=[hbm, vmem, hbm, hbm, hbm, hbm, vmem, vmem, smem],
        out_specs=hbm,
        out_shape=jax.ShapeDtypeStruct(x.shape, f32),
        scratch_shapes=[
            pltpu.VMEM(x.shape, f32),
            pltpu.VMEM((samples * wins, tokens, width), f32),
            pltpu.VMEM((samples, 2, blocks, quarter, width), bf16),
            pltpu.VMEM((samples, 2, blocks, quarter, width), bf16),
            pltpu.VMEM((samples, blocks, quarter, width), bf16),
            pltpu.VMEM((samples, 1, quarter, width), bf16),
            pltpu.VMEM((samples, blocks, quarter, width), bf16),
            pltpu.VMEM((samples, 1, quarter, width), bf16),
            pltpu.VMEM((wins, tokens, tokens + 3 * (width // logit_scale.shape[1] // 2)), f32),
            pltpu.VMEM((tokens, width), f32),
            pltpu.VMEM((tokens, width), bf16),
            pltpu.VMEM((2, width), f32),
            pltpu.VMEM(qkv_weight.shape, bf16),
            pltpu.VMEM(out_weight.shape, bf16),
            pltpu.VMEM(up_weight.shape, bf16),
            pltpu.VMEM(down_weight.shape, bf16),
            sem((2, 4)),
            sem((samples,)),
            sem((samples, wins)),
            sem((samples, copies)),
            sem((samples, copies)),
            sem((samples, copies)),
            sem((samples, copies)),
        ],
        compiler_params=pltpu.CompilerParams(
            vmem_limit_bytes=VMEM_LIMIT, collective_id=0, has_side_effects=True
        ),
        name="both_layers",
    )(x, ids, qkv_weight, out_weight, up_weight, down_weight, norm_gain, norm_bias, logit_scale)
    return y.transpose(0, 3, 1, 2, 4)


def solution(mesh):
    in_specs = (P("ens", None, "lat", "lon", None), P("ens", "lat", "lon")) + (P(),) * 7
    out_specs = P("ens", None, "lat", "lon", None)
    return jax.shard_map(local, mesh=mesh, in_specs=in_specs, out_specs=out_specs, check_vma=False)
```

```python
import functools

import jax
import jax.numpy as jnp
from jax import lax
from jax.experimental import pallas as pl
from jax.experimental.pallas import tpu as pltpu
from jax.sharding import PartitionSpec as P

WIN_LAT = 6
WIN_LON = 12
HALF_LAT = WIN_LAT // 2
HALF_LON = WIN_LON // 2
LOG2E = 1.4426950408889634
VMEM_LIMIT = 60 * 1024 * 1024

f32 = jnp.float32
bf16 = jnp.bfloat16


MESH = pl.DeviceIdType.MESH


def mm(a, b):
    return jnp.dot(a, b, preferred_element_type=f32)


def attend_window(operand, qkv_weight, scale_row, bias_ref, head_dim, store):
    tokens, width = operand.shape
    group = 4 * head_dim
    pair = 2 * head_dim
    rest = pair // 4
    main = tokens - rest
    last = (((1,), (1,)), ((), ()))
    query = mm(operand, qkv_weight[:, :width])
    key = mm(operand, qkv_weight[:, width : 2 * width])
    value = mm(operand, qkv_weight[:, 2 * width :]).astype(bf16)
    d0 = lax.broadcasted_iota(jnp.int32, (group, group), 0)
    d1 = lax.broadcasted_iota(jnp.int32, (group, group), 1)
    same_head = lax.shift_right_logical(d0, head_dim.bit_length() - 1) == lax.shift_right_logical(
        d1, head_dim.bit_length() - 1
    )
    same_head = same_head.astype(f32).astype(bf16)

    def lanes(rows, cols, at, size):
        lane = lax.broadcasted_iota(jnp.int32, (rows, cols), 1)
        return ((lane >= at) & (lane < at + size)).astype(f32).astype(bf16)

    first_b = lanes(tokens, pair, 0, head_dim)
    second_b = lanes(tokens, pair, head_dim, head_dim)
    first = lax.broadcasted_iota(jnp.int32, (tokens, pair), 1) < head_dim

    def unit(part, scale):
        rounded = part.astype(bf16)
        inv = lax.rsqrt(mm(rounded * rounded, same_head) + 1e-06)
        if scale is not None:
            inv = inv * scale
        return (part * inv).astype(bf16)

    for g in range(width // group):
        at = g * group
        q = unit(query[:, at : at + group], scale_row[:, at : at + group])
        k = unit(key[:, at : at + group], None)
        v = value[:, at : at + group]
        k_rest = jnp.concatenate(
            [k[main:] * lanes(rest, group, h * head_dim, head_dim) for h in range(4)], axis=0
        )
        rest_score = lax.dot_general(q, k_rest, last, preferred_element_type=f32)
        if bias_ref is not None:
            rest_score = rest_score + bias_ref[:, main:]
        rest_weights = jnp.exp2(rest_score).astype(bf16)
        columns = []
        for h in range(4):
            side = h % 2
            own, other = (first_b, second_b)[side][:rest], (second_b, first_b)[side][:rest]
            v_rest = v[main:, (h // 2) * pair : (h // 2 + 1) * pair] * own + other
            zero = jnp.zeros_like(v_rest)
            columns.append(jnp.concatenate([v_rest if i == h else zero for i in range(4)], axis=0))
        rest_out = mm(rest_weights, jnp.concatenate(columns, axis=1))
        shares = []
        for h in range(4):
            cut = slice((h // 2) * pair, (h // 2 + 1) * pair)
            own = (first_b, second_b)[h % 2][:main]
            score = lax.dot_general(q[:, cut], k[:main, cut] * own, last, preferred_element_type=f32)
            if bias_ref is not None:
                score = score + bias_ref[:, :main]
            shares.append(jnp.exp2(score).astype(bf16))
        for p in range(2):
            cut = slice(p * pair, (p + 1) * pair)
            v_pair = v[:main, cut]
            both = []
            for side, (own, other) in enumerate(((first_b, second_b), (second_b, first_b))):
                h = 2 * p + side
                both.append(
                    mm(shares[h], v_pair * own[:main] + other[:main]) + rest_out[:, h * pair : (h + 1) * pair]
                )
            result = jnp.where(first, both[0], both[1])
            total = pltpu.roll(jnp.where(first, both[1], both[0]), head_dim, 1)
            store(slice(at + p * pair, at + (p + 1) * pair), (result / total).astype(bf16))


def scale_lanes(scale_ref, layer, width, heads):
    lane = lax.broadcasted_iota(jnp.int32, (1, width), 1)
    row = jnp.zeros((1, width), f32)
    for h in range(heads):
        row = jnp.where(lane >= h * (width // heads), scale_ref[layer, h] * LOG2E, row)
    return row


def norm_rows(values, gain_row, bias_row):
    average = jnp.mean(values, -1, keepdims=True)
    centred = values - average
    spread = jnp.mean(centred * centred, -1, keepdims=True)
    return centred * (lax.rsqrt(spread + 1e-05)) * gain_row + bias_row


def gelu_twice(x):
    c = 0.7978845608028654
    x = x.astype(bf16)
    one = jnp.ones((), bf16)
    inner = x * (jnp.asarray(c, bf16) + jnp.asarray(c * 0.044715, bf16) * (x * x))
    return x * (one + jnp.tanh(inner))


def finish_window(x, attended, out_weight, up_ref, down_ref, gain, bias):
    after = x + norm_rows(mm(attended, out_weight), gain[0:1], bias[0:1])
    after_b = after.astype(bf16)
    ff = up_ref.shape[1]
    step = min(512, ff)
    total = None
    for at in range(0, ff, step):
        hidden = gelu_twice(mm(after_b, up_ref[:, at : at + step]))
        part = mm(hidden, down_ref[at : at + step, :])
        total = part if total is None else total + part
    return after + norm_rows(0.5 * total, gain[1:2], bias[1:2])


def window_keys(ids_ref, j, cols, main, rest, levels, base, lat_total):
    run = HALF_LON * levels
    quarter = HALF_LAT * run
    shape = (1, cols)
    at = lax.broadcasted_iota(jnp.int32, shape, 1)
    t = jnp.where(at < main, at, main + ((at - main) & (rest - 1))).astype(f32)

    def cut(value, by):
        return jnp.floor((value + 0.5) * (1.0 / by))

    q = cut(t, quarter)
    half = cut(q, 2)
    block = q - 2 * half
    inside = t - quarter * q
    r = cut(inside, run)
    column = half * HALF_LON + cut(inside - run * r, levels)
    row = base + block * HALF_LAT + r
    key = jnp.zeros(shape, f32)
    ids = ids_ref[j * WIN_LAT, 0:1, :].astype(f32)
    for c in range(WIN_LON):
        key = jnp.where(column == c, ids[:, c : c + 1], key)
    band = jnp.where(row >= lat_total - WIN_LAT, 1.0, 0.0) + jnp.where(row >= lat_total - HALF_LAT, 1.0, 0.0)
    return key * 3 + band


def kernel(lat_size, x_hbm, ids_ref, qkv_hbm, out_hbm, up_hbm, down_hbm, gain_ref, bias_ref, scale_ref,
           y_hbm, x_s, first_s, op_s, att_s, send_s, send_own, back_s, back_own, mask_s, win_f, win_b,
           scale_s, qkv_s, out_s, up_s, down_s, w_sem, x_sem, y_sem, send1, recv1, send2, recv2):
    samples, lat_rows, lon_cols, levels, width = x_s.shape
    wins = lat_rows // WIN_LAT
    blocks = 2 * wins
    run = HALF_LON * levels
    quarter = HALF_LAT * run
    last_block = blocks - 1

    loads = [
        [
            pltpu.make_async_copy(src.at[layer], dst.at[layer], w_sem.at[layer, k])
            for k, (src, dst) in enumerate(
                ((qkv_hbm, qkv_s), (out_hbm, out_s), (up_hbm, up_s), (down_hbm, down_s))
            )
        ]
        for layer in range(2)
    ]

    def x_load(s):
        return pltpu.make_async_copy(x_hbm.at[s], x_s.at[s], x_sem.at[s])

    x_load(0).start()
    for copy in loads[0]:
        copy.start()
    for s in range(1, samples):
        x_load(s).start()
    for copy in loads[1]:
        copy.start()

    lon, lat = lax.axis_index("lon"), lax.axis_index("lat")
    lon_size = lax.axis_size("lon")
    west = lax.rem(lon + lon_size - 1, lon_size)
    east = lax.rem(lon + 1, lon_size)
    before = lax.rem(lat + lat_size - 1, lat_size)
    after = lax.rem(lat + 1, lat_size)

    barrier = pltpu.get_barrier_semaphore()
    peers = ((west, lat), (west, before), (lon, before), (lon, after), (east, lat), (east, after))
    for to_lon, to_lat in peers:
        pl.semaphore_signal(barrier, inc=1, device_id={"lon": to_lon, "lat": to_lat}, device_id_type=MESH)

    heads = scale_ref.shape[1]
    head_dim = width // heads
    rest = head_dim // 2
    tokens = 4 * quarter
    for layer in range(2):
        scale_s[layer : layer + 1, :] = scale_lanes(scale_ref, layer, width, heads)

    lat_total = lat_size * lat_rows
    cols = tokens + 3 * rest
    for j in range(wins):
        base = (lat * lat_rows + j * WIN_LAT).astype(f32)
        key = window_keys(ids_ref, j, cols, tokens - rest, rest, levels, base, lat_total)
        kinds = lax.broadcasted_iota(jnp.int32, (16, cols), 0).astype(f32)
        member = (kinds == key).astype(f32).astype(bf16)
        same = lax.dot_general(member[:, :tokens], member, (((0,), (0,)), ((), ())), preferred_element_type=f32)
        mask_s[j] = (same - 1.0) * 1e30

    def remote(src, dst, send, recv, to_lon, to_lat):
        return pltpu.make_async_remote_copy(
            src_ref=src, dst_ref=dst, send_sem=send, recv_sem=recv,
            device_id={"lon": to_lon, "lat": to_lat}, device_id_type=MESH,
        )

    def ahead(s, k):
        if k == 0:
            return remote(send_s.at[s, pl.ds(1, 1)], op_s.at[s, 1, pl.ds(0, 1)], send1.at[s, k], recv1.at[s, k], west, lat)
        if k == 1:
            return remote(send_s.at[s, pl.ds(0, 1)], op_s.at[s, 1, pl.ds(last_block, 1)], send1.at[s, k], recv1.at[s, k], west, before)
        if k == 2:
            return remote(send_own.at[s], op_s.at[s, 0, pl.ds(last_block, 1)], send1.at[s, k], recv1.at[s, k], lon, before)
        j = k - 2
        return remote(send_s.at[s, pl.ds(2 * j, 2)], op_s.at[s, 1, pl.ds(2 * j - 1, 2)], send1.at[s, k], recv1.at[s, k], west, lat)

    def back(s, k):
        if k == 0:
            return remote(back_s.at[s, pl.ds(last_block - 1, 1)], att_s.at[s, 0, pl.ds(last_block, 1)], send2.at[s, k], recv2.at[s, k], east, lat)
        if k == 1:
            return remote(back_s.at[s, pl.ds(last_block, 1)], att_s.at[s, 0, pl.ds(0, 1)], send2.at[s, k], recv2.at[s, k], east, after)
        if k == 2:
            return remote(back_own.at[s], att_s.at[s, 1, pl.ds(0, 1)], send2.at[s, k], recv2.at[s, k], lon, after)
        j = k - 3
        return remote(back_s.at[s, pl.ds(2 * j, 2)], att_s.at[s, 0, pl.ds(2 * j + 1, 2)], send2.at[s, k], recv2.at[s, k], east, lat)

    copies = 3 + wins - 1

    def store(cut, value):
        win_b[:, cut] = value

    def layer_first(i, carry):
        s, j = lax.div(i, wins), lax.rem(i, wins)

        @pl.when(j == 0)
        def _():
            x_load(s).wait()

        @pl.when(i == 0)
        def _():
            loads[0][0].wait()

        for half in range(2):
            for block in range(2):
                for r in range(HALF_LAT):
                    row = (half * 2 + block) * quarter + r * run
                    part = x_s[s, j * WIN_LAT + block * HALF_LAT + r, half * HALF_LON : (half + 1) * HALF_LON]
                    first_s[i, row : row + run, :] = part.reshape(run, width)
        attend_window(first_s[i].astype(bf16), qkv_s.at[0], scale_s[0:1, :], None, head_dim, store)

        @pl.when(i == 0)
        def _():
            for copy in loads[0][1:]:
                copy.wait()

        first_s[i] = finish_window(first_s[i], win_b[...], out_s[0], up_s.at[0], down_s.at[0], gain_ref[0], bias_ref[0])

        def block_of(q):
            return first_s[i, q * quarter : (q + 1) * quarter, :].astype(bf16)

        @pl.when(i == 0)
        def _():
            pl.semaphore_wait(barrier, len(peers))

        send_s[s, 2 * j] = block_of(0)
        send_s[s, 2 * j + 1] = block_of(1)
        op_s[s, 0, 2 * j] = block_of(3)

        @pl.when(j == 0)
        def _():
            send_own[s, 0] = block_of(2)
            for k in range(3):
                ahead(s, k).start()

        for jj in range(1, wins):

            @pl.when(j == jj)
            def _():
                op_s[s, 0, 2 * jj - 1] = block_of(2)
                ahead(s, 2 + jj).start()

        return carry

    def shifted_attention(i, carry):
        s, j = lax.div(i, wins), lax.rem(i, wins)

        @pl.when(j == 0)
        def _():
            for k in range(copies):
                ahead(s, k).wait_recv()

        @pl.when(i == 0)
        def _():
            loads[1][0].wait()

        for half in range(2):
            for block in range(2):
                row = (half * 2 + block) * quarter
                win_f[row : row + quarter, :] = op_s[s, half, 2 * j + block].astype(f32)
        attend_window(win_f[...].astype(bf16), qkv_s.at[1], scale_s[1:2, :], mask_s.at[j], head_dim, store)
        win_f[...] = win_b[...].astype(f32)

        def block_of(q):
            return win_f[q * quarter : (q + 1) * quarter, :].astype(bf16)

        att_s[s, 1, 2 * j + 1] = block_of(0)
        back_s[s, 2 * j] = block_of(2)
        back_s[s, 2 * j + 1] = block_of(3)

        @pl.when(j == wins - 1)
        def _():
            back_own[s, 0] = block_of(1)
            for k in range(3):
                back(s, k).start()

        for jj in range(wins - 1):

            @pl.when(j == jj)
            def _():
                att_s[s, 1, 2 * jj + 2] = block_of(1)
                back(s, 3 + jj).start()

        return carry

    def y_copy(s, j):
        rows = pl.ds(j * WIN_LAT, WIN_LAT)
        return pltpu.make_async_copy(x_s.at[s, rows], y_hbm.at[s, rows], y_sem.at[s, j])

    def layer_last(i, carry):
        s, j = lax.div(i, wins), lax.rem(i, wins)

        @pl.when(j == 0)
        def _():
            for k in range(copies):
                back(s, k).wait_recv()

        @pl.when(i == 0)
        def _():
            for copy in loads[1][1:]:
                copy.wait()

        for half in range(2):
            for block in range(2):
                row = (half * 2 + block) * quarter
                win_f[row : row + quarter, :] = att_s[s, half, 2 * j + block].astype(f32)
        win_f[...] = finish_window(
            first_s[i], win_f[...].astype(bf16), out_s[1], up_s.at[1], down_s.at[1], gain_ref[1], bias_ref[1]
        )
        for half in range(2):
            for block in range(2):
                for r in range(HALF_LAT):
                    row = (half * 2 + block) * quarter + r * run
                    x_s[s, j * WIN_LAT + block * HALF_LAT + r, half * HALF_LON : (half + 1) * HALF_LON] = win_f[
                        row : row + run, :
                    ].reshape(HALF_LON, levels, width)
        y_copy(s, j).start()
        return carry

    for step in (layer_first, shifted_attention, layer_last):
        lax.fori_loop(0, samples * wins, step, 0)

    def drain(s, carry):
        for k in range(copies):
            ahead(s, k).wait_send()
            back(s, k).wait_send()
        for j in range(wins):
            y_copy(s, j).wait()
        return carry

    lax.fori_loop(0, samples, drain, 0)


def local(stream, region_ids, qkv_weight, out_weight, up_weight, down_weight, norm_gain, norm_bias, logit_scale):
    samples, levels, lat_rows, lon_cols, width = stream.shape
    assert lon_cols == WIN_LON
    wins = lat_rows // WIN_LAT
    blocks = 2 * wins
    quarter = levels * HALF_LAT * HALF_LON
    tokens = 4 * quarter
    copies = 3 + wins - 1
    x = stream.transpose(0, 2, 3, 1, 4)
    ids = region_ids.transpose(1, 0, 2)
    hbm = pl.BlockSpec(memory_space=pl.ANY)
    vmem = pl.BlockSpec(memory_space=pltpu.VMEM)
    smem = pl.BlockSpec(memory_space=pltpu.SMEM)
    sem = pltpu.SemaphoreType.DMA
    y = pl.pallas_call(
        functools.partial(kernel, lax.axis_size("lat")),
        in_specs=[hbm, vmem, hbm, hbm, hbm, hbm, vmem, vmem, smem],
        out_specs=hbm,
        out_shape=jax.ShapeDtypeStruct(x.shape, f32),
        scratch_shapes=[
            pltpu.VMEM(x.shape, f32),
            pltpu.VMEM((samples * wins, tokens, width), f32),
            pltpu.VMEM((samples, 2, blocks, quarter, width), bf16),
            pltpu.VMEM((samples, 2, blocks, quarter, width), bf16),
            pltpu.VMEM((samples, blocks, quarter, width), bf16),
            pltpu.VMEM((samples, 1, quarter, width), bf16),
            pltpu.VMEM((samples, blocks, quarter, width), bf16),
            pltpu.VMEM((samples, 1, quarter, width), bf16),
            pltpu.VMEM((wins, tokens, tokens + 3 * (width // logit_scale.shape[1] // 2)), f32),
            pltpu.VMEM((tokens, width), f32),
            pltpu.VMEM((tokens, width), bf16),
            pltpu.VMEM((2, width), f32),
            pltpu.VMEM(qkv_weight.shape, bf16),
            pltpu.VMEM(out_weight.shape, bf16),
            pltpu.VMEM(up_weight.shape, bf16),
            pltpu.VMEM(down_weight.shape, bf16),
            sem((2, 4)),
            sem((samples,)),
            sem((samples, wins)),
            sem((samples, copies)),
            sem((samples, copies)),
            sem((samples, copies)),
            sem((samples, copies)),
        ],
        compiler_params=pltpu.CompilerParams(
            vmem_limit_bytes=VMEM_LIMIT, collective_id=0, has_side_effects=True
        ),
        name="both_layers",
    )(x, ids, qkv_weight, out_weight, up_weight, down_weight, norm_gain, norm_bias, logit_scale)
    return y.transpose(0, 3, 1, 2, 4)


def solution(mesh):
    in_specs = (P("ens", None, "lat", "lon", None), P("ens", "lat", "lon")) + (P(),) * 7
    out_specs = P("ens", None, "lat", "lon", None)
    return jax.shard_map(local, mesh=mesh, in_specs=in_specs, out_specs=out_specs, check_vma=False)
```

```python
import functools

import jax
import jax.numpy as jnp
from jax import lax
from jax.experimental import pallas as pl
from jax.experimental.pallas import tpu as pltpu
from jax.sharding import PartitionSpec as P

WIN_LAT = 6
WIN_LON = 12
HALF_LAT = WIN_LAT // 2
HALF_LON = WIN_LON // 2
LOG2E = 1.4426950408889634
VMEM_LIMIT = 60 * 1024 * 1024

f32 = jnp.float32
bf16 = jnp.bfloat16


MESH = pl.DeviceIdType.MESH


def mm(a, b):
    return jnp.dot(a, b, preferred_element_type=f32)


def attend_window(operand, qkv_weight, scale_row, bias_ref, head_dim, store):
    tokens, width = operand.shape
    group = 4 * head_dim
    pair = 2 * head_dim
    rest = pair // 4
    main = tokens - rest
    last = (((1,), (1,)), ((), ()))
    query = mm(operand, qkv_weight[:, :width])
    key = mm(operand, qkv_weight[:, width : 2 * width])
    value = mm(operand, qkv_weight[:, 2 * width :]).astype(bf16)
    d0 = lax.broadcasted_iota(jnp.int32, (group, group), 0)
    d1 = lax.broadcasted_iota(jnp.int32, (group, group), 1)
    same_head = lax.shift_right_logical(d0, head_dim.bit_length() - 1) == lax.shift_right_logical(
        d1, head_dim.bit_length() - 1
    )
    same_head = same_head.astype(f32).astype(bf16)

    def lanes(rows, cols, at, size):
        lane = lax.broadcasted_iota(jnp.int32, (rows, cols), 1)
        return ((lane >= at) & (lane < at + size)).astype(f32).astype(bf16)

    first_b = lanes(tokens, pair, 0, head_dim)
    second_b = lanes(tokens, pair, head_dim, head_dim)
    first = lax.broadcasted_iota(jnp.int32, (tokens, pair), 1) < head_dim

    def unit(part, scale):
        rounded = part.astype(bf16)
        inv = lax.rsqrt(mm(rounded * rounded, same_head) + 1e-06)
        if scale is not None:
            inv = inv * scale
        return (part * inv).astype(bf16)

    for g in range(width // group):
        at = g * group
        q = unit(query[:, at : at + group], scale_row[:, at : at + group])
        k = unit(key[:, at : at + group], None)
        v = value[:, at : at + group]
        k_rest = jnp.concatenate(
            [k[main:] * lanes(rest, group, h * head_dim, head_dim) for h in range(4)], axis=0
        )
        rest_score = lax.dot_general(q, k_rest, last, preferred_element_type=f32)
        if bias_ref is not None:
            rest_score = rest_score + bias_ref[:, main:]
        rest_weights = jnp.exp2(rest_score).astype(bf16)
        columns = []
        for h in range(4):
            side = h % 2
            own, other = (first_b, second_b)[side][:rest], (second_b, first_b)[side][:rest]
            v_rest = v[main:, (h // 2) * pair : (h // 2 + 1) * pair] * own + other
            zero = jnp.zeros_like(v_rest)
            columns.append(jnp.concatenate([v_rest if i == h else zero for i in range(4)], axis=0))
        rest_out = mm(rest_weights, jnp.concatenate(columns, axis=1))
        shares = []
        for h in range(4):
            cut = slice((h // 2) * pair, (h // 2 + 1) * pair)
            own = (first_b, second_b)[h % 2][:main]
            score = lax.dot_general(q[:, cut], k[:main, cut] * own, last, preferred_element_type=f32)
            if bias_ref is not None:
                score = score + bias_ref[:, :main]
            shares.append(jnp.exp2(score).astype(bf16))
        for p in range(2):
            cut = slice(p * pair, (p + 1) * pair)
            v_pair = v[:main, cut]
            both = []
            for side, (own, other) in enumerate(((first_b, second_b), (second_b, first_b))):
                h = 2 * p + side
                both.append(
                    mm(shares[h], v_pair * own[:main] + other[:main]) + rest_out[:, h * pair : (h + 1) * pair]
                )
            result = jnp.where(first, both[0], both[1])
            total = pltpu.roll(jnp.where(first, both[1], both[0]), head_dim, 1)
            store(slice(at + p * pair, at + (p + 1) * pair), (result / total).astype(bf16))


def scale_lanes(scale_ref, layer, width, heads):
    lane = lax.broadcasted_iota(jnp.int32, (1, width), 1)
    row = jnp.zeros((1, width), f32)
    for h in range(heads):
        row = jnp.where(lane >= h * (width // heads), scale_ref[layer, h] * LOG2E, row)
    return row


def norm_rows(values, gain_row, bias_row):
    average = jnp.mean(values, -1, keepdims=True)
    centred = values - average
    spread = jnp.mean(centred * centred, -1, keepdims=True)
    return centred * (lax.rsqrt(spread + 1e-05)) * gain_row + bias_row


def gelu_twice(x):
    c = 0.7978845608028654
    x = x.astype(bf16)
    one = jnp.ones((), bf16)
    inner = x * (jnp.asarray(c, bf16) + jnp.asarray(c * 0.044715, bf16) * (x * x))
    return x * (one + jnp.tanh(inner))


def finish_window(x, attended, out_weight, up_ref, down_ref, gain, bias):
    after = x + norm_rows(mm(attended, out_weight), gain[0:1], bias[0:1])
    after_b = after.astype(bf16)
    ff = up_ref.shape[1]
    step = min(512, ff)
    total = None
    for at in range(0, ff, step):
        hidden = gelu_twice(mm(after_b, up_ref[:, at : at + step]))
        part = mm(hidden, down_ref[at : at + step, :])
        total = part if total is None else total + part
    return after + norm_rows(0.5 * total, gain[1:2], bias[1:2])


def window_keys(ids_ref, j, cols, main, rest, levels, base, lat_total):
    run = HALF_LON * levels
    quarter = HALF_LAT * run
    shape = (1, cols)
    at = lax.broadcasted_iota(jnp.int32, shape, 1)
    t = jnp.where(at < main, at, main + ((at - main) & (rest - 1))).astype(f32)

    def cut(value, by):
        return jnp.floor((value + 0.5) * (1.0 / by))

    q = cut(t, quarter)
    half = cut(q, 2)
    block = q - 2 * half
    inside = t - quarter * q
    r = cut(inside, run)
    column = half * HALF_LON + cut(inside - run * r, levels)
    row = base + block * HALF_LAT + r
    key = jnp.zeros(shape, f32)
    ids = ids_ref[j * WIN_LAT, 0:1, :].astype(f32)
    for c in range(WIN_LON):
        key = jnp.where(column == c, ids[:, c : c + 1], key)
    band = jnp.where(row >= lat_total - WIN_LAT, 1.0, 0.0) + jnp.where(row >= lat_total - HALF_LAT, 1.0, 0.0)
    return key * 3 + band


ORDER = "FFFFSSFFSSLLSSLLLL"


def order(count):
    seen = {"F": 0, "S": 0, "L": 0}
    plan = []
    for kind in ORDER:
        plan.append(("FSL".index(kind), seen[kind]))
        seen[kind] += 1
    assert min(seen.values()) == max(seen.values()) == count
    return plan


def kernel(lat_size, x_hbm, ids_ref, qkv_hbm, out_hbm, up_hbm, down_hbm, gain_ref, bias_ref, scale_ref,
           x_s, first_s, op_s, att_s, send_s, send_own, back_s, back_own, mask_s, win_f, win_b,
           scale_s, qkv_s, out_s, up_s, down_s, w_sem, x_sem, send1, recv1, send2, recv2):
    samples, lat_rows, lon_cols, levels, width = x_s.shape
    wins = lat_rows // WIN_LAT
    blocks = 2 * wins
    run = HALF_LON * levels
    quarter = HALF_LAT * run
    last_block = blocks - 1

    loads = [
        [
            pltpu.make_async_copy(src.at[layer], dst.at[layer], w_sem.at[layer, k])
            for k, (src, dst) in enumerate(
                ((qkv_hbm, qkv_s), (out_hbm, out_s), (up_hbm, up_s), (down_hbm, down_s))
            )
        ]
        for layer in range(2)
    ]

    def x_load(s):
        return pltpu.make_async_copy(x_hbm.at[s], x_s.at[s], x_sem.at[s])

    x_load(0).start()
    for copy in loads[0]:
        copy.start()
    for s in range(1, samples):
        x_load(s).start()
    for copy in loads[1]:
        copy.start()

    lon, lat = lax.axis_index("lon"), lax.axis_index("lat")
    lon_size = lax.axis_size("lon")
    west = lax.rem(lon + lon_size - 1, lon_size)
    east = lax.rem(lon + 1, lon_size)
    before = lax.rem(lat + lat_size - 1, lat_size)
    after = lax.rem(lat + 1, lat_size)

    barrier = pltpu.get_barrier_semaphore()
    peers = ((west, lat), (west, before), (lon, before), (lon, after), (east, lat), (east, after))
    for to_lon, to_lat in peers:
        pl.semaphore_signal(barrier, inc=1, device_id={"lon": to_lon, "lat": to_lat}, device_id_type=MESH)

    heads = scale_ref.shape[1]
    head_dim = width // heads
    rest = head_dim // 2
    tokens = 4 * quarter
    for layer in range(2):
        scale_s[layer : layer + 1, :] = scale_lanes(scale_ref, layer, width, heads)

    lat_total = lat_size * lat_rows
    cols = tokens + 3 * rest
    for j in range(wins):
        base = (lat * lat_rows + j * WIN_LAT).astype(f32)
        key = window_keys(ids_ref, j, cols, tokens - rest, rest, levels, base, lat_total)
        kinds = lax.broadcasted_iota(jnp.int32, (16, cols), 0).astype(f32)
        member = (kinds == key).astype(f32).astype(bf16)
        same = lax.dot_general(member[:, :tokens], member, (((0,), (0,)), ((), ())), preferred_element_type=f32)
        mask_s[j] = (same - 1.0) * 1e30

    def remote(src, dst, send, recv, to_lon, to_lat):
        return pltpu.make_async_remote_copy(
            src_ref=src, dst_ref=dst, send_sem=send, recv_sem=recv,
            device_id={"lon": to_lon, "lat": to_lat}, device_id_type=MESH,
        )

    def ahead(s, k):
        if k == 0:
            return remote(send_s.at[s, pl.ds(1, 1)], op_s.at[s, 1, pl.ds(0, 1)], send1.at[s, k], recv1.at[s, k], west, lat)
        if k == 1:
            return remote(send_s.at[s, pl.ds(0, 1)], op_s.at[s, 1, pl.ds(last_block, 1)], send1.at[s, k], recv1.at[s, k], west, before)
        if k == 2:
            return remote(send_own.at[s], op_s.at[s, 0, pl.ds(last_block, 1)], send1.at[s, k], recv1.at[s, k], lon, before)
        j = k - 2
        return remote(send_s.at[s, pl.ds(2 * j, 2)], op_s.at[s, 1, pl.ds(2 * j - 1, 2)], send1.at[s, k], recv1.at[s, k], west, lat)

    def back(s, k):
        if k == 0:
            return remote(back_s.at[s, pl.ds(last_block - 1, 1)], att_s.at[s, 0, pl.ds(last_block, 1)], send2.at[s, k], recv2.at[s, k], east, lat)
        if k == 1:
            return remote(back_s.at[s, pl.ds(last_block, 1)], att_s.at[s, 0, pl.ds(0, 1)], send2.at[s, k], recv2.at[s, k], east, after)
        if k == 2:
            return remote(back_own.at[s], att_s.at[s, 1, pl.ds(0, 1)], send2.at[s, k], recv2.at[s, k], lon, after)
        j = k - 3
        return remote(back_s.at[s, pl.ds(2 * j, 2)], att_s.at[s, 0, pl.ds(2 * j + 1, 2)], send2.at[s, k], recv2.at[s, k], east, lat)

    copies = 3 + wins - 1

    def store(cut, value):
        win_b[:, cut] = value

    def layer_first(i, carry):
        s, j = lax.div(i, wins), lax.rem(i, wins)

        @pl.when(j == 0)
        def _():
            x_load(s).wait()

        @pl.when(i == 0)
        def _():
            loads[0][0].wait()

        for half in range(2):
            for block in range(2):
                for r in range(HALF_LAT):
                    row = (half * 2 + block) * quarter + r * run
                    part = x_s[s, j * WIN_LAT + block * HALF_LAT + r, half * HALF_LON : (half + 1) * HALF_LON]
                    first_s[i, row : row + run, :] = part.reshape(run, width)
        attend_window(first_s[i].astype(bf16), qkv_s.at[0], scale_s[0:1, :], None, head_dim, store)

        @pl.when(i == 0)
        def _():
            for copy in loads[0][1:]:
                copy.wait()

        first_s[i] = finish_window(first_s[i], win_b[...], out_s[0], up_s.at[0], down_s.at[0], gain_ref[0], bias_ref[0])

        def block_of(q):
            return first_s[i, q * quarter : (q + 1) * quarter, :].astype(bf16)

        @pl.when(i == 0)
        def _():
            pl.semaphore_wait(barrier, len(peers))

        send_s[s, 2 * j] = block_of(0)
        send_s[s, 2 * j + 1] = block_of(1)
        op_s[s, 0, 2 * j] = block_of(3)

        @pl.when(j == 0)
        def _():
            send_own[s, 0] = block_of(2)
            for k in range(3):
                ahead(s, k).start()

        for jj in range(1, wins):

            @pl.when(j == jj)
            def _():
                op_s[s, 0, 2 * jj - 1] = block_of(2)
                ahead(s, 2 + jj).start()

        return carry

    def shifted_attention(i, carry):
        s, j = lax.div(i, wins), lax.rem(i, wins)

        @pl.when(j == 0)
        def _():
            for k in range(copies):
                ahead(s, k).wait_recv()

        @pl.when(i == 0)
        def _():
            loads[1][0].wait()

        for half in range(2):
            for block in range(2):
                row = (half * 2 + block) * quarter
                win_f[row : row + quarter, :] = op_s[s, half, 2 * j + block].astype(f32)
        attend_window(win_f[...].astype(bf16), qkv_s.at[1], scale_s[1:2, :], mask_s.at[j], head_dim, store)
        win_f[...] = win_b[...].astype(f32)

        def block_of(q):
            return win_f[q * quarter : (q + 1) * quarter, :].astype(bf16)

        att_s[s, 1, 2 * j + 1] = block_of(0)
        back_s[s, 2 * j] = block_of(2)
        back_s[s, 2 * j + 1] = block_of(3)

        @pl.when(j == wins - 1)
        def _():
            back_own[s, 0] = block_of(1)
            for k in range(3):
                back(s, k).start()

        for jj in range(wins - 1):

            @pl.when(j == jj)
            def _():
                att_s[s, 1, 2 * jj + 2] = block_of(1)
                back(s, 3 + jj).start()

        return carry

    def layer_last(i, carry):
        s, j = lax.div(i, wins), lax.rem(i, wins)

        @pl.when(j == 0)
        def _():
            for k in range(copies):
                back(s, k).wait_recv()

        @pl.when(i == 0)
        def _():
            for copy in loads[1][1:]:
                copy.wait()

        for half in range(2):
            for block in range(2):
                row = (half * 2 + block) * quarter
                win_f[row : row + quarter, :] = att_s[s, half, 2 * j + block].astype(f32)
        win_f[...] = finish_window(
            first_s[i], win_f[...].astype(bf16), out_s[1], up_s.at[1], down_s.at[1], gain_ref[1], bias_ref[1]
        )
        for half in range(2):
            for block in range(2):
                for r in range(HALF_LAT):
                    row = (half * 2 + block) * quarter + r * run
                    x_s[s, j * WIN_LAT + block * HALF_LAT + r, half * HALF_LON : (half + 1) * HALF_LON] = win_f[
                        row : row + run, :
                    ].reshape(HALF_LON, levels, width)
        return carry

    plan = order(samples * wins)

    def pick(t, values):
        value = jnp.int32(values[0])
        for n in range(1, len(values)):
            if values[n] != values[n - 1]:
                value = jnp.where(t >= n, jnp.int32(values[n]), value)
        return value

    def advance(t, carry):
        kind = pick(t, [k for k, _ in plan])
        i = pick(t, [n for _, n in plan])
        for k, step in enumerate((layer_first, shifted_attention, layer_last)):

            @pl.when(kind == k)
            def _():
                step(i, 0)

        return carry

    lax.fori_loop(0, len(plan), advance, 0)

    def drain(s, carry):
        for k in range(copies):
            ahead(s, k).wait_send()
            back(s, k).wait_send()
        return carry

    lax.fori_loop(0, samples, drain, 0)


def local(stream, region_ids, qkv_weight, out_weight, up_weight, down_weight, norm_gain, norm_bias, logit_scale):
    samples, levels, lat_rows, lon_cols, width = stream.shape
    assert lon_cols == WIN_LON
    wins = lat_rows // WIN_LAT
    blocks = 2 * wins
    quarter = levels * HALF_LAT * HALF_LON
    tokens = 4 * quarter
    copies = 3 + wins - 1
    x = stream.transpose(0, 2, 3, 1, 4)
    ids = region_ids.transpose(1, 0, 2)
    hbm = pl.BlockSpec(memory_space=pl.ANY)
    vmem = pl.BlockSpec(memory_space=pltpu.VMEM)
    smem = pl.BlockSpec(memory_space=pltpu.SMEM)
    sem = pltpu.SemaphoreType.DMA
    y = pl.pallas_call(
        functools.partial(kernel, lax.axis_size("lat")),
        in_specs=[hbm, vmem, hbm, hbm, hbm, hbm, vmem, vmem, smem],
        out_specs=vmem,
        out_shape=pltpu.VMEM(x.shape, f32),
        scratch_shapes=[
            pltpu.VMEM((samples * wins, tokens, width), f32),
            pltpu.VMEM((samples, 2, blocks, quarter, width), bf16),
            pltpu.VMEM((samples, 2, blocks, quarter, width), bf16),
            pltpu.VMEM((samples, blocks, quarter, width), bf16),
            pltpu.VMEM((samples, 1, quarter, width), bf16),
            pltpu.VMEM((samples, blocks, quarter, width), bf16),
            pltpu.VMEM((samples, 1, quarter, width), bf16),
            pltpu.VMEM((wins, tokens, tokens + 3 * (width // logit_scale.shape[1] // 2)), f32),
            pltpu.VMEM((tokens, width), f32),
            pltpu.VMEM((tokens, width), bf16),
            pltpu.VMEM((2, width), f32),
            pltpu.VMEM(qkv_weight.shape, bf16),
            pltpu.VMEM(out_weight.shape, bf16),
            pltpu.VMEM(up_weight.shape, bf16),
            pltpu.VMEM(down_weight.shape, bf16),
            sem((2, 4)),
            sem((samples,)),
            sem((samples, copies)),
            sem((samples, copies)),
            sem((samples, copies)),
            sem((samples, copies)),
        ],
        compiler_params=pltpu.CompilerParams(
            vmem_limit_bytes=VMEM_LIMIT, collective_id=0, has_side_effects=True
        ),
        name="both_layers",
    )(x, ids, qkv_weight, out_weight, up_weight, down_weight, norm_gain, norm_bias, logit_scale)
    return y.transpose(0, 3, 1, 2, 4)


def solution(mesh):
    in_specs = (P("ens", None, "lat", "lon", None), P("ens", "lat", "lon")) + (P(),) * 7
    out_specs = P("ens", None, "lat", "lon", None)
    return jax.shard_map(local, mesh=mesh, in_specs=in_specs, out_specs=out_specs, check_vma=False)
```

```python
import functools

import jax
import jax.numpy as jnp
from jax import lax
from jax.experimental import pallas as pl
from jax.experimental.pallas import tpu as pltpu
from jax.sharding import PartitionSpec as P

WIN_LAT = 6
WIN_LON = 12
HALF_LAT = WIN_LAT // 2
HALF_LON = WIN_LON // 2
LOG2E = 1.4426950408889634
VMEM_LIMIT = 60 * 1024 * 1024

f32 = jnp.float32
bf16 = jnp.bfloat16


MESH = pl.DeviceIdType.MESH


def mm(a, b):
    return jnp.dot(a, b, preferred_element_type=f32)


def attend_window(operand, qkv_weight, scale_row, bias_ref, head_dim, store):
    tokens, width = operand.shape
    group = 4 * head_dim
    pair = 2 * head_dim
    rest = pair // 4
    main = tokens - rest
    last = (((1,), (1,)), ((), ()))
    query = mm(operand, qkv_weight[:, :width])
    key = mm(operand, qkv_weight[:, width : 2 * width])
    value = mm(operand, qkv_weight[:, 2 * width :]).astype(bf16)
    d0 = lax.broadcasted_iota(jnp.int32, (group, group), 0)
    d1 = lax.broadcasted_iota(jnp.int32, (group, group), 1)
    same_head = lax.shift_right_logical(d0, head_dim.bit_length() - 1) == lax.shift_right_logical(
        d1, head_dim.bit_length() - 1
    )
    same_head = same_head.astype(f32).astype(bf16)

    def lanes(rows, cols, at, size):
        lane = lax.broadcasted_iota(jnp.int32, (rows, cols), 1)
        return ((lane >= at) & (lane < at + size)).astype(f32).astype(bf16)

    first_b = lanes(tokens, pair, 0, head_dim)
    second_b = lanes(tokens, pair, head_dim, head_dim)
    first = lax.broadcasted_iota(jnp.int32, (tokens, pair), 1) < head_dim

    def unit(part, scale):
        rounded = part.astype(bf16)
        inv = lax.rsqrt(mm(rounded * rounded, same_head) + 1e-06)
        if scale is not None:
            inv = inv * scale
        return (part * inv).astype(bf16)

    for g in range(width // group):
        at = g * group
        q = unit(query[:, at : at + group], scale_row[:, at : at + group])
        k = unit(key[:, at : at + group], None)
        v = value[:, at : at + group]
        k_rest = jnp.concatenate(
            [k[main:] * lanes(rest, group, h * head_dim, head_dim) for h in range(4)], axis=0
        )
        rest_score = lax.dot_general(q, k_rest, last, preferred_element_type=f32)
        if bias_ref is not None:
            rest_score = rest_score + bias_ref[:, main:]
        rest_weights = jnp.exp2(rest_score).astype(bf16)
        columns = []
        for h in range(4):
            side = h % 2
            own, other = (first_b, second_b)[side][:rest], (second_b, first_b)[side][:rest]
            v_rest = v[main:, (h // 2) * pair : (h // 2 + 1) * pair] * own + other
            zero = jnp.zeros_like(v_rest)
            columns.append(jnp.concatenate([v_rest if i == h else zero for i in range(4)], axis=0))
        rest_out = mm(rest_weights, jnp.concatenate(columns, axis=1))
        shares = []
        for h in range(4):
            cut = slice((h // 2) * pair, (h // 2 + 1) * pair)
            own = (first_b, second_b)[h % 2][:main]
            score = lax.dot_general(q[:, cut], k[:main, cut] * own, last, preferred_element_type=f32)
            if bias_ref is not None:
                score = score + bias_ref[:, :main]
            shares.append(jnp.exp2(score).astype(bf16))
        for p in range(2):
            cut = slice(p * pair, (p + 1) * pair)
            v_pair = v[:main, cut]
            both = []
            for side, (own, other) in enumerate(((first_b, second_b), (second_b, first_b))):
                h = 2 * p + side
                both.append(
                    mm(shares[h], v_pair * own[:main] + other[:main]) + rest_out[:, h * pair : (h + 1) * pair]
                )
            result = jnp.where(first, both[0], both[1])
            total = pltpu.roll(jnp.where(first, both[1], both[0]), head_dim, 1)
            store(slice(at + p * pair, at + (p + 1) * pair), (result / total).astype(bf16))


def scale_lanes(scale_ref, layer, width, heads):
    lane = lax.broadcasted_iota(jnp.int32, (1, width), 1)
    row = jnp.zeros((1, width), f32)
    for h in range(heads):
        row = jnp.where(lane >= h * (width // heads), scale_ref[layer, h] * LOG2E, row)
    return row


def norm_rows(values, gain_row, bias_row):
    average = jnp.mean(values, -1, keepdims=True)
    centred = values - average
    spread = jnp.mean(centred * centred, -1, keepdims=True)
    return centred * (lax.rsqrt(spread + 1e-05)) * gain_row + bias_row


def gelu_twice(x):
    c = 0.7978845608028654
    x = x.astype(bf16)
    one = jnp.ones((), bf16)
    inner = x * (jnp.asarray(c, bf16) + jnp.asarray(c * 0.044715, bf16) * (x * x))
    return x * (one + jnp.tanh(inner))


def finish_window(x, attended, out_weight, up_ref, down_ref, gain, bias):
    after = x + norm_rows(mm(attended, out_weight), gain[0:1], bias[0:1])
    after_b = after.astype(bf16)
    ff = up_ref.shape[1]
    step = min(512, ff)
    total = None
    for at in range(0, ff, step):
        hidden = gelu_twice(mm(after_b, up_ref[:, at : at + step]))
        part = mm(hidden, down_ref[at : at + step, :])
        total = part if total is None else total + part
    return after + norm_rows(0.5 * total, gain[1:2], bias[1:2])


def window_keys(ids_ref, j, cols, main, rest, levels, base, lat_total):
    run = HALF_LON * levels
    quarter = HALF_LAT * run
    shape = (1, cols)
    at = lax.broadcasted_iota(jnp.int32, shape, 1)
    t = jnp.where(at < main, at, main + ((at - main) & (rest - 1))).astype(f32)

    def cut(value, by):
        return jnp.floor((value + 0.5) * (1.0 / by))

    q = cut(t, quarter)
    half = cut(q, 2)
    block = q - 2 * half
    inside = t - quarter * q
    r = cut(inside, run)
    column = half * HALF_LON + cut(inside - run * r, levels)
    row = base + block * HALF_LAT + r
    key = jnp.zeros(shape, f32)
    ids = ids_ref[j * WIN_LAT, 0:1, :].astype(f32)
    for c in range(WIN_LON):
        key = jnp.where(column == c, ids[:, c : c + 1], key)
    band = jnp.where(row >= lat_total - WIN_LAT, 1.0, 0.0) + jnp.where(row >= lat_total - HALF_LAT, 1.0, 0.0)
    return key * 3 + band


ORDER = "FFFFSSFFSSLLSSLLLL"


def order(count):
    seen = {"F": 0, "S": 0, "L": 0}
    plan = []
    for kind in ORDER:
        plan.append(("FSL".index(kind), seen[kind]))
        seen[kind] += 1
    assert min(seen.values()) == max(seen.values()) == count
    return plan


def kernel(lat_size, x_hbm, ids_ref, qkv_hbm, out_hbm, up_hbm, down_hbm, gain_ref, bias_ref, scale_ref,
           x_s, first_s, op_s, att_s, send_s, send_own, back_s, back_own, mask_s, win_f, win_b,
           scale_s, qkv_s, out_s, up_s, down_s, w_sem, x_sem, send1, recv1, send2, recv2, ids_s, ids_sem):
    samples, lat_rows, lon_cols, levels, width = x_s.shape
    wins = lat_rows // WIN_LAT
    blocks = 2 * wins
    run = HALF_LON * levels
    quarter = HALF_LAT * run
    last_block = blocks - 1

    loads = [
        [
            pltpu.make_async_copy(src.at[layer], dst.at[layer], w_sem.at[layer, k])
            for k, (src, dst) in enumerate(
                ((qkv_hbm, qkv_s), (out_hbm, out_s), (up_hbm, up_s), (down_hbm, down_s))
            )
        ]
        for layer in range(2)
    ]

    def x_load(s):
        return pltpu.make_async_copy(x_hbm.at[s], x_s.at[s], x_sem.at[s])

    x_load(0).start()
    for copy in loads[0]:
        copy.start()
    for s in range(1, samples):
        x_load(s).start()
    for copy in loads[1]:
        copy.start()

    lon, lat = lax.axis_index("lon"), lax.axis_index("lat")
    lon_size = lax.axis_size("lon")
    west = lax.rem(lon + lon_size - 1, lon_size)
    east = lax.rem(lon + 1, lon_size)
    before = lax.rem(lat + lat_size - 1, lat_size)
    after = lax.rem(lat + 1, lat_size)

    barrier = pltpu.get_barrier_semaphore()
    peers = ((east, lat), (east, before), (lon, before), (lon, after), (west, lat), (west, after))
    for to_lon, to_lat in peers:
        pl.semaphore_signal(barrier, inc=1, device_id={"lon": to_lon, "lat": to_lat}, device_id_type=MESH)

    heads = scale_ref.shape[1]
    head_dim = width // heads
    rest = head_dim // 2
    tokens = 4 * quarter
    for layer in range(2):
        scale_s[layer : layer + 1, :] = scale_lanes(scale_ref, layer, width, heads)

    def remote(src, dst, send, recv, to_lon, to_lat):
        return pltpu.make_async_remote_copy(
            src_ref=src, dst_ref=dst, send_sem=send, recv_sem=recv,
            device_id={"lon": to_lon, "lat": to_lat}, device_id_type=MESH,
        )

    def ahead(s, k):
        if k == 0:
            return remote(send_s.at[s, pl.ds(1, 1)], op_s.at[s, 0, pl.ds(0, 1)], send1.at[s, k], recv1.at[s, k], east, lat)
        if k == 1:
            return remote(send_s.at[s, pl.ds(0, 1)], op_s.at[s, 0, pl.ds(last_block, 1)], send1.at[s, k], recv1.at[s, k], east, before)
        if k == 2:
            return remote(send_own.at[s], op_s.at[s, 1, pl.ds(last_block, 1)], send1.at[s, k], recv1.at[s, k], lon, before)
        j = k - 2
        return remote(send_s.at[s, pl.ds(2 * j, 2)], op_s.at[s, 0, pl.ds(2 * j - 1, 2)], send1.at[s, k], recv1.at[s, k], east, lat)

    def back(s, k):
        if k == 0:
            return remote(back_s.at[s, pl.ds(last_block - 1, 1)], att_s.at[s, 1, pl.ds(last_block, 1)], send2.at[s, k], recv2.at[s, k], west, lat)
        if k == 1:
            return remote(back_s.at[s, pl.ds(last_block, 1)], att_s.at[s, 1, pl.ds(0, 1)], send2.at[s, k], recv2.at[s, k], west, after)
        if k == 2:
            return remote(back_own.at[s], att_s.at[s, 0, pl.ds(0, 1)], send2.at[s, k], recv2.at[s, k], lon, after)
        j = k - 3
        return remote(back_s.at[s, pl.ds(2 * j, 2)], att_s.at[s, 1, pl.ds(2 * j + 1, 2)], send2.at[s, k], recv2.at[s, k], west, lat)

    def ids_copy():
        return remote(ids_ref, ids_s, ids_sem.at[0], ids_sem.at[1], east, lat)

    def make_masks():
        lat_total = lat_size * lat_rows
        cols = tokens + 3 * rest
        for j in range(wins):
            base = (lat * lat_rows + j * WIN_LAT).astype(f32)
            key = window_keys(ids_s, j, cols, tokens - rest, rest, levels, base, lat_total)
            kinds = lax.broadcasted_iota(jnp.int32, (16, cols), 0).astype(f32)
            member = (kinds == key).astype(f32).astype(bf16)
            same = lax.dot_general(member[:, :tokens], member, (((0,), (0,)), ((), ())), preferred_element_type=f32)
            mask_s[j] = (same - 1.0) * 1e30

    copies = 3 + wins - 1

    def store(cut, value):
        win_b[:, cut] = value

    def layer_first(i, carry):
        s, j = lax.div(i, wins), lax.rem(i, wins)

        @pl.when(j == 0)
        def _():
            x_load(s).wait()

        @pl.when(i == 0)
        def _():
            loads[0][0].wait()

        for half in range(2):
            for block in range(2):
                for r in range(HALF_LAT):
                    row = (half * 2 + block) * quarter + r * run
                    part = x_s[s, j * WIN_LAT + block * HALF_LAT + r, half * HALF_LON : (half + 1) * HALF_LON]
                    first_s[i, row : row + run, :] = part.reshape(run, width)
        attend_window(first_s[i].astype(bf16), qkv_s.at[0], scale_s[0:1, :], None, head_dim, store)

        @pl.when(i == 0)
        def _():
            for copy in loads[0][1:]:
                copy.wait()

        first_s[i] = finish_window(first_s[i], win_b[...], out_s[0], up_s.at[0], down_s.at[0], gain_ref[0], bias_ref[0])

        def block_of(q):
            return first_s[i, q * quarter : (q + 1) * quarter, :].astype(bf16)

        @pl.when(i == 0)
        def _():
            pl.semaphore_wait(barrier, len(peers))
            ids_copy().start()

        send_s[s, 2 * j] = block_of(2)
        send_s[s, 2 * j + 1] = block_of(3)
        op_s[s, 1, 2 * j] = block_of(1)

        @pl.when(j == 0)
        def _():
            send_own[s, 0] = block_of(0)
            for k in range(3):
                ahead(s, k).start()

        for jj in range(1, wins):

            @pl.when(j == jj)
            def _():
                op_s[s, 1, 2 * jj - 1] = block_of(0)
                ahead(s, 2 + jj).start()

        return carry

    def shifted_attention(i, carry):
        s, j = lax.div(i, wins), lax.rem(i, wins)

        @pl.when(j == 0)
        def _():
            ahead(s, 0).wait_recv()

        for jj in range(1, wins):

            @pl.when(j == jj - 1)
            def _():
                ahead(s, 2 + jj).wait_recv()

        @pl.when(j == wins - 1)
        def _():
            for k in (1, 2):
                ahead(s, k).wait_recv()

        @pl.when(i == 0)
        def _():
            loads[1][0].wait()
            ids_copy().wait_recv()
            make_masks()

        for half in range(2):
            for block in range(2):
                row = (half * 2 + block) * quarter
                win_f[row : row + quarter, :] = op_s[s, half, 2 * j + block].astype(f32)
        attend_window(win_f[...].astype(bf16), qkv_s.at[1], scale_s[1:2, :], mask_s.at[j], head_dim, store)
        win_f[...] = win_b[...].astype(f32)

        def block_of(q):
            return win_f[q * quarter : (q + 1) * quarter, :].astype(bf16)

        att_s[s, 0, 2 * j + 1] = block_of(2)
        back_s[s, 2 * j] = block_of(0)
        back_s[s, 2 * j + 1] = block_of(1)

        @pl.when(j == wins - 1)
        def _():
            back_own[s, 0] = block_of(3)
            for k in range(3):
                back(s, k).start()

        for jj in range(wins - 1):

            @pl.when(j == jj)
            def _():
                att_s[s, 0, 2 * jj + 2] = block_of(3)
                back(s, 3 + jj).start()

        return carry

    def layer_last(i, carry):
        s, j = lax.div(i, wins), lax.rem(i, wins)

        @pl.when(j == 0)
        def _():
            for k in (1, 2):
                back(s, k).wait_recv()

        for jj in range(wins - 1):

            @pl.when(j == jj)
            def _():
                back(s, 3 + jj).wait_recv()

        @pl.when(j == wins - 1)
        def _():
            back(s, 0).wait_recv()

        @pl.when(i == 0)
        def _():
            for copy in loads[1][1:]:
                copy.wait()

        for half in range(2):
            for block in range(2):
                row = (half * 2 + block) * quarter
                win_f[row : row + quarter, :] = att_s[s, half, 2 * j + block].astype(f32)
        win_f[...] = finish_window(
            first_s[i], win_f[...].astype(bf16), out_s[1], up_s.at[1], down_s.at[1], gain_ref[1], bias_ref[1]
        )
        for half in range(2):
            for block in range(2):
                for r in range(HALF_LAT):
                    row = (half * 2 + block) * quarter + r * run
                    x_s[s, j * WIN_LAT + block * HALF_LAT + r, half * HALF_LON : (half + 1) * HALF_LON] = win_f[
                        row : row + run, :
                    ].reshape(HALF_LON, levels, width)
        return carry

    plan = order(samples * wins)

    def pick(t, values):
        value = jnp.int32(values[0])
        for n in range(1, len(values)):
            if values[n] != values[n - 1]:
                value = jnp.where(t >= n, jnp.int32(values[n]), value)
        return value

    def advance(t, carry):
        kind = pick(t, [k for k, _ in plan])
        i = pick(t, [n for _, n in plan])
        for k, step in enumerate((layer_first, shifted_attention, layer_last)):

            @pl.when(kind == k)
            def _():
                step(i, 0)

        return carry

    lax.fori_loop(0, len(plan), advance, 0)

    def drain(s, carry):
        for k in range(copies):
            ahead(s, k).wait_send()
            back(s, k).wait_send()
        return carry

    lax.fori_loop(0, samples, drain, 0)
    ids_copy().wait_send()


def local(stream, region_ids, qkv_weight, out_weight, up_weight, down_weight, norm_gain, norm_bias, logit_scale):
    samples, levels, lat_rows, lon_cols, width = stream.shape
    assert lon_cols == WIN_LON
    wins = lat_rows // WIN_LAT
    blocks = 2 * wins
    quarter = levels * HALF_LAT * HALF_LON
    tokens = 4 * quarter
    copies = 3 + wins - 1
    x = stream.transpose(0, 2, 3, 1, 4)
    ids = region_ids.transpose(1, 0, 2)
    hbm = pl.BlockSpec(memory_space=pl.ANY)
    vmem = pl.BlockSpec(memory_space=pltpu.VMEM)
    smem = pl.BlockSpec(memory_space=pltpu.SMEM)
    sem = pltpu.SemaphoreType.DMA
    y = pl.pallas_call(
        functools.partial(kernel, lax.axis_size("lat")),
        in_specs=[hbm, vmem, hbm, hbm, hbm, hbm, vmem, vmem, smem],
        out_specs=vmem,
        out_shape=pltpu.VMEM(x.shape, f32),
        scratch_shapes=[
            pltpu.VMEM((samples * wins, tokens, width), f32),
            pltpu.VMEM((samples, 2, blocks, quarter, width), bf16),
            pltpu.VMEM((samples, 2, blocks, quarter, width), bf16),
            pltpu.VMEM((samples, blocks, quarter, width), bf16),
            pltpu.VMEM((samples, 1, quarter, width), bf16),
            pltpu.VMEM((samples, blocks, quarter, width), bf16),
            pltpu.VMEM((samples, 1, quarter, width), bf16),
            pltpu.VMEM((wins, tokens, tokens + 3 * (width // logit_scale.shape[1] // 2)), f32),
            pltpu.VMEM((tokens, width), f32),
            pltpu.VMEM((tokens, width), bf16),
            pltpu.VMEM((2, width), f32),
            pltpu.VMEM(qkv_weight.shape, bf16),
            pltpu.VMEM(out_weight.shape, bf16),
            pltpu.VMEM(up_weight.shape, bf16),
            pltpu.VMEM(down_weight.shape, bf16),
            sem((2, 4)),
            sem((samples,)),
            sem((samples, copies)),
            sem((samples, copies)),
            sem((samples, copies)),
            sem((samples, copies)),
            pltpu.VMEM(ids.shape, jnp.int32),
            sem((2,)),
        ],
        compiler_params=pltpu.CompilerParams(
            vmem_limit_bytes=VMEM_LIMIT, collective_id=0, has_side_effects=True
        ),
        name="both_layers",
    )(x, ids, qkv_weight, out_weight, up_weight, down_weight, norm_gain, norm_bias, logit_scale)
    return y.transpose(0, 3, 1, 2, 4)


def solution(mesh):
    in_specs = (P("ens", None, "lat", "lon", None), P("ens", "lat", "lon")) + (P(),) * 7
    out_specs = P("ens", None, "lat", "lon", None)
    return jax.shard_map(local, mesh=mesh, in_specs=in_specs, out_specs=out_specs, check_vma=False)
```

```python
import functools

import jax
import jax.numpy as jnp
from jax import lax
from jax.experimental import pallas as pl
from jax.experimental.pallas import tpu as pltpu
from jax.sharding import PartitionSpec as P

WIN_LAT = 6
WIN_LON = 12
HALF_LAT = WIN_LAT // 2
HALF_LON = WIN_LON // 2
LOG2E = 1.4426950408889634
VMEM_LIMIT = 60 * 1024 * 1024

f32 = jnp.float32
bf16 = jnp.bfloat16


MESH = pl.DeviceIdType.MESH


def mm(a, b):
    return jnp.dot(a, b, preferred_element_type=f32)


def head_blocks(group, head_dim):
    d0 = lax.broadcasted_iota(jnp.int32, (group, group), 0)
    d1 = lax.broadcasted_iota(jnp.int32, (group, group), 1)
    shift = head_dim.bit_length() - 1
    same_head = lax.shift_right_logical(d0, shift) == lax.shift_right_logical(d1, shift)
    return same_head.astype(f32).astype(bf16)


def when(condition):
    if isinstance(condition, bool):
        return (lambda run: run()) if condition else (lambda run: None)
    return pl.when(condition)


def project_windows(operand, qkv_weight, tokens, head_dim):
    rows, width = operand.shape
    group = 4 * head_dim
    groups = width // group
    same_head = head_blocks(group, head_dim)

    def project(block, g):
        at = block * width + g * group
        return mm(operand, qkv_weight[:, at : at + group])

    def square_sum(part):
        rounded = part.astype(bf16)
        return mm(rounded * rounded, same_head)

    raw = [(project(0, g), project(1, g)) for g in range(groups)]
    sums = [[square_sum(part) for part in raw[g]] for g in range(groups)]
    value = [project(2, g).astype(bf16) for g in range(groups)]
    windows = []
    for at in range(0, rows, tokens):
        cut = slice(at, at + tokens)
        windows.append(
            (
                [[part[cut] for part in raw[g]] for g in range(groups)],
                [[part[cut] for part in sums[g]] for g in range(groups)],
                [part[cut] for part in value],
            )
        )
    return windows


def attend_window(projected, scale_row, bias_ref, head_dim, store, between=None):
    raw, sums, value = projected
    tokens = value[0].shape[0]
    width = sum(part.shape[1] for part in value)
    group = 4 * head_dim
    pair = 2 * head_dim
    rest = pair // 4
    main = tokens - rest
    last = (((1,), (1,)), ((), ()))
    groups = width // group

    def lanes(rows, cols, at, size):
        lane = lax.broadcasted_iota(jnp.int32, (rows, cols), 1)
        return ((lane >= at) & (lane < at + size)).astype(f32).astype(bf16)

    first_b = lanes(tokens, pair, 0, head_dim)
    second_b = lanes(tokens, pair, head_dim, head_dim)
    first = lax.broadcasted_iota(jnp.int32, (tokens, pair), 1) < head_dim

    def unit(part, total, scale):
        inv = lax.rsqrt(total + 1e-06)
        if scale is not None:
            inv = inv * scale
        return (part * inv).astype(bf16)

    def rest_shares(q, k):
        k_rest = jnp.concatenate(
            [k[main:] * lanes(rest, group, h * head_dim, head_dim) for h in range(4)], axis=0
        )
        score = lax.dot_general(q, k_rest, last, preferred_element_type=f32)
        if bias_ref is not None:
            score = score + bias_ref[:, main:]
        return jnp.exp2(score).astype(bf16)

    def rest_part(weights, v):
        columns = []
        for h in range(4):
            side = h % 2
            own, other = (first_b, second_b)[side][:rest], (second_b, first_b)[side][:rest]
            v_rest = v[main:, (h // 2) * pair : (h // 2 + 1) * pair] * own + other
            zero = jnp.zeros_like(v_rest)
            columns.append(jnp.concatenate([v_rest if i == h else zero for i in range(4)], axis=0))
        return mm(weights, jnp.concatenate(columns, axis=1))

    def main_share(q, k, h):
        cut = slice((h // 2) * pair, (h // 2 + 1) * pair)
        own = (first_b, second_b)[h % 2][:main]
        score = lax.dot_general(q[:, cut], k[:main, cut] * own, last, preferred_element_type=f32)
        if bias_ref is not None:
            score = score + bias_ref[:, :main]
        return jnp.exp2(score).astype(bf16)

    def main_part(share, v, h):
        cut = slice((h // 2) * pair, (h // 2 + 1) * pair)
        own, other = ((first_b, second_b), (second_b, first_b))[h % 2]
        return mm(share, v[:main, cut] * own[:main] + other[:main])

    def combine(g, p, even, odd):
        result = jnp.where(first, even, odd)
        total = pltpu.roll(jnp.where(first, odd, even), head_dim, 1)
        at = g * group + p * pair
        store(slice(at, at + pair), result / total)

    units = [None] * groups

    def scaled(g):
        at = g * group
        return (
            unit(raw[g][0], sums[g][0], scale_row[:, at : at + group]),
            unit(raw[g][1], sums[g][1], None),
        )

    units[0] = scaled(0)

    shares = [rest_shares(*units[0])] + [main_share(*units[0], h) for h in range(4)]
    for g in range(groups):
        following = g + 1 < groups
        if following:
            units[g + 1] = scaled(g + 1)
        ahead = []
        rest_out = rest_part(shares[0], value[g])
        if following:
            ahead.append(rest_shares(*units[g + 1]))
        elif between is not None and g > 0:
            between(g - 1)
        parts = []
        for h in range(4):
            parts.append(main_part(shares[1 + h], value[g], h) + rest_out[:, h * pair : (h + 1) * pair])
            if following:
                ahead.append(main_share(*units[g + 1], h))
            if h % 2 == 1:
                combine(g, h // 2, parts[h - 1], parts[h])
        shares = ahead


def scale_lanes(scale_ref, layer, width, heads):
    lane = lax.broadcasted_iota(jnp.int32, (1, width), 1)
    row = jnp.zeros((1, width), f32)
    for h in range(heads):
        row = jnp.where(lane >= h * (width // heads), scale_ref[layer, h] * LOG2E, row)
    return row


def norm_rows(values, gain_row, bias_row):
    average = jnp.mean(values, -1, keepdims=True)
    centred = values - average
    spread = jnp.mean(centred * centred, -1, keepdims=True)
    return centred * (lax.rsqrt(spread + 1e-05)) * gain_row + bias_row


def gelu_twice(x):
    c = 0.7978845608028654
    x = x.astype(bf16)
    one = jnp.ones((), bf16)
    inner = x * (jnp.asarray(c, bf16) + jnp.asarray(c * 0.044715, bf16) * (x * x))
    return x * (one + jnp.tanh(inner))


def finish_window(x, projected, up_ref, down_ref, gain, bias):
    after = x + norm_rows(projected, gain[0:1], bias[0:1])
    after_b = after.astype(bf16)
    ff = up_ref.shape[1]
    step = min(512, ff)
    total = None
    for at in range(0, ff, step):
        hidden = gelu_twice(mm(after_b, up_ref[:, at : at + step]))
        part = mm(hidden, down_ref[at : at + step, :])
        total = part if total is None else total + part
    return after + norm_rows(0.5 * total, gain[1:2], bias[1:2])


def window_keys(ids_ref, j, cols, main, rest, levels, base, lat_total):
    run = HALF_LON * levels
    quarter = HALF_LAT * run
    shape = (1, cols)
    at = lax.broadcasted_iota(jnp.int32, shape, 1)
    t = jnp.where(at < main, at, main + ((at - main) & (rest - 1))).astype(f32)

    def cut(value, by):
        return jnp.floor((value + 0.5) * (1.0 / by))

    q = cut(t, quarter)
    half = cut(q, 2)
    block = q - 2 * half
    inside = t - quarter * q
    r = cut(inside, run)
    column = half * HALF_LON + cut(inside - run * r, levels)
    row = base + block * HALF_LAT + r
    key = jnp.zeros(shape, f32)
    ids = ids_ref[j * WIN_LAT, 0:1, :].astype(f32)
    for c in range(WIN_LON):
        key = jnp.where(column == c, ids[:, c : c + 1], key)
    band = jnp.where(row >= lat_total - WIN_LAT, 1.0, 0.0) + jnp.where(row >= lat_total - HALF_LAT, 1.0, 0.0)
    return key * 3 + band


PAIR_F = False
PAIR_L = (lambda s, n: True)


def order(samples, wins):
    plan = []
    for k in range(samples + 2):
        for s, whole, single in ((k, PAIR_F and k > 0, "f"), (k - 1, False, "S"), (k - 2, PAIR_L(k - 2, samples), "l")):
            if 0 <= s < samples:
                plan += [(single.upper(), s)] if whole else [(single, s * wins + j) for j in range(wins)]
    return plan


def kernel(lat_size, x_hbm, ids_ref, qkv_hbm, out_hbm, up_hbm, down_hbm, gain_ref, bias_ref, scale_ref,
           x_s, first_s, op_s, att_s, send_s, send_own, back_s, back_own, mask_s, keep_s, win_b,
           scale_s, qkv_s, out_s, up_s, down_s, w_sem, x_sem, send1, recv1, send2, recv2, ids_s, ids_sem):
    samples, lat_rows, lon_cols, levels, width = x_s.shape
    wins = lat_rows // WIN_LAT
    blocks = 2 * wins
    run = HALF_LON * levels
    quarter = HALF_LAT * run
    last_block = blocks - 1

    loads = [
        [
            pltpu.make_async_copy(src.at[layer], dst.at[layer], w_sem.at[layer, k])
            for k, (src, dst) in enumerate(
                ((qkv_hbm, qkv_s), (out_hbm, out_s), (up_hbm, up_s), (down_hbm, down_s))
            )
        ]
        for layer in range(2)
    ]

    def x_load(s):
        return pltpu.make_async_copy(x_hbm.at[s], x_s.at[s], x_sem.at[s])

    x_load(0).start()
    for copy in loads[0]:
        copy.start()
    for s in range(1, samples):
        x_load(s).start()
    for copy in loads[1]:
        copy.start()

    lon, lat = lax.axis_index("lon"), lax.axis_index("lat")
    lon_size = lax.axis_size("lon")
    west = lax.rem(lon + lon_size - 1, lon_size)
    east = lax.rem(lon + 1, lon_size)
    before = lax.rem(lat + lat_size - 1, lat_size)
    after = lax.rem(lat + 1, lat_size)

    barrier = pltpu.get_barrier_semaphore()
    peers = ((east, lat), (east, before), (lon, before), (lon, after), (west, lat), (west, after))
    for to_lon, to_lat in peers:
        pl.semaphore_signal(barrier, inc=1, device_id={"lon": to_lon, "lat": to_lat}, device_id_type=MESH)

    heads = scale_ref.shape[1]
    head_dim = width // heads
    rest = head_dim // 2
    tokens = 4 * quarter
    for layer in range(2):
        scale_s[layer : layer + 1, :] = scale_lanes(scale_ref, layer, width, heads)

    def remote(src, dst, send, recv, to_lon, to_lat):
        return pltpu.make_async_remote_copy(
            src_ref=src, dst_ref=dst, send_sem=send, recv_sem=recv,
            device_id={"lon": to_lon, "lat": to_lat}, device_id_type=MESH,
        )

    def ahead(s, k):
        if k == 0:
            return remote(send_s.at[s, pl.ds(1, 1)], op_s.at[s, 0, pl.ds(0, 1)], send1.at[s, k], recv1.at[s, k], east, lat)
        if k == 1:
            return remote(send_s.at[s, pl.ds(0, 1)], op_s.at[s, 0, pl.ds(last_block, 1)], send1.at[s, k], recv1.at[s, k], east, before)
        if k == 2:
            return remote(send_own.at[s], op_s.at[s, 1, pl.ds(last_block, 1)], send1.at[s, k], recv1.at[s, k], lon, before)
        j = k - 2
        return remote(send_s.at[s, pl.ds(2 * j, 2)], op_s.at[s, 0, pl.ds(2 * j - 1, 2)], send1.at[s, k], recv1.at[s, k], east, lat)

    def back(s, k):
        if k == 0:
            return remote(back_s.at[s, pl.ds(last_block - 1, 1)], att_s.at[s, 1, pl.ds(last_block, 1)], send2.at[s, k], recv2.at[s, k], west, lat)
        if k == 1:
            return remote(back_s.at[s, pl.ds(last_block, 1)], att_s.at[s, 1, pl.ds(0, 1)], send2.at[s, k], recv2.at[s, k], west, after)
        if k == 2:
            return remote(back_own.at[s], att_s.at[s, 0, pl.ds(0, 1)], send2.at[s, k], recv2.at[s, k], lon, after)
        j = k - 3
        return remote(back_s.at[s, pl.ds(2 * j, 2)], att_s.at[s, 1, pl.ds(2 * j + 1, 2)], send2.at[s, k], recv2.at[s, k], west, lat)

    def ids_copy():
        return remote(ids_ref, ids_s, ids_sem.at[0], ids_sem.at[1], east, lat)

    def make_masks():
        lat_total = lat_size * lat_rows
        cols = tokens + 3 * rest
        for j in range(wins):
            base = (lat * lat_rows + j * WIN_LAT).astype(f32)
            key = window_keys(ids_s, j, cols, tokens - rest, rest, levels, base, lat_total)
            kinds = lax.broadcasted_iota(jnp.int32, (16, cols), 0).astype(f32)
            member = (kinds == key).astype(f32).astype(bf16)
            same = lax.dot_general(member[:, :tokens], member, (((0,), (0,)), ((), ())), preferred_element_type=f32)
            mask_s[j] = (same - 1.0) * 1e30

    copies = 3 + wins - 1

    def layer_first(items, first):
        for i, s, j in items:

            @when(j == 0)
            def _():
                x_load(s).wait()

        if first:

            @pl.when(items[0][0] == 0)
            def _():
                loads[0][0].wait()

        for i, s, j in items:
            for half in range(2):
                for block in range(2):
                    for r in range(HALF_LAT):
                        row = (half * 2 + block) * quarter + r * run
                        part = x_s[s, j * WIN_LAT + block * HALF_LAT + r, half * HALF_LON : (half + 1) * HALF_LON]
                        first_s[i, row : row + run, :] = part.reshape(run, width)

        if first:

            @pl.when(items[0][0] == 0)
            def _():
                for copy in loads[0][1:]:
                    copy.wait()

        def residual():
            return jnp.concatenate([first_s[i] for i, _, _ in items], axis=0)

        rows = len(items) * tokens
        products = []

        def project(g):
            cut = slice(g * 4 * head_dim, (g + 1) * 4 * head_dim)
            products.append(mm(win_b[:rows, cut], out_s[0, cut, :]))

        windows = project_windows(residual().astype(bf16), qkv_s.at[0], tokens, head_dim)
        for n, window in enumerate(windows):

            def store(cut, value):
                win_b[n * tokens : (n + 1) * tokens, cut] = value.astype(bf16)

            attend_window(
                window, scale_s[0:1, :], None, head_dim, store, project if n == len(windows) - 1 else None
            )
        project(len(products))
        total = products[0]
        for part in products[1:]:
            total = total + part
        result = finish_window(residual(), total, up_s.at[0], down_s.at[0], gain_ref[0], bias_ref[0])

        for n, (i, s, j) in enumerate(items):
            mine = result[n * tokens : (n + 1) * tokens]
            first_s[i] = mine

            def block_of(q):
                return mine[q * quarter : (q + 1) * quarter, :].astype(bf16)

            send_s[s, 2 * j] = block_of(2)
            send_s[s, 2 * j + 1] = block_of(3)
            op_s[s, 1, 2 * j] = block_of(1)
            if isinstance(j, int):
                if j == 0:
                    send_own[s, 0] = block_of(0)
                else:
                    op_s[s, 1, 2 * j - 1] = block_of(0)
            else:
                keep_s[...] = block_of(0)

        if first:

            @pl.when(items[0][0] == 0)
            def _():
                pl.semaphore_wait(barrier, len(peers))
                ids_copy().start()

        for i, s, j in items:

            @when(j == 0)
            def _():
                if not isinstance(j, int):
                    send_own[s, 0] = keep_s[...]
                for k in range(3):
                    ahead(s, k).start()

            for jj in range(1, wins):

                @when(j == jj)
                def _():
                    if not isinstance(j, int):
                        op_s[s, 1, 2 * jj - 1] = keep_s[...]
                    ahead(s, 2 + jj).start()

    def first_window(i):
        layer_first([(i, lax.div(i, wins), lax.rem(i, wins))], True)

    def first_sample(s):
        layer_first([(s * wins + j, s, j) for j in range(wins)], False)

    def shifted_attention(i):
        s, j = lax.div(i, wins), lax.rem(i, wins)

        @pl.when(j == 0)
        def _():
            ahead(s, 0).wait_recv()

        for jj in range(1, wins):

            @pl.when(j == jj - 1)
            def _():
                ahead(s, 2 + jj).wait_recv()

        @pl.when(j == wins - 1)
        def _():
            for k in (1, 2):
                ahead(s, k).wait_recv()

        @pl.when(i == 0)
        def _():
            loads[1][0].wait()
            ids_copy().wait_recv()
            make_masks()

        operand = jnp.concatenate(
            [op_s[s, half, 2 * j + block].astype(f32) for half in range(2) for block in range(2)], axis=0
        ).astype(bf16)

        def store(cut, value):
            parts = [value[q * quarter : (q + 1) * quarter, :].astype(bf16) for q in range(4)]
            back_s[s, 2 * j, :, cut] = parts[0]
            back_s[s, 2 * j + 1, :, cut] = parts[1]
            att_s[s, 0, 2 * j + 1, :, cut] = parts[2]
            keep_s[:, cut] = parts[3]

        window = project_windows(operand, qkv_s.at[1], tokens, head_dim)[0]
        attend_window(window, scale_s[1:2, :], mask_s.at[j], head_dim, store)

        @pl.when(j == wins - 1)
        def _():
            back_own[s, 0] = keep_s[...]
            for k in range(3):
                back(s, k).start()

        for jj in range(wins - 1):

            @pl.when(j == jj)
            def _():
                att_s[s, 0, 2 * jj + 2] = keep_s[...]
                back(s, 3 + jj).start()

    def layer_last(items):
        for i, s, j in items:

            @when(j == 0)
            def _():
                for k in (1, 2):
                    back(s, k).wait_recv()

            for jj in range(wins - 1):

                @when(j == jj)
                def _():
                    back(s, 3 + jj).wait_recv()

            @when(j == wins - 1)
            def _():
                back(s, 0).wait_recv()

        @pl.when(items[0][0] == 0)
        def _():
            for copy in loads[1][1:]:
                copy.wait()

        attended = jnp.concatenate(
            [att_s[s, half, 2 * j + block].astype(f32) for _, s, j in items for half in range(2) for block in range(2)],
            axis=0,
        ).astype(bf16)
        result = finish_window(
            jnp.concatenate([first_s[i] for i, _, _ in items], axis=0),
            mm(attended, out_s[1]), up_s.at[1], down_s.at[1], gain_ref[1], bias_ref[1],
        )
        for n, (_, s, j) in enumerate(items):
            for half in range(2):
                for block in range(2):
                    for r in range(HALF_LAT):
                        row = n * tokens + (half * 2 + block) * quarter + r * run
                        x_s[s, j * WIN_LAT + block * HALF_LAT + r, half * HALF_LON : (half + 1) * HALF_LON] = result[
                            row : row + run, :
                        ].reshape(HALF_LON, levels, width)

    def last_window(i):
        layer_last([(i, lax.div(i, wins), lax.rem(i, wins))])

    def last_sample(s):
        layer_last([(s * wins + j, s, j) for j in range(wins)])

    plan = order(samples, wins)
    steps = {"f": first_window, "F": first_sample, "S": shifted_attention, "l": last_window, "L": last_sample}
    kinds = [kind for kind in steps if any(kind == k for k, _ in plan)]

    def pick(t, values):
        value = jnp.int32(values[0])
        for n in range(1, len(values)):
            if values[n] != values[n - 1]:
                value = jnp.where(t >= n, jnp.int32(values[n]), value)
        return value

    def advance(t, carry):
        kind = pick(t, [kinds.index(k) for k, _ in plan])
        n = pick(t, [n for _, n in plan])
        for k, name in enumerate(kinds):

            @pl.when(kind == k)
            def _():
                steps[name](n)

        return carry

    lax.fori_loop(0, len(plan), advance, 0)

    def drain(s, carry):
        for k in range(copies):
            ahead(s, k).wait_send()
            back(s, k).wait_send()
        return carry

    lax.fori_loop(0, samples, drain, 0)
    ids_copy().wait_send()


def local(stream, region_ids, qkv_weight, out_weight, up_weight, down_weight, norm_gain, norm_bias, logit_scale):
    samples, levels, lat_rows, lon_cols, width = stream.shape
    assert lon_cols == WIN_LON
    wins = lat_rows // WIN_LAT
    blocks = 2 * wins
    quarter = levels * HALF_LAT * HALF_LON
    tokens = 4 * quarter
    copies = 3 + wins - 1
    x = stream.transpose(0, 2, 3, 1, 4)
    ids = region_ids.transpose(1, 0, 2)
    hbm = pl.BlockSpec(memory_space=pl.ANY)
    vmem = pl.BlockSpec(memory_space=pltpu.VMEM)
    smem = pl.BlockSpec(memory_space=pltpu.SMEM)
    sem = pltpu.SemaphoreType.DMA
    y = pl.pallas_call(
        functools.partial(kernel, lax.axis_size("lat")),
        in_specs=[hbm, vmem, hbm, hbm, hbm, hbm, vmem, vmem, smem],
        out_specs=vmem,
        out_shape=pltpu.VMEM(x.shape, f32),
        scratch_shapes=[
            pltpu.VMEM((samples * wins, tokens, width), f32),
            pltpu.VMEM((samples, 2, blocks, quarter, width), bf16),
            pltpu.VMEM((samples, 2, blocks, quarter, width), bf16),
            pltpu.VMEM((samples, blocks, quarter, width), bf16),
            pltpu.VMEM((samples, 1, quarter, width), bf16),
            pltpu.VMEM((samples, blocks, quarter, width), bf16),
            pltpu.VMEM((samples, 1, quarter, width), bf16),
            pltpu.VMEM((wins, tokens, tokens + 3 * (width // logit_scale.shape[1] // 2)), f32),
            pltpu.VMEM((quarter, width), bf16),
            pltpu.VMEM((wins * tokens, width), bf16),
            pltpu.VMEM((2, width), f32),
            pltpu.VMEM(qkv_weight.shape, bf16),
            pltpu.VMEM(out_weight.shape, bf16),
            pltpu.VMEM(up_weight.shape, bf16),
            pltpu.VMEM(down_weight.shape, bf16),
            sem((2, 4)),
            sem((samples,)),
            sem((samples, copies)),
            sem((samples, copies)),
            sem((samples, copies)),
            sem((samples, copies)),
            pltpu.VMEM(ids.shape, jnp.int32),
            sem((2,)),
        ],
        compiler_params=pltpu.CompilerParams(
            vmem_limit_bytes=VMEM_LIMIT, collective_id=0, has_side_effects=True
        ),
        name="both_layers",
    )(x, ids, qkv_weight, out_weight, up_weight, down_weight, norm_gain, norm_bias, logit_scale)
    return y.transpose(0, 3, 1, 2, 4)


def solution(mesh):
    in_specs = (P("ens", None, "lat", "lon", None), P("ens", "lat", "lon")) + (P(),) * 7
    out_specs = P("ens", None, "lat", "lon", None)
    return jax.shard_map(local, mesh=mesh, in_specs=in_specs, out_specs=out_specs, check_vma=False)
```

```python
import functools

import jax
import jax.numpy as jnp
from jax import lax
from jax.experimental import pallas as pl
from jax.experimental.pallas import tpu as pltpu
from jax.sharding import PartitionSpec as P

WIN_LAT = 6
WIN_LON = 12
HALF_LAT = WIN_LAT // 2
HALF_LON = WIN_LON // 2
LOG2E = 1.4426950408889634
VMEM_LIMIT = 60 * 1024 * 1024

f32 = jnp.float32
bf16 = jnp.bfloat16


MESH = pl.DeviceIdType.MESH


def mm(a, b):
    return jnp.dot(a, b, preferred_element_type=f32)


def head_blocks(group, head_dim):
    d0 = lax.broadcasted_iota(jnp.int32, (group, group), 0)
    d1 = lax.broadcasted_iota(jnp.int32, (group, group), 1)
    shift = head_dim.bit_length() - 1
    same_head = lax.shift_right_logical(d0, shift) == lax.shift_right_logical(d1, shift)
    return same_head.astype(f32).astype(bf16)


def when(condition):
    if isinstance(condition, bool):
        return (lambda run: run()) if condition else (lambda run: None)
    return pl.when(condition)


def project_windows(operand, qkv_weight, tokens, head_dim):
    rows, width = operand.shape
    group = 4 * head_dim
    groups = width // group
    same_head = head_blocks(group, head_dim)

    def project(block, g):
        at = block * width + g * group
        return mm(operand, qkv_weight[:, at : at + group])

    def square_sum(part):
        rounded = part.astype(bf16)
        return mm(rounded * rounded, same_head)

    raw = [(project(0, g), project(1, g)) for g in range(groups)]
    sums = [[square_sum(part) for part in raw[g]] for g in range(groups)]
    value = [project(2, g).astype(bf16) for g in range(groups)]
    windows = []
    for at in range(0, rows, tokens):
        cut = slice(at, at + tokens)
        windows.append(
            (
                [[part[cut] for part in raw[g]] for g in range(groups)],
                [[part[cut] for part in sums[g]] for g in range(groups)],
                [part[cut] for part in value],
            )
        )
    return windows


def attend_window(projected, scale_row, bias_ref, head_dim, store, between=None):
    raw, sums, value = projected
    tokens = value[0].shape[0]
    width = sum(part.shape[1] for part in value)
    group = 4 * head_dim
    pair = 2 * head_dim
    rest = pair // 4
    main = tokens - rest
    last = (((1,), (1,)), ((), ()))
    groups = width // group

    def lanes(rows, cols, at, size):
        lane = lax.broadcasted_iota(jnp.int32, (rows, cols), 1)
        return ((lane >= at) & (lane < at + size)).astype(f32).astype(bf16)

    first_b = lanes(tokens, pair, 0, head_dim)
    second_b = lanes(tokens, pair, head_dim, head_dim)
    first = lax.broadcasted_iota(jnp.int32, (tokens, pair), 1) < head_dim

    def unit(part, total, scale):
        inv = lax.rsqrt(total + 1e-06)
        if scale is not None:
            inv = inv * scale
        return (part * inv).astype(bf16)

    def rest_shares(q, k):
        k_rest = jnp.concatenate(
            [k[main:] * lanes(rest, group, h * head_dim, head_dim) for h in range(4)], axis=0
        )
        score = lax.dot_general(q, k_rest, last, preferred_element_type=f32)
        if bias_ref is not None:
            score = score + bias_ref[:, main:]
        return jnp.exp2(score).astype(bf16)

    def rest_part(weights, v):
        columns = []
        for h in range(4):
            side = h % 2
            own, other = (first_b, second_b)[side][:rest], (second_b, first_b)[side][:rest]
            v_rest = v[main:, (h // 2) * pair : (h // 2 + 1) * pair] * own + other
            zero = jnp.zeros_like(v_rest)
            columns.append(jnp.concatenate([v_rest if i == h else zero for i in range(4)], axis=0))
        return mm(weights, jnp.concatenate(columns, axis=1))

    def main_share(q, k, h):
        cut = slice((h // 2) * pair, (h // 2 + 1) * pair)
        own = (first_b, second_b)[h % 2][:main]
        score = lax.dot_general(q[:, cut], k[:main, cut] * own, last, preferred_element_type=f32)
        if bias_ref is not None:
            score = score + bias_ref[:, :main]
        return jnp.exp2(score).astype(bf16)

    def main_part(share, v, h):
        cut = slice((h // 2) * pair, (h // 2 + 1) * pair)
        own, other = ((first_b, second_b), (second_b, first_b))[h % 2]
        return mm(share, v[:main, cut] * own[:main] + other[:main])

    def combine(g, p, even, odd):
        result = jnp.where(first, even, odd)
        total = pltpu.roll(jnp.where(first, odd, even), head_dim, 1)
        at = g * group + p * pair
        store(slice(at, at + pair), result / total)

    units = [None] * groups

    def scaled(g):
        at = g * group
        return (
            unit(raw[g][0], sums[g][0], scale_row[:, at : at + group]),
            unit(raw[g][1], sums[g][1], None),
        )

    units[0] = scaled(0)

    shares = [rest_shares(*units[0])] + [main_share(*units[0], h) for h in range(4)]
    for g in range(groups):
        following = g + 1 < groups
        if following:
            units[g + 1] = scaled(g + 1)
        ahead = []
        rest_out = rest_part(shares[0], value[g])
        if following:
            ahead.append(rest_shares(*units[g + 1]))
        elif between is not None and g > 0:
            between(g - 1)
        parts = []
        for h in range(4):
            parts.append(main_part(shares[1 + h], value[g], h) + rest_out[:, h * pair : (h + 1) * pair])
            if following:
                ahead.append(main_share(*units[g + 1], h))
            if h % 2 == 1:
                combine(g, h // 2, parts[h - 1], parts[h])
        shares = ahead


def scale_lanes(scale_ref, layer, width, heads):
    lane = lax.broadcasted_iota(jnp.int32, (1, width), 1)
    row = jnp.zeros((1, width), f32)
    for h in range(heads):
        row = jnp.where(lane >= h * (width // heads), scale_ref[layer, h] * LOG2E, row)
    return row


def norm_rows(values, gain_row, bias_row):
    average = jnp.mean(values, -1, keepdims=True)
    centred = values - average
    spread = jnp.mean(centred * centred, -1, keepdims=True)
    return centred * (lax.rsqrt(spread + 1e-05)) * gain_row + bias_row


def gelu_twice(x):
    c = 0.7978845608028654
    x = x.astype(bf16)
    one = jnp.ones((), bf16)
    inner = x * (jnp.asarray(c, bf16) + jnp.asarray(c * 0.044715, bf16) * (x * x))
    return x * (one + jnp.tanh(inner))


def finish_window(x, projected, up_ref, down_ref, gain, bias):
    after = x + norm_rows(projected, gain[0:1], bias[0:1])
    after_b = after.astype(bf16)
    ff = up_ref.shape[1]
    step = min(512, ff)
    total = None
    for at in range(0, ff, step):
        hidden = gelu_twice(mm(after_b, up_ref[:, at : at + step]))
        part = mm(hidden, down_ref[at : at + step, :])
        total = part if total is None else total + part
    return after + norm_rows(0.5 * total, gain[1:2], bias[1:2])


def window_keys(ids_ref, j, cols, main, rest, levels, base, lat_total):
    run = HALF_LON * levels
    quarter = HALF_LAT * run
    shape = (1, cols)
    at = lax.broadcasted_iota(jnp.int32, shape, 1)
    t = jnp.where(at < main, at, main + ((at - main) & (rest - 1))).astype(f32)

    def cut(value, by):
        return jnp.floor((value + 0.5) * (1.0 / by))

    q = cut(t, quarter)
    half = cut(q, 2)
    block = q - 2 * half
    inside = t - quarter * q
    r = cut(inside, run)
    column = half * HALF_LON + cut(inside - run * r, levels)
    row = base + block * HALF_LAT + r
    key = jnp.zeros(shape, f32)
    ids = ids_ref[j * WIN_LAT, 0:1, :].astype(f32)
    for c in range(WIN_LON):
        key = jnp.where(column == c, ids[:, c : c + 1], key)
    band = jnp.where(row >= lat_total - WIN_LAT, 1.0, 0.0) + jnp.where(row >= lat_total - HALF_LAT, 1.0, 0.0)
    return key * 3 + band


PAIR_LAST = False


def order(samples, wins):
    plan = []
    for k in range(samples + 2):
        for s, kind in ((k, "f"), (k - 1, "S"), (k - 2, "l")):
            if 0 <= s < samples:
                if kind == "l" and (s < samples - 1 or PAIR_LAST):
                    plan.append(("L", s))
                else:
                    plan += [(kind, s * wins + j) for j in range(wins)]
    plan[0] = ("a", 0)
    return plan


def kernel(lat_size, x_hbm, ids_ref, qkv_hbm, out_hbm, up_hbm, down_hbm, gain_ref, bias_ref, scale_ref,
           x_s, first_s, op_s, att_s, send_s, send_own, back_s, back_own, mask_s, keep_s, win_b,
           scale_s, qkv_s, out_s, up_s, down_s, w_sem, x_sem, send1, recv1, send2, recv2, ids_s, ids_sem):
    samples, lat_rows, lon_cols, levels, width = x_s.shape
    wins = lat_rows // WIN_LAT
    blocks = 2 * wins
    run = HALF_LON * levels
    quarter = HALF_LAT * run
    last_block = blocks - 1

    loads = [
        [
            pltpu.make_async_copy(src.at[layer], dst.at[layer], w_sem.at[layer, k])
            for k, (src, dst) in enumerate(
                ((qkv_hbm, qkv_s), (out_hbm, out_s), (up_hbm, up_s), (down_hbm, down_s))
            )
        ]
        for layer in range(2)
    ]

    def x_load(s, j):
        rows = pl.ds(j * WIN_LAT, WIN_LAT)
        return pltpu.make_async_copy(x_hbm.at[s, rows], x_s.at[s, rows], x_sem.at[s, j])

    x_load(0, 0).start()
    for copy in loads[0]:
        copy.start()
    for s in range(samples):
        for j in range(wins):
            if s + j > 0:
                x_load(s, j).start()
    for copy in loads[1]:
        copy.start()

    lon, lat = lax.axis_index("lon"), lax.axis_index("lat")
    lon_size = lax.axis_size("lon")
    west = lax.rem(lon + lon_size - 1, lon_size)
    east = lax.rem(lon + 1, lon_size)
    before = lax.rem(lat + lat_size - 1, lat_size)
    after = lax.rem(lat + 1, lat_size)

    barrier = pltpu.get_barrier_semaphore()
    peers = ((east, lat), (east, before), (lon, before), (lon, after), (west, lat), (west, after))
    for to_lon, to_lat in peers:
        pl.semaphore_signal(barrier, inc=1, device_id={"lon": to_lon, "lat": to_lat}, device_id_type=MESH)

    heads = scale_ref.shape[1]
    head_dim = width // heads
    rest = head_dim // 2
    tokens = 4 * quarter
    for layer in range(2):
        scale_s[layer : layer + 1, :] = scale_lanes(scale_ref, layer, width, heads)

    def remote(src, dst, send, recv, to_lon, to_lat):
        return pltpu.make_async_remote_copy(
            src_ref=src, dst_ref=dst, send_sem=send, recv_sem=recv,
            device_id={"lon": to_lon, "lat": to_lat}, device_id_type=MESH,
        )

    def ahead(s, k):
        if k == 0:
            return remote(send_s.at[s, pl.ds(1, 1)], op_s.at[s, 0, pl.ds(0, 1)], send1.at[s, k], recv1.at[s, k], east, lat)
        if k == 1:
            return remote(send_s.at[s, pl.ds(0, 1)], op_s.at[s, 0, pl.ds(last_block, 1)], send1.at[s, k], recv1.at[s, k], east, before)
        if k == 2:
            return remote(send_own.at[s], op_s.at[s, 1, pl.ds(last_block, 1)], send1.at[s, k], recv1.at[s, k], lon, before)
        j = k - 2
        return remote(send_s.at[s, pl.ds(2 * j, 2)], op_s.at[s, 0, pl.ds(2 * j - 1, 2)], send1.at[s, k], recv1.at[s, k], east, lat)

    def back(s, k):
        if k == 0:
            return remote(back_s.at[s, pl.ds(last_block - 1, 1)], att_s.at[s, 1, pl.ds(last_block, 1)], send2.at[s, k], recv2.at[s, k], west, lat)
        if k == 1:
            return remote(back_s.at[s, pl.ds(last_block, 1)], att_s.at[s, 1, pl.ds(0, 1)], send2.at[s, k], recv2.at[s, k], west, after)
        if k == 2:
            return remote(back_own.at[s], att_s.at[s, 0, pl.ds(0, 1)], send2.at[s, k], recv2.at[s, k], lon, after)
        j = k - 3
        return remote(back_s.at[s, pl.ds(2 * j, 2)], att_s.at[s, 1, pl.ds(2 * j + 1, 2)], send2.at[s, k], recv2.at[s, k], west, lat)

    def ids_copy():
        return remote(ids_ref, ids_s, ids_sem.at[0], ids_sem.at[1], east, lat)

    def make_masks():
        lat_total = lat_size * lat_rows
        cols = tokens + 3 * rest
        for j in range(wins):
            base = (lat * lat_rows + j * WIN_LAT).astype(f32)
            key = window_keys(ids_s, j, cols, tokens - rest, rest, levels, base, lat_total)
            kinds = lax.broadcasted_iota(jnp.int32, (16, cols), 0).astype(f32)
            member = (kinds == key).astype(f32).astype(bf16)
            same = lax.dot_general(member[:, :tokens], member, (((0,), (0,)), ((), ())), preferred_element_type=f32)
            mask_s[j] = (same - 1.0) * 1e30

    copies = 3 + wins - 1

    def layer_first(items, first):
        for i, s, j in items:
            x_load(s, j).wait()
        if first:
            loads[0][0].wait()

        for i, s, j in items:
            for half in range(2):
                for block in range(2):
                    for r in range(HALF_LAT):
                        row = (half * 2 + block) * quarter + r * run
                        part = x_s[s, j * WIN_LAT + block * HALF_LAT + r, half * HALF_LON : (half + 1) * HALF_LON]
                        first_s[i, row : row + run, :] = part.reshape(run, width)

        def residual():
            return jnp.concatenate([first_s[i] for i, _, _ in items], axis=0)

        rows = len(items) * tokens
        products = []

        def project(g):
            cut = slice(g * 4 * head_dim, (g + 1) * 4 * head_dim)
            products.append(mm(win_b[:rows, cut], out_s[0, cut, :]))

        windows = project_windows(residual().astype(bf16), qkv_s.at[0], tokens, head_dim)
        for n, window in enumerate(windows):

            def store(cut, value):
                win_b[n * tokens : (n + 1) * tokens, cut] = value.astype(bf16)

            attend_window(
                window,
                scale_s[0:1, :],
                None,
                head_dim,
                store,
                project if n == len(windows) - 1 and not first else None,
            )
        if first:
            for copy in loads[0][1:]:
                copy.wait()
        while len(products) * 4 * head_dim < width:
            project(len(products))
        total = products[0]
        for part in products[1:]:
            total = total + part
        result = finish_window(residual(), total, up_s.at[0], down_s.at[0], gain_ref[0], bias_ref[0])

        for n, (i, s, j) in enumerate(items):
            mine = result[n * tokens : (n + 1) * tokens]
            first_s[i] = mine

            def block_of(q):
                return mine[q * quarter : (q + 1) * quarter, :].astype(bf16)

            send_s[s, 2 * j] = block_of(2)
            send_s[s, 2 * j + 1] = block_of(3)
            op_s[s, 1, 2 * j] = block_of(1)
            if isinstance(j, int):
                if j == 0:
                    send_own[s, 0] = block_of(0)
                else:
                    op_s[s, 1, 2 * j - 1] = block_of(0)
            else:
                keep_s[...] = block_of(0)

        if first:
            pl.semaphore_wait(barrier, len(peers))
            ids_copy().start()

        for i, s, j in items:

            @when(j == 0)
            def _():
                if not isinstance(j, int):
                    send_own[s, 0] = keep_s[...]
                for k in range(3):
                    ahead(s, k).start()

            for jj in range(1, wins):

                @when(j == jj)
                def _():
                    if not isinstance(j, int):
                        op_s[s, 1, 2 * jj - 1] = keep_s[...]
                    ahead(s, 2 + jj).start()

    def opening(i):
        layer_first([(0, 0, 0)], True)

    def first_window(i):
        layer_first([(i, lax.div(i, wins), lax.rem(i, wins))], False)

    def first_sample(s):
        layer_first([(s * wins + j, s, j) for j in range(wins)], False)

    def shifted_attention(i):
        s, j = lax.div(i, wins), lax.rem(i, wins)

        @pl.when(j == 0)
        def _():
            ahead(s, 0).wait_recv()

        for jj in range(1, wins):

            @pl.when(j == jj - 1)
            def _():
                ahead(s, 2 + jj).wait_recv()

        @pl.when(j == wins - 1)
        def _():
            for k in (1, 2):
                ahead(s, k).wait_recv()

        @pl.when(i == 0)
        def _():
            loads[1][0].wait()
            ids_copy().wait_recv()
            make_masks()

        operand = jnp.concatenate(
            [op_s[s, half, 2 * j + block].astype(f32) for half in range(2) for block in range(2)], axis=0
        ).astype(bf16)

        def store(cut, value):
            parts = [value[q * quarter : (q + 1) * quarter, :].astype(bf16) for q in range(4)]
            back_s[s, 2 * j, :, cut] = parts[0]
            back_s[s, 2 * j + 1, :, cut] = parts[1]
            att_s[s, 0, 2 * j + 1, :, cut] = parts[2]
            keep_s[:, cut] = parts[3]

        window = project_windows(operand, qkv_s.at[1], tokens, head_dim)[0]
        attend_window(window, scale_s[1:2, :], mask_s.at[j], head_dim, store)

        @pl.when(j == wins - 1)
        def _():
            back_own[s, 0] = keep_s[...]
            for k in (1, 0, 2):
                back(s, k).start()

        for jj in range(wins - 1):

            @pl.when(j == jj)
            def _():
                att_s[s, 0, 2 * jj + 2] = keep_s[...]
                back(s, 3 + jj).start()

    def layer_last(items):
        for i, s, j in items:

            @when(j == 0)
            def _():
                for k in (1, 2):
                    back(s, k).wait_recv()

            for jj in range(wins - 1):

                @when(j == jj)
                def _():
                    back(s, 3 + jj).wait_recv()

            @when(j == wins - 1)
            def _():
                back(s, 0).wait_recv()

        @pl.when(items[0][0] == 0)
        def _():
            for copy in loads[1][1:]:
                copy.wait()

        attended = jnp.concatenate(
            [att_s[s, half, 2 * j + block].astype(f32) for _, s, j in items for half in range(2) for block in range(2)],
            axis=0,
        ).astype(bf16)
        result = finish_window(
            jnp.concatenate([first_s[i] for i, _, _ in items], axis=0),
            mm(attended, out_s[1]), up_s.at[1], down_s.at[1], gain_ref[1], bias_ref[1],
        )
        for n, (_, s, j) in enumerate(items):
            for half in range(2):
                for block in range(2):
                    for r in range(HALF_LAT):
                        row = n * tokens + (half * 2 + block) * quarter + r * run
                        x_s[s, j * WIN_LAT + block * HALF_LAT + r, half * HALF_LON : (half + 1) * HALF_LON] = result[
                            row : row + run, :
                        ].reshape(HALF_LON, levels, width)

    def last_window(i):
        layer_last([(i, lax.div(i, wins), lax.rem(i, wins))])

    def last_sample(s):
        layer_last([(s * wins + j, s, j) for j in range(wins)])

    plan = order(samples, wins)
    steps = {"a": opening, "f": first_window, "F": first_sample, "S": shifted_attention, "l": last_window, "L": last_sample}
    kinds = [kind for kind in steps if any(kind == k for k, _ in plan)]

    def pick(t, values):
        value = jnp.int32(values[0])
        for n in range(1, len(values)):
            if values[n] != values[n - 1]:
                value = jnp.where(t >= n, jnp.int32(values[n]), value)
        return value

    def advance(t, carry):
        kind = pick(t, [kinds.index(k) for k, _ in plan])
        n = pick(t, [n for _, n in plan])
        for k, name in enumerate(kinds):

            @pl.when(kind == k)
            def _():
                steps[name](n)

        return carry

    lax.fori_loop(0, len(plan), advance, 0)

    def drain(s, carry):
        for k in range(copies):
            ahead(s, k).wait_send()
            back(s, k).wait_send()
        return carry

    lax.fori_loop(0, samples, drain, 0)
    ids_copy().wait_send()


def local(stream, region_ids, qkv_weight, out_weight, up_weight, down_weight, norm_gain, norm_bias, logit_scale):
    samples, levels, lat_rows, lon_cols, width = stream.shape
    assert lon_cols == WIN_LON
    wins = lat_rows // WIN_LAT
    blocks = 2 * wins
    quarter = levels * HALF_LAT * HALF_LON
    tokens = 4 * quarter
    copies = 3 + wins - 1
    x = stream.transpose(0, 2, 3, 1, 4)
    ids = region_ids.transpose(1, 0, 2)
    hbm = pl.BlockSpec(memory_space=pl.ANY)
    vmem = pl.BlockSpec(memory_space=pltpu.VMEM)
    smem = pl.BlockSpec(memory_space=pltpu.SMEM)
    sem = pltpu.SemaphoreType.DMA
    y = pl.pallas_call(
        functools.partial(kernel, lax.axis_size("lat")),
        in_specs=[hbm, vmem, hbm, hbm, hbm, hbm, vmem, vmem, smem],
        out_specs=vmem,
        out_shape=pltpu.VMEM(x.shape, f32),
        scratch_shapes=[
            pltpu.VMEM((samples * wins, tokens, width), f32),
            pltpu.VMEM((samples, 2, blocks, quarter, width), bf16),
            pltpu.VMEM((samples, 2, blocks, quarter, width), bf16),
            pltpu.VMEM((samples, blocks, quarter, width), bf16),
            pltpu.VMEM((samples, 1, quarter, width), bf16),
            pltpu.VMEM((samples, blocks, quarter, width), bf16),
            pltpu.VMEM((samples, 1, quarter, width), bf16),
            pltpu.VMEM((wins, tokens, tokens + 3 * (width // logit_scale.shape[1] // 2)), f32),
            pltpu.VMEM((quarter, width), bf16),
            pltpu.VMEM((wins * tokens, width), bf16),
            pltpu.VMEM((2, width), f32),
            pltpu.VMEM(qkv_weight.shape, bf16),
            pltpu.VMEM(out_weight.shape, bf16),
            pltpu.VMEM(up_weight.shape, bf16),
            pltpu.VMEM(down_weight.shape, bf16),
            sem((2, 4)),
            sem((samples, wins)),
            sem((samples, copies)),
            sem((samples, copies)),
            sem((samples, copies)),
            sem((samples, copies)),
            pltpu.VMEM(ids.shape, jnp.int32),
            sem((2,)),
        ],
        compiler_params=pltpu.CompilerParams(
            vmem_limit_bytes=VMEM_LIMIT, collective_id=0, has_side_effects=True
        ),
        name="both_layers",
    )(x, ids, qkv_weight, out_weight, up_weight, down_weight, norm_gain, norm_bias, logit_scale)
    return y.transpose(0, 3, 1, 2, 4)


def solution(mesh):
    in_specs = (P("ens", None, "lat", "lon", None), P("ens", "lat", "lon")) + (P(),) * 7
    out_specs = P("ens", None, "lat", "lon", None)
    return jax.shard_map(local, mesh=mesh, in_specs=in_specs, out_specs=out_specs, check_vma=False)
```

```python
import functools

import jax
import jax.numpy as jnp
from jax import lax
from jax.experimental import pallas as pl
from jax.experimental.pallas import tpu as pltpu
from jax.sharding import PartitionSpec as P

WIN_LAT = 6
WIN_LON = 12
HALF_LAT = WIN_LAT // 2
HALF_LON = WIN_LON // 2
LOG2E = 1.4426950408889634
VMEM_LIMIT = 51 * 1024 * 1024 + 512 * 1024
CLOSING_LIMIT = 40 * 1024 * 1024

f32 = jnp.float32
bf16 = jnp.bfloat16


MESH = pl.DeviceIdType.MESH


def mm(a, b):
    return jnp.dot(a, b, preferred_element_type=f32)


def head_blocks(group, head_dim):
    d0 = lax.broadcasted_iota(jnp.int32, (group, group), 0)
    d1 = lax.broadcasted_iota(jnp.int32, (group, group), 1)
    shift = head_dim.bit_length() - 1
    same_head = lax.shift_right_logical(d0, shift) == lax.shift_right_logical(d1, shift)
    return same_head.astype(f32).astype(bf16)


def when(condition):
    if isinstance(condition, bool):
        return (lambda run: run()) if condition else (lambda run: None)
    return pl.when(condition)


def project_windows(operand, qkv_weight, tokens, head_dim):
    rows, width = operand.shape
    group = 4 * head_dim
    groups = width // group
    same_head = head_blocks(group, head_dim)

    def project(block, g):
        at = block * width + g * group
        return mm(operand, qkv_weight[:, at : at + group])

    def square_sum(part):
        rounded = part.astype(bf16)
        return mm(rounded * rounded, same_head)

    raw = [(project(0, g), project(1, g)) for g in range(groups)]
    sums = [[square_sum(part) for part in raw[g]] for g in range(groups)]
    value = [project(2, g).astype(bf16) for g in range(groups)]
    windows = []
    for at in range(0, rows, tokens):
        cut = slice(at, at + tokens)
        windows.append(
            (
                [[part[cut] for part in raw[g]] for g in range(groups)],
                [[part[cut] for part in sums[g]] for g in range(groups)],
                [part[cut] for part in value],
            )
        )
    return windows


def attend_window(projected, scale_row, bias_ref, head_dim, store, between=None):
    raw, sums, value = projected
    tokens = value[0].shape[0]
    width = sum(part.shape[1] for part in value)
    group = 4 * head_dim
    pair = 2 * head_dim
    rest = pair // 4
    main = tokens - rest
    last = (((1,), (1,)), ((), ()))
    groups = width // group

    def lanes(rows, cols, at, size):
        lane = lax.broadcasted_iota(jnp.int32, (rows, cols), 1)
        return ((lane >= at) & (lane < at + size)).astype(f32).astype(bf16)

    first_b = lanes(tokens, pair, 0, head_dim)
    second_b = lanes(tokens, pair, head_dim, head_dim)
    first = lax.broadcasted_iota(jnp.int32, (tokens, pair), 1) < head_dim

    def unit(part, total, scale):
        inv = lax.rsqrt(total + 1e-06)
        if scale is not None:
            inv = inv * scale
        return (part * inv).astype(bf16)

    def rest_shares(q, k):
        k_rest = jnp.concatenate(
            [k[main:] * lanes(rest, group, h * head_dim, head_dim) for h in range(4)], axis=0
        )
        score = lax.dot_general(q, k_rest, last, preferred_element_type=f32)
        if bias_ref is not None:
            score = score + bias_ref[:, main:]
        return jnp.exp2(score).astype(bf16)

    def rest_part(weights, v):
        columns = []
        for h in range(4):
            side = h % 2
            own, other = (first_b, second_b)[side][:rest], (second_b, first_b)[side][:rest]
            v_rest = v[main:, (h // 2) * pair : (h // 2 + 1) * pair] * own + other
            zero = jnp.zeros_like(v_rest)
            columns.append(jnp.concatenate([v_rest if i == h else zero for i in range(4)], axis=0))
        return mm(weights, jnp.concatenate(columns, axis=1))

    def main_share(q, k, h):
        cut = slice((h // 2) * pair, (h // 2 + 1) * pair)
        own = (first_b, second_b)[h % 2][:main]
        score = lax.dot_general(q[:, cut], k[:main, cut] * own, last, preferred_element_type=f32)
        if bias_ref is not None:
            score = score + bias_ref[:, :main]
        return jnp.exp2(score).astype(bf16)

    def main_part(share, v, h):
        cut = slice((h // 2) * pair, (h // 2 + 1) * pair)
        own, other = ((first_b, second_b), (second_b, first_b))[h % 2]
        return mm(share, v[:main, cut] * own[:main] + other[:main])

    def combine(g, p, even, odd):
        result = jnp.where(first, even, odd)
        total = pltpu.roll(jnp.where(first, odd, even), head_dim, 1)
        at = g * group + p * pair
        store(slice(at, at + pair), result / total)

    units = [None] * groups

    def scaled(g):
        at = g * group
        return (
            unit(raw[g][0], sums[g][0], scale_row[:, at : at + group]),
            unit(raw[g][1], sums[g][1], None),
        )

    units[0] = scaled(0)

    shares = [rest_shares(*units[0])] + [main_share(*units[0], h) for h in range(4)]
    for g in range(groups):
        following = g + 1 < groups
        if following:
            units[g + 1] = scaled(g + 1)
        ahead = []
        rest_out = rest_part(shares[0], value[g])
        if following:
            ahead.append(rest_shares(*units[g + 1]))
        elif between is not None and g > 0:
            between(g - 1)
        parts = []
        for h in range(4):
            parts.append(main_part(shares[1 + h], value[g], h) + rest_out[:, h * pair : (h + 1) * pair])
            if following:
                ahead.append(main_share(*units[g + 1], h))
            if h % 2 == 1:
                combine(g, h // 2, parts[h - 1], parts[h])
        shares = ahead


def scale_lanes(scale_ref, layer, width, heads):
    lane = lax.broadcasted_iota(jnp.int32, (1, width), 1)
    row = jnp.zeros((1, width), f32)
    for h in range(heads):
        row = jnp.where(lane >= h * (width // heads), scale_ref[layer, h] * LOG2E, row)
    return row


def norm_rows(values, gain_row, bias_row):
    average = jnp.mean(values, -1, keepdims=True)
    centred = values - average
    spread = jnp.mean(centred * centred, -1, keepdims=True)
    return centred * (lax.rsqrt(spread + 1e-05)) * gain_row + bias_row


def gelu_twice(x):
    c = 0.7978845608028654
    x = x.astype(bf16)
    one = jnp.ones((), bf16)
    inner = x * (jnp.asarray(c, bf16) + jnp.asarray(c * 0.044715, bf16) * (x * x))
    return x * (one + jnp.tanh(inner))


def finish_window(x, projected, up_ref, down_ref, gain, bias):
    after = x + norm_rows(projected, gain[0:1], bias[0:1])
    after_b = after.astype(bf16)
    ff = up_ref.shape[1]
    step = min(512, ff)
    total = None
    for at in range(0, ff, step):
        hidden = gelu_twice(mm(after_b, up_ref[:, at : at + step]))
        part = mm(hidden, down_ref[at : at + step, :])
        total = part if total is None else total + part
    return after + norm_rows(0.5 * total, gain[1:2], bias[1:2])


def window_keys(ids_ref, j, cols, main, rest, levels, base, lat_total):
    run = HALF_LON * levels
    quarter = HALF_LAT * run
    shape = (1, cols)
    at = lax.broadcasted_iota(jnp.int32, shape, 1)
    t = jnp.where(at < main, at, main + ((at - main) & (rest - 1))).astype(f32)

    def cut(value, by):
        return jnp.floor((value + 0.5) * (1.0 / by))

    q = cut(t, quarter)
    half = cut(q, 2)
    block = q - 2 * half
    inside = t - quarter * q
    r = cut(inside, run)
    column = half * HALF_LON + cut(inside - run * r, levels)
    row = base + block * HALF_LAT + r
    key = jnp.zeros(shape, f32)
    ids = ids_ref[j * WIN_LAT, 0:1, :].astype(f32)
    for c in range(WIN_LON):
        key = jnp.where(column == c, ids[:, c : c + 1], key)
    band = jnp.where(row >= lat_total - WIN_LAT, 1.0, 0.0) + jnp.where(row >= lat_total - HALF_LAT, 1.0, 0.0)
    return key * 3 + band


def order(samples, wins):
    plan = []
    for k in range(samples + 2):
        for s, kind in ((k, "f"), (k - 1, "S"), (k - 2, "l")):
            if 0 <= s < samples:
                if kind == "l" and s < samples - 1:
                    plan.append(("L", s))
                else:
                    plan += [(kind, s * wins + j) for j in range(wins)]
    plan[0] = ("a", 0)
    return plan[:-1]


def kernel(lat_size, x_hbm, ids_ref, qkv_hbm, out_hbm, up_hbm, down_hbm, gain_ref, bias_ref, scale_ref,
           x_s, first_o, att_o, out1_s, up1_s, down1_s, first_s, op_s, att_s, send_s, send_own, back_s, back_own, mask_s, keep_s, win_b,
           scale_s, qkv_s, out_s, up_s, down_s, w_sem, x_sem, send1, recv1, send2, recv2, ids_s, ids_sem):
    samples, lat_rows, lon_cols, levels, width = x_s.shape
    wins = lat_rows // WIN_LAT
    blocks = 2 * wins
    run = HALF_LON * levels
    quarter = HALF_LAT * run
    last_block = blocks - 1

    loads = [
        [
            pltpu.make_async_copy(src.at[layer], dst, w_sem.at[layer, k])
            for k, (src, dst) in enumerate(zip((qkv_hbm, out_hbm, up_hbm, down_hbm), targets))
        ]
        for layer, targets in enumerate(
            ((qkv_s.at[0], out_s, up_s, down_s), (qkv_s.at[1], out1_s, up1_s, down1_s))
        )
    ]

    def x_load(s, j):
        rows = pl.ds(j * WIN_LAT, WIN_LAT)
        return pltpu.make_async_copy(x_hbm.at[s, rows], x_s.at[s, rows], x_sem.at[s, j])

    x_load(0, 0).start()
    for copy in loads[0]:
        copy.start()
    for s in range(samples):
        for j in range(wins):
            if s + j > 0:
                x_load(s, j).start()
    for copy in loads[1]:
        copy.start()

    lon, lat = lax.axis_index("lon"), lax.axis_index("lat")
    lon_size = lax.axis_size("lon")
    west = lax.rem(lon + lon_size - 1, lon_size)
    east = lax.rem(lon + 1, lon_size)
    before = lax.rem(lat + lat_size - 1, lat_size)
    after = lax.rem(lat + 1, lat_size)

    barrier = pltpu.get_barrier_semaphore()
    peers = ((east, lat), (east, before), (lon, before), (lon, after), (west, lat), (west, after))
    for to_lon, to_lat in peers:
        pl.semaphore_signal(barrier, inc=1, device_id={"lon": to_lon, "lat": to_lat}, device_id_type=MESH)

    heads = scale_ref.shape[1]
    head_dim = width // heads
    rest = head_dim // 2
    tokens = 4 * quarter
    for layer in range(2):
        scale_s[layer : layer + 1, :] = scale_lanes(scale_ref, layer, width, heads)

    def remote(src, dst, send, recv, to_lon, to_lat):
        return pltpu.make_async_remote_copy(
            src_ref=src, dst_ref=dst, send_sem=send, recv_sem=recv,
            device_id={"lon": to_lon, "lat": to_lat}, device_id_type=MESH,
        )

    def ahead(s, k):
        if k == 0:
            return remote(send_s.at[s, pl.ds(1, 1)], op_s.at[s, 0, pl.ds(0, 1)], send1.at[s, k], recv1.at[s, k], east, lat)
        if k == 1:
            return remote(send_s.at[s, pl.ds(0, 1)], op_s.at[s, 0, pl.ds(last_block, 1)], send1.at[s, k], recv1.at[s, k], east, before)
        if k == 2:
            return remote(send_own.at[s], op_s.at[s, 1, pl.ds(last_block, 1)], send1.at[s, k], recv1.at[s, k], lon, before)
        j = k - 2
        return remote(send_s.at[s, pl.ds(2 * j, 2)], op_s.at[s, 0, pl.ds(2 * j - 1, 2)], send1.at[s, k], recv1.at[s, k], east, lat)

    def back(s, k):
        if k == 0:
            return remote(back_s.at[s, pl.ds(last_block - 1, 1)], att_s.at[s, 1, pl.ds(last_block, 1)], send2.at[s, k], recv2.at[s, k], west, lat)
        if k == 1:
            return remote(back_s.at[s, pl.ds(last_block, 1)], att_s.at[s, 1, pl.ds(0, 1)], send2.at[s, k], recv2.at[s, k], west, after)
        if k == 2:
            return remote(back_own.at[s], att_s.at[s, 0, pl.ds(0, 1)], send2.at[s, k], recv2.at[s, k], lon, after)
        j = k - 3
        return remote(back_s.at[s, pl.ds(2 * j, 2)], att_s.at[s, 1, pl.ds(2 * j + 1, 2)], send2.at[s, k], recv2.at[s, k], west, lat)

    def ids_copy():
        return remote(ids_ref, ids_s, ids_sem.at[0], ids_sem.at[1], east, lat)

    def make_masks():
        lat_total = lat_size * lat_rows
        cols = tokens + 3 * rest
        for j in range(wins):
            base = (lat * lat_rows + j * WIN_LAT).astype(f32)
            key = window_keys(ids_s, j, cols, tokens - rest, rest, levels, base, lat_total)
            kinds = lax.broadcasted_iota(jnp.int32, (16, cols), 0).astype(f32)
            member = (kinds == key).astype(f32).astype(bf16)
            same = lax.dot_general(member[:, :tokens], member, (((0,), (0,)), ((), ())), preferred_element_type=f32)
            mask_s[j] = (same - 1.0) * 1e30

    copies = 3 + wins - 1

    def layer_first(items, first):
        for i, s, j in items:
            x_load(s, j).wait()
        if first:
            loads[0][0].wait()

        for i, s, j in items:
            for half in range(2):
                for block in range(2):
                    for r in range(HALF_LAT):
                        row = (half * 2 + block) * quarter + r * run
                        part = x_s[s, j * WIN_LAT + block * HALF_LAT + r, half * HALF_LON : (half + 1) * HALF_LON]
                        first_s[i, row : row + run, :] = part.reshape(run, width)

        def residual():
            return jnp.concatenate([first_s[i] for i, _, _ in items], axis=0)

        rows = len(items) * tokens
        products = []

        def project(g):
            cut = slice(g * 4 * head_dim, (g + 1) * 4 * head_dim)
            products.append(mm(win_b[:rows, cut], out_s[cut, :]))

        windows = project_windows(residual().astype(bf16), qkv_s.at[0], tokens, head_dim)
        for n, window in enumerate(windows):

            def store(cut, value):
                win_b[n * tokens : (n + 1) * tokens, cut] = value.astype(bf16)

            attend_window(
                window,
                scale_s[0:1, :],
                None,
                head_dim,
                store,
                project if n == len(windows) - 1 and not first else None,
            )
        if first:
            for copy in loads[0][1:]:
                copy.wait()
        while len(products) * 4 * head_dim < width:
            project(len(products))
        total = products[0]
        for part in products[1:]:
            total = total + part
        result = finish_window(residual(), total, up_s, down_s, gain_ref[0], bias_ref[0])

        for n, (i, s, j) in enumerate(items):
            mine = result[n * tokens : (n + 1) * tokens]
            first_s[i] = mine

            def block_of(q):
                return mine[q * quarter : (q + 1) * quarter, :].astype(bf16)

            send_s[s, 2 * j] = block_of(2)
            send_s[s, 2 * j + 1] = block_of(3)
            op_s[s, 1, 2 * j] = block_of(1)
            if isinstance(j, int):
                if j == 0:
                    send_own[s, 0] = block_of(0)
                else:
                    op_s[s, 1, 2 * j - 1] = block_of(0)
            else:
                keep_s[...] = block_of(0)

        if first:
            pl.semaphore_wait(barrier, len(peers))
            ids_copy().start()

        for i, s, j in items:

            @when(j == 0)
            def _():
                if not isinstance(j, int):
                    send_own[s, 0] = keep_s[...]
                for k in range(3):
                    ahead(s, k).start()

            for jj in range(1, wins):

                @when(j == jj)
                def _():
                    if not isinstance(j, int):
                        op_s[s, 1, 2 * jj - 1] = keep_s[...]
                    ahead(s, 2 + jj).start()

    def opening(i):
        layer_first([(0, 0, 0)], True)

    def first_window(i):
        layer_first([(i, lax.div(i, wins), lax.rem(i, wins))], False)

    def first_sample(s):
        layer_first([(s * wins + j, s, j) for j in range(wins)], False)

    def shifted_attention(i):
        s, j = lax.div(i, wins), lax.rem(i, wins)

        @pl.when(j == 0)
        def _():
            ahead(s, 0).wait_recv()

        for jj in range(1, wins):

            @pl.when(j == jj - 1)
            def _():
                ahead(s, 2 + jj).wait_recv()

        @pl.when(j == wins - 1)
        def _():
            for k in (1, 2):
                ahead(s, k).wait_recv()

        @pl.when(i == 0)
        def _():
            loads[1][0].wait()
            ids_copy().wait_recv()
            make_masks()

        operand = jnp.concatenate(
            [op_s[s, half, 2 * j + block].astype(f32) for half in range(2) for block in range(2)], axis=0
        ).astype(bf16)

        def store(cut, value):
            parts = [value[q * quarter : (q + 1) * quarter, :].astype(bf16) for q in range(4)]
            back_s[s, 2 * j, :, cut] = parts[0]
            back_s[s, 2 * j + 1, :, cut] = parts[1]
            att_s[s, 0, 2 * j + 1, :, cut] = parts[2]
            keep_s[:, cut] = parts[3]

        window = project_windows(operand, qkv_s.at[1], tokens, head_dim)[0]
        attend_window(window, scale_s[1:2, :], mask_s.at[j], head_dim, store)

        @pl.when(j == wins - 1)
        def _():
            back_own[s, 0] = keep_s[...]
            for k in (1, 0, 2):
                back(s, k).start()

        for jj in range(wins - 1):

            @pl.when(j == jj)
            def _():
                att_s[s, 0, 2 * jj + 2] = keep_s[...]
                back(s, 3 + jj).start()

    def layer_last(items):
        for i, s, j in items:

            @when(j == 0)
            def _():
                for k in (1, 2):
                    back(s, k).wait_recv()

            for jj in range(wins - 1):

                @when(j == jj)
                def _():
                    back(s, 3 + jj).wait_recv()

            @when(j == wins - 1)
            def _():
                back(s, 0).wait_recv()

        @pl.when(items[0][0] == 0)
        def _():
            for copy in loads[1][1:]:
                copy.wait()

        attended = jnp.concatenate(
            [att_s[s, half, 2 * j + block].astype(f32) for _, s, j in items for half in range(2) for block in range(2)],
            axis=0,
        ).astype(bf16)
        result = finish_window(
            jnp.concatenate([first_s[i] for i, _, _ in items], axis=0),
            mm(attended, out1_s[...]), up1_s, down1_s, gain_ref[1], bias_ref[1],
        )
        for n, (_, s, j) in enumerate(items):
            for half in range(2):
                for block in range(2):
                    for r in range(HALF_LAT):
                        row = n * tokens + (half * 2 + block) * quarter + r * run
                        x_s[s, j * WIN_LAT + block * HALF_LAT + r, half * HALF_LON : (half + 1) * HALF_LON] = result[
                            row : row + run, :
                        ].reshape(HALF_LON, levels, width)

    def last_window(i):
        layer_last([(i, lax.div(i, wins), lax.rem(i, wins))])

    def last_sample(s):
        layer_last([(s * wins + j, s, j) for j in range(wins)])

    plan = order(samples, wins)
    steps = {"a": opening, "f": first_window, "F": first_sample, "S": shifted_attention, "l": last_window, "L": last_sample}
    kinds = [kind for kind in steps if any(kind == k for k, _ in plan)]

    def pick(t, values):
        value = jnp.int32(values[0])
        for n in range(1, len(values)):
            if values[n] != values[n - 1]:
                value = jnp.where(t >= n, jnp.int32(values[n]), value)
        return value

    def advance(t, carry):
        kind = pick(t, [kinds.index(k) for k, _ in plan])
        n = pick(t, [n for _, n in plan])
        for k, name in enumerate(kinds):

            @pl.when(kind == k)
            def _():
                steps[name](n)

        return carry

    lax.fori_loop(0, len(plan), advance, 0)

    if samples * wins == 1:
        for copy in loads[1][1:]:
            copy.wait()
    if wins == 1:
        for k in (1, 2):
            back(samples - 1, k).wait_recv()
    back(samples - 1, 0).wait_recv()
    first_o[...] = first_s[samples * wins - 1]
    for half in range(2):
        for block in range(2):
            att_o[half, block] = att_s[samples - 1, half, blocks - 2 + block]

    def drain(s, carry):
        for k in range(copies):
            ahead(s, k).wait_send()
            back(s, k).wait_send()
        return carry

    lax.fori_loop(0, samples, drain, 0)
    ids_copy().wait_send()


def closing(x_ref, first_ref, att_ref, out_ref, up_ref, down_ref, gain_ref, bias_ref, y_hbm, last_s, sems):
    samples, lat_rows, lon_cols, levels, width = x_ref.shape
    wins = lat_rows // WIN_LAT
    run = HALF_LON * levels
    quarter = HALF_LAT * run

    def store(src, s, j):
        return pltpu.make_async_copy(src, y_hbm.at[s, pl.ds(j * WIN_LAT, WIN_LAT)], sems.at[s, j])

    copies = [
        store(x_ref.at[s, pl.ds(j * WIN_LAT, WIN_LAT)], s, j)
        for s in range(samples)
        for j in range(wins)
        if s * wins + j < samples * wins - 1
    ]
    for copy in copies:
        copy.start()
    attended = jnp.concatenate(
        [att_ref[half, block].astype(f32) for half in range(2) for block in range(2)], axis=0
    ).astype(bf16)
    result = finish_window(
        first_ref[...], mm(attended, out_ref[...]), up_ref, down_ref, gain_ref[1], bias_ref[1]
    )
    for half in range(2):
        for block in range(2):
            for r in range(HALF_LAT):
                row = (half * 2 + block) * quarter + r * run
                last_s[block * HALF_LAT + r, half * HALF_LON : (half + 1) * HALF_LON] = result[
                    row : row + run, :
                ].reshape(HALF_LON, levels, width)
    copies.append(store(last_s, samples - 1, wins - 1))
    copies[-1].start()
    for copy in copies:
        copy.wait()


def local(stream, region_ids, qkv_weight, out_weight, up_weight, down_weight, norm_gain, norm_bias, logit_scale):
    samples, levels, lat_rows, lon_cols, width = stream.shape
    assert lon_cols == WIN_LON
    wins = lat_rows // WIN_LAT
    blocks = 2 * wins
    quarter = levels * HALF_LAT * HALF_LON
    tokens = 4 * quarter
    copies = 3 + wins - 1
    x = stream.transpose(0, 2, 3, 1, 4)
    ids = region_ids.transpose(1, 0, 2)
    hbm = pl.BlockSpec(memory_space=pl.ANY)
    vmem = pl.BlockSpec(memory_space=pltpu.VMEM)
    smem = pl.BlockSpec(memory_space=pltpu.SMEM)
    sem = pltpu.SemaphoreType.DMA
    handed = [
        pltpu.VMEM(x.shape, f32),
        pltpu.VMEM((tokens, width), f32),
        pltpu.VMEM((2, 2, quarter, width), bf16),
        pltpu.VMEM(out_weight.shape[1:], bf16),
        pltpu.VMEM(up_weight.shape[1:], bf16),
        pltpu.VMEM(down_weight.shape[1:], bf16),
    ]
    parts = pl.pallas_call(
        functools.partial(kernel, lax.axis_size("lat")),
        in_specs=[hbm, vmem, hbm, hbm, hbm, hbm, vmem, vmem, smem],
        out_specs=[vmem] * len(handed),
        out_shape=handed,
        scratch_shapes=[
            pltpu.VMEM((samples * wins, tokens, width), f32),
            pltpu.VMEM((samples, 2, blocks, quarter, width), bf16),
            pltpu.VMEM((samples, 2, blocks, quarter, width), bf16),
            pltpu.VMEM((samples, blocks, quarter, width), bf16),
            pltpu.VMEM((samples, 1, quarter, width), bf16),
            pltpu.VMEM((samples, blocks, quarter, width), bf16),
            pltpu.VMEM((samples, 1, quarter, width), bf16),
            pltpu.VMEM((wins, tokens, tokens + 3 * (width // logit_scale.shape[1] // 2)), f32),
            pltpu.VMEM((quarter, width), bf16),
            pltpu.VMEM((wins * tokens, width), bf16),
            pltpu.VMEM((2, width), f32),
            pltpu.VMEM(qkv_weight.shape, bf16),
            pltpu.VMEM(out_weight.shape[1:], bf16),
            pltpu.VMEM(up_weight.shape[1:], bf16),
            pltpu.VMEM(down_weight.shape[1:], bf16),
            sem((2, 4)),
            sem((samples, wins)),
            sem((samples, copies)),
            sem((samples, copies)),
            sem((samples, copies)),
            sem((samples, copies)),
            pltpu.VMEM(ids.shape, jnp.int32),
            sem((2,)),
        ],
        compiler_params=pltpu.CompilerParams(
            vmem_limit_bytes=VMEM_LIMIT, collective_id=0, has_side_effects=True
        ),
        name="both_layers",
    )(x, ids, qkv_weight, out_weight, up_weight, down_weight, norm_gain, norm_bias, logit_scale)
    y = pl.pallas_call(
        closing,
        in_specs=[vmem] * (len(handed) + 2),
        out_specs=hbm,
        out_shape=jax.ShapeDtypeStruct(x.shape, f32),
        scratch_shapes=[pltpu.VMEM((WIN_LAT,) + x.shape[2:], f32), sem((samples, wins))],
        compiler_params=pltpu.CompilerParams(vmem_limit_bytes=CLOSING_LIMIT),
        name="closing",
    )(*[pltpu.with_memory_space_constraint(part, pltpu.VMEM) for part in parts], norm_gain, norm_bias)
    return y.transpose(0, 3, 1, 2, 4)


def solution(mesh):
    in_specs = (P("ens", None, "lat", "lon", None), P("ens", "lat", "lon")) + (P(),) * 7
    out_specs = P("ens", None, "lat", "lon", None)
    return jax.shard_map(local, mesh=mesh, in_specs=in_specs, out_specs=out_specs, check_vma=False)
```

```python
import functools

import jax
import jax.numpy as jnp
from jax import lax
from jax.experimental import pallas as pl
from jax.experimental.pallas import tpu as pltpu
from jax.sharding import PartitionSpec as P

WIN_LAT = 6
WIN_LON = 12
HALF_LAT = WIN_LAT // 2
HALF_LON = WIN_LON // 2
LOG2E = 1.4426950408889634
VMEM_LIMIT = 51 * 1024 * 1024 + 512 * 1024
CLOSING_LIMIT = 40 * 1024 * 1024

f32 = jnp.float32
bf16 = jnp.bfloat16


MESH = pl.DeviceIdType.MESH


def mm(a, b):
    return jnp.dot(a, b, preferred_element_type=f32)


def head_blocks(group, head_dim):
    d0 = lax.broadcasted_iota(jnp.int32, (group, group), 0)
    d1 = lax.broadcasted_iota(jnp.int32, (group, group), 1)
    shift = head_dim.bit_length() - 1
    same_head = lax.shift_right_logical(d0, shift) == lax.shift_right_logical(d1, shift)
    return same_head.astype(f32).astype(bf16)


def when(condition):
    if isinstance(condition, bool):
        return (lambda run: run()) if condition else (lambda run: None)
    return pl.when(condition)


def project_windows(operand, qkv_weight, tokens, head_dim, joint):
    rows, width = operand.shape
    group = 4 * head_dim
    groups = width // group
    same_head = head_blocks(group, head_dim)

    def project(block, g):
        at = block * width + g * group
        return mm(operand, qkv_weight[:, at : at + group])

    def square(part):
        rounded = part.astype(bf16)
        return rounded * rounded

    raw = [(project(0, g), project(1, g)) for g in range(groups)]
    if joint:
        every = mm(jnp.concatenate([square(part) for g in range(groups) for part in raw[g]], axis=0), same_head)
        sums = [[every[(2 * g + n) * rows : (2 * g + n + 1) * rows] for n in range(2)] for g in range(groups)]
    else:
        sums = [[mm(square(part), same_head) for part in raw[g]] for g in range(groups)]
    value = [project(2, g).astype(bf16) for g in range(groups)]
    windows = []
    for at in range(0, rows, tokens):
        cut = slice(at, at + tokens)
        windows.append(
            (
                [[part[cut] for part in raw[g]] for g in range(groups)],
                [[part[cut] for part in sums[g]] for g in range(groups)],
                [part[cut] for part in value],
            )
        )
    return windows


def attend_window(projected, scale_row, bias_ref, head_dim, store, between=None):
    raw, sums, value = projected
    tokens = value[0].shape[0]
    width = sum(part.shape[1] for part in value)
    group = 4 * head_dim
    pair = 2 * head_dim
    rest = pair // 4
    main = tokens - rest
    last = (((1,), (1,)), ((), ()))
    groups = width // group

    def lanes(rows, cols, at, size):
        lane = lax.broadcasted_iota(jnp.int32, (rows, cols), 1)
        return ((lane >= at) & (lane < at + size)).astype(f32).astype(bf16)

    first_b = lanes(tokens, pair, 0, head_dim)
    second_b = lanes(tokens, pair, head_dim, head_dim)
    first = lax.broadcasted_iota(jnp.int32, (tokens, pair), 1) < head_dim

    def unit(part, total, scale):
        inv = lax.rsqrt(total + 1e-06)
        if scale is not None:
            inv = inv * scale
        return (part * inv).astype(bf16)

    def rest_shares(q, k):
        k_rest = jnp.concatenate(
            [k[main:] * lanes(rest, group, h * head_dim, head_dim) for h in range(4)], axis=0
        )
        score = lax.dot_general(q, k_rest, last, preferred_element_type=f32)
        if bias_ref is not None:
            score = score + bias_ref[:, main:]
        return jnp.exp2(score).astype(bf16)

    def rest_part(weights, v):
        columns = []
        for h in range(4):
            side = h % 2
            own, other = (first_b, second_b)[side][:rest], (second_b, first_b)[side][:rest]
            v_rest = v[main:, (h // 2) * pair : (h // 2 + 1) * pair] * own + other
            zero = jnp.zeros_like(v_rest)
            columns.append(jnp.concatenate([v_rest if i == h else zero for i in range(4)], axis=0))
        return mm(weights, jnp.concatenate(columns, axis=1))

    def main_share(q, k, h):
        cut = slice((h // 2) * pair, (h // 2 + 1) * pair)
        own = (first_b, second_b)[h % 2][:main]
        score = lax.dot_general(q[:, cut], k[:main, cut] * own, last, preferred_element_type=f32)
        if bias_ref is not None:
            score = score + bias_ref[:, :main]
        return jnp.exp2(score).astype(bf16)

    def main_part(share, v, h):
        cut = slice((h // 2) * pair, (h // 2 + 1) * pair)
        own, other = ((first_b, second_b), (second_b, first_b))[h % 2]
        return mm(share, v[:main, cut] * own[:main] + other[:main])

    def combine(g, p, even, odd):
        result = jnp.where(first, even, odd)
        total = pltpu.roll(jnp.where(first, odd, even), head_dim, 1)
        at = g * group + p * pair
        store(slice(at, at + pair), result / total)

    units = [None] * groups

    def scaled(g):
        at = g * group
        return (
            unit(raw[g][0], sums[g][0], scale_row[:, at : at + group]),
            unit(raw[g][1], sums[g][1], None),
        )

    units[0] = scaled(0)

    shares = [rest_shares(*units[0])] + [main_share(*units[0], h) for h in range(4)]
    for g in range(groups):
        following = g + 1 < groups
        if following:
            units[g + 1] = scaled(g + 1)
        ahead = []
        rest_out = rest_part(shares[0], value[g])
        if following:
            ahead.append(rest_shares(*units[g + 1]))
        elif between is not None and g > 0:
            between(g - 1)
        parts = []
        for h in range(4):
            parts.append(main_part(shares[1 + h], value[g], h) + rest_out[:, h * pair : (h + 1) * pair])
            if following:
                ahead.append(main_share(*units[g + 1], h))
            if h % 2 == 1:
                combine(g, h // 2, parts[h - 1], parts[h])
        shares = ahead


def scale_lanes(scale_ref, layer, width, heads):
    lane = lax.broadcasted_iota(jnp.int32, (1, width), 1)
    row = jnp.zeros((1, width), f32)
    for h in range(heads):
        row = jnp.where(lane >= h * (width // heads), scale_ref[layer, h] * LOG2E, row)
    return row


def norm_rows(values, gain_row, bias_row):
    average = jnp.mean(values, -1, keepdims=True)
    centred = values - average
    spread = jnp.mean(centred * centred, -1, keepdims=True)
    return centred * (lax.rsqrt(spread + 1e-05)) * gain_row + bias_row


def gelu_twice(x):
    c = 0.7978845608028654
    x = x.astype(bf16)
    one = jnp.ones((), bf16)
    inner = x * (jnp.asarray(c, bf16) + jnp.asarray(c * 0.044715, bf16) * (x * x))
    return x * (one + jnp.tanh(inner))


def finish_window(x, projected, up_ref, down_ref, gain, bias):
    after = x + norm_rows(projected, gain[0:1], bias[0:1])
    after_b = after.astype(bf16)
    ff = up_ref.shape[1]
    step = min(512, ff)
    total = None
    for at in range(0, ff, step):
        hidden = gelu_twice(mm(after_b, up_ref[:, at : at + step]))
        part = mm(hidden, down_ref[at : at + step, :])
        total = part if total is None else total + part
    return after + norm_rows(0.5 * total, gain[1:2], bias[1:2])


def window_keys(ids_ref, j, cols, main, rest, levels, base, lat_total):
    run = HALF_LON * levels
    quarter = HALF_LAT * run
    shape = (1, cols)
    at = lax.broadcasted_iota(jnp.int32, shape, 1)
    t = jnp.where(at < main, at, main + ((at - main) & (rest - 1))).astype(f32)

    def cut(value, by):
        return jnp.floor((value + 0.5) * (1.0 / by))

    q = cut(t, quarter)
    half = cut(q, 2)
    block = q - 2 * half
    inside = t - quarter * q
    r = cut(inside, run)
    column = half * HALF_LON + cut(inside - run * r, levels)
    row = base + block * HALF_LAT + r
    key = jnp.zeros(shape, f32)
    ids = ids_ref[j * WIN_LAT, 0:1, :].astype(f32)
    for c in range(WIN_LON):
        key = jnp.where(column == c, ids[:, c : c + 1], key)
    band = jnp.where(row >= lat_total - WIN_LAT, 1.0, 0.0) + jnp.where(row >= lat_total - HALF_LAT, 1.0, 0.0)
    return key * 3 + band


def order(samples, wins):
    plan = []
    for k in range(samples + 2):
        for s, kind in ((k, "f"), (k - 1, "S"), (k - 2, "l")):
            if 0 <= s < samples:
                if kind == "l" and s < samples - 1:
                    plan.append(("L", s))
                else:
                    plan += [(kind, s * wins + j) for j in range(wins)]
    plan[0] = ("a", 0)
    return plan[:-1]


def kernel(lat_size, x_hbm, ids_ref, qkv_hbm, out_hbm, up_hbm, down_hbm, gain_ref, bias_ref, scale_ref,
           x_s, first_o, att_o, out1_s, up1_s, down1_s, first_s, op_s, att_s, send_s, send_own, back_s, back_own, mask_s, keep_s, win_b,
           scale_s, qkv_s, out_s, up_s, down_s, w_sem, x_sem, send1, recv1, send2, recv2, ids_s, ids_sem):
    samples, lat_rows, lon_cols, levels, width = x_s.shape
    wins = lat_rows // WIN_LAT
    blocks = 2 * wins
    run = HALF_LON * levels
    quarter = HALF_LAT * run
    last_block = blocks - 1

    loads = [
        [
            pltpu.make_async_copy(src.at[layer], dst, w_sem.at[layer, k])
            for k, (src, dst) in enumerate(zip((qkv_hbm, out_hbm, up_hbm, down_hbm), targets))
        ]
        for layer, targets in enumerate(
            ((qkv_s.at[0], out_s, up_s, down_s), (qkv_s.at[1], out1_s, up1_s, down1_s))
        )
    ]

    def x_load(s, j):
        rows = pl.ds(j * WIN_LAT, WIN_LAT)
        return pltpu.make_async_copy(x_hbm.at[s, rows], x_s.at[s, rows], x_sem.at[s, j])

    x_load(0, 0).start()
    for copy in loads[0]:
        copy.start()
    for s in range(samples):
        for j in range(wins):
            if s + j > 0:
                x_load(s, j).start()
    for copy in loads[1]:
        copy.start()

    lon, lat = lax.axis_index("lon"), lax.axis_index("lat")
    lon_size = lax.axis_size("lon")
    west = lax.rem(lon + lon_size - 1, lon_size)
    east = lax.rem(lon + 1, lon_size)
    before = lax.rem(lat + lat_size - 1, lat_size)
    after = lax.rem(lat + 1, lat_size)

    barrier = pltpu.get_barrier_semaphore()
    peers = ((east, lat), (east, before), (lon, before), (lon, after), (west, lat), (west, after))
    for to_lon, to_lat in peers:
        pl.semaphore_signal(barrier, inc=1, device_id={"lon": to_lon, "lat": to_lat}, device_id_type=MESH)

    heads = scale_ref.shape[1]
    head_dim = width // heads
    rest = head_dim // 2
    tokens = 4 * quarter
    for layer in range(2):
        scale_s[layer : layer + 1, :] = scale_lanes(scale_ref, layer, width, heads)

    def remote(src, dst, send, recv, to_lon, to_lat):
        return pltpu.make_async_remote_copy(
            src_ref=src, dst_ref=dst, send_sem=send, recv_sem=recv,
            device_id={"lon": to_lon, "lat": to_lat}, device_id_type=MESH,
        )

    def ahead(s, k):
        if k == 0:
            return remote(send_s.at[s, pl.ds(1, 1)], op_s.at[s, 0, pl.ds(0, 1)], send1.at[s, k], recv1.at[s, k], east, lat)
        if k == 1:
            return remote(send_s.at[s, pl.ds(0, 1)], op_s.at[s, 0, pl.ds(last_block, 1)], send1.at[s, k], recv1.at[s, k], east, before)
        if k == 2:
            return remote(send_own.at[s], op_s.at[s, 1, pl.ds(last_block, 1)], send1.at[s, k], recv1.at[s, k], lon, before)
        j = k - 2
        return remote(send_s.at[s, pl.ds(2 * j, 2)], op_s.at[s, 0, pl.ds(2 * j - 1, 2)], send1.at[s, k], recv1.at[s, k], east, lat)

    def back(s, k):
        if k == 0:
            return remote(back_s.at[s, pl.ds(last_block - 1, 1)], att_s.at[s, 1, pl.ds(last_block, 1)], send2.at[s, k], recv2.at[s, k], west, lat)
        if k == 1:
            return remote(back_s.at[s, pl.ds(last_block, 1)], att_s.at[s, 1, pl.ds(0, 1)], send2.at[s, k], recv2.at[s, k], west, after)
        if k == 2:
            return remote(back_own.at[s], att_s.at[s, 0, pl.ds(0, 1)], send2.at[s, k], recv2.at[s, k], lon, after)
        j = k - 3
        return remote(back_s.at[s, pl.ds(2 * j, 2)], att_s.at[s, 1, pl.ds(2 * j + 1, 2)], send2.at[s, k], recv2.at[s, k], west, lat)

    def ids_copy():
        return remote(ids_ref, ids_s, ids_sem.at[0], ids_sem.at[1], east, lat)

    def make_masks():
        lat_total = lat_size * lat_rows
        cols = tokens + 3 * rest
        for j in range(wins):
            base = (lat * lat_rows + j * WIN_LAT).astype(f32)
            key = window_keys(ids_s, j, cols, tokens - rest, rest, levels, base, lat_total)
            kinds = lax.broadcasted_iota(jnp.int32, (16, cols), 0).astype(f32)
            member = (kinds == key).astype(f32).astype(bf16)
            same = lax.dot_general(member[:, :tokens], member, (((0,), (0,)), ((), ())), preferred_element_type=f32)
            mask_s[j] = (same - 1.0) * 1e30

    copies = 3 + wins - 1

    def layer_first(items, first):
        for i, s, j in items:
            x_load(s, j).wait()
        if first:
            loads[0][0].wait()

        for i, s, j in items:
            for half in range(2):
                for block in range(2):
                    for r in range(HALF_LAT):
                        row = (half * 2 + block) * quarter + r * run
                        part = x_s[s, j * WIN_LAT + block * HALF_LAT + r, half * HALF_LON : (half + 1) * HALF_LON]
                        first_s[i, row : row + run, :] = part.reshape(run, width)

        def residual():
            return jnp.concatenate([first_s[i] for i, _, _ in items], axis=0)

        rows = len(items) * tokens
        products = []

        def project(g):
            cut = slice(g * 4 * head_dim, (g + 1) * 4 * head_dim)
            products.append(mm(win_b[:rows, cut], out_s[cut, :]))

        windows = project_windows(residual().astype(bf16), qkv_s.at[0], tokens, head_dim, True)
        for n, window in enumerate(windows):

            def store(cut, value):
                win_b[n * tokens : (n + 1) * tokens, cut] = value.astype(bf16)

            attend_window(
                window,
                scale_s[0:1, :],
                None,
                head_dim,
                store,
                project if n == len(windows) - 1 and not first else None,
            )
        if first:
            for copy in loads[0][1:]:
                copy.wait()
        while len(products) * 4 * head_dim < width:
            project(len(products))
        total = products[0]
        for part in products[1:]:
            total = total + part
        result = finish_window(residual(), total, up_s, down_s, gain_ref[0], bias_ref[0])

        for n, (i, s, j) in enumerate(items):
            mine = result[n * tokens : (n + 1) * tokens]
            first_s[i] = mine

            def block_of(q):
                return mine[q * quarter : (q + 1) * quarter, :].astype(bf16)

            send_s[s, 2 * j] = block_of(2)
            send_s[s, 2 * j + 1] = block_of(3)
            op_s[s, 1, 2 * j] = block_of(1)
            if isinstance(j, int):
                if j == 0:
                    send_own[s, 0] = block_of(0)
                else:
                    op_s[s, 1, 2 * j - 1] = block_of(0)
            else:
                keep_s[...] = block_of(0)

        if first:
            pl.semaphore_wait(barrier, len(peers))
            ids_copy().start()

        for i, s, j in items:

            @when(j == 0)
            def _():
                if not isinstance(j, int):
                    send_own[s, 0] = keep_s[...]
                for k in range(3):
                    ahead(s, k).start()

            for jj in range(1, wins):

                @when(j == jj)
                def _():
                    if not isinstance(j, int):
                        op_s[s, 1, 2 * jj - 1] = keep_s[...]
                    ahead(s, 2 + jj).start()

    def opening(i):
        layer_first([(0, 0, 0)], True)

    def first_window(i):
        layer_first([(i, lax.div(i, wins), lax.rem(i, wins))], False)

    def first_sample(s):
        layer_first([(s * wins + j, s, j) for j in range(wins)], False)

    def shifted_attention(i):
        s, j = lax.div(i, wins), lax.rem(i, wins)

        @pl.when(j == 0)
        def _():
            ahead(s, 0).wait_recv()

        for jj in range(1, wins):

            @pl.when(j == jj - 1)
            def _():
                ahead(s, 2 + jj).wait_recv()

        @pl.when(j == wins - 1)
        def _():
            for k in (1, 2):
                ahead(s, k).wait_recv()

        @pl.when(i == 0)
        def _():
            loads[1][0].wait()
            ids_copy().wait_recv()
            make_masks()

        operand = jnp.concatenate(
            [op_s[s, half, 2 * j + block].astype(f32) for half in range(2) for block in range(2)], axis=0
        ).astype(bf16)

        def store(cut, value):
            parts = [value[q * quarter : (q + 1) * quarter, :].astype(bf16) for q in range(4)]
            back_s[s, 2 * j, :, cut] = parts[0]
            back_s[s, 2 * j + 1, :, cut] = parts[1]
            att_s[s, 0, 2 * j + 1, :, cut] = parts[2]
            keep_s[:, cut] = parts[3]

        window = project_windows(operand, qkv_s.at[1], tokens, head_dim, False)[0]
        attend_window(window, scale_s[1:2, :], mask_s.at[j], head_dim, store)

        @pl.when(j == wins - 1)
        def _():
            back_own[s, 0] = keep_s[...]
            for k in (1, 0, 2):
                back(s, k).start()

        for jj in range(wins - 1):

            @pl.when(j == jj)
            def _():
                att_s[s, 0, 2 * jj + 2] = keep_s[...]
                back(s, 3 + jj).start()

    def layer_last(items):
        for i, s, j in items:

            @when(j == 0)
            def _():
                for k in (1, 2):
                    back(s, k).wait_recv()

            for jj in range(wins - 1):

                @when(j == jj)
                def _():
                    back(s, 3 + jj).wait_recv()

            @when(j == wins - 1)
            def _():
                back(s, 0).wait_recv()

        @pl.when(items[0][0] == 0)
        def _():
            for copy in loads[1][1:]:
                copy.wait()

        attended = jnp.concatenate(
            [att_s[s, half, 2 * j + block].astype(f32) for _, s, j in items for half in range(2) for block in range(2)],
            axis=0,
        ).astype(bf16)
        result = finish_window(
            jnp.concatenate([first_s[i] for i, _, _ in items], axis=0),
            mm(attended, out1_s[...]), up1_s, down1_s, gain_ref[1], bias_ref[1],
        )
        for n, (_, s, j) in enumerate(items):
            for half in range(2):
                for block in range(2):
                    for r in range(HALF_LAT):
                        row = n * tokens + (half * 2 + block) * quarter + r * run
                        x_s[s, j * WIN_LAT + block * HALF_LAT + r, half * HALF_LON : (half + 1) * HALF_LON] = result[
                            row : row + run, :
                        ].reshape(HALF_LON, levels, width)

    def last_window(i):
        layer_last([(i, lax.div(i, wins), lax.rem(i, wins))])

    def last_sample(s):
        layer_last([(s * wins + j, s, j) for j in range(wins)])

    plan = order(samples, wins)
    steps = {"a": opening, "f": first_window, "F": first_sample, "S": shifted_attention, "l": last_window, "L": last_sample}
    kinds = [kind for kind in steps if any(kind == k for k, _ in plan)]

    def pick(t, values):
        value = jnp.int32(values[0])
        for n in range(1, len(values)):
            if values[n] != values[n - 1]:
                value = jnp.where(t >= n, jnp.int32(values[n]), value)
        return value

    def advance(t, carry):
        kind = pick(t, [kinds.index(k) for k, _ in plan])
        n = pick(t, [n for _, n in plan])
        for k, name in enumerate(kinds):

            @pl.when(kind == k)
            def _():
                steps[name](n)

        return carry

    lax.fori_loop(0, len(plan), advance, 0)

    if samples * wins == 1:
        for copy in loads[1][1:]:
            copy.wait()
    if wins == 1:
        for k in (1, 2):
            back(samples - 1, k).wait_recv()
    back(samples - 1, 0).wait_recv()
    first_o[...] = first_s[samples * wins - 1]
    for half in range(2):
        for block in range(2):
            att_o[half, block] = att_s[samples - 1, half, blocks - 2 + block]

    def drain(s, carry):
        for k in range(copies):
            ahead(s, k).wait_send()
            back(s, k).wait_send()
        return carry

    lax.fori_loop(0, samples, drain, 0)
    ids_copy().wait_send()


def closing(x_ref, first_ref, att_ref, out_ref, up_ref, down_ref, gain_ref, bias_ref, y_hbm, last_s, sems):
    samples, lat_rows, lon_cols, levels, width = x_ref.shape
    wins = lat_rows // WIN_LAT
    run = HALF_LON * levels
    quarter = HALF_LAT * run

    def store(src, s, j):
        return pltpu.make_async_copy(src, y_hbm.at[s, pl.ds(j * WIN_LAT, WIN_LAT)], sems.at[s, j])

    copies = [
        store(x_ref.at[s, pl.ds(j * WIN_LAT, WIN_LAT)], s, j)
        for s in range(samples)
        for j in range(wins)
        if s * wins + j < samples * wins - 1
    ]
    for copy in copies:
        copy.start()
    attended = jnp.concatenate(
        [att_ref[half, block].astype(f32) for half in range(2) for block in range(2)], axis=0
    ).astype(bf16)
    result = finish_window(
        first_ref[...], mm(attended, out_ref[...]), up_ref, down_ref, gain_ref[1], bias_ref[1]
    )
    for half in range(2):
        for block in range(2):
            for r in range(HALF_LAT):
                row = (half * 2 + block) * quarter + r * run
                last_s[block * HALF_LAT + r, half * HALF_LON : (half + 1) * HALF_LON] = result[
                    row : row + run, :
                ].reshape(HALF_LON, levels, width)
    copies.append(store(last_s, samples - 1, wins - 1))
    copies[-1].start()
    for copy in copies:
        copy.wait()


def local(stream, region_ids, qkv_weight, out_weight, up_weight, down_weight, norm_gain, norm_bias, logit_scale):
    samples, levels, lat_rows, lon_cols, width = stream.shape
    assert lon_cols == WIN_LON
    wins = lat_rows // WIN_LAT
    blocks = 2 * wins
    quarter = levels * HALF_LAT * HALF_LON
    tokens = 4 * quarter
    copies = 3 + wins - 1
    x = stream.transpose(0, 2, 3, 1, 4)
    ids = region_ids.transpose(1, 0, 2)
    hbm = pl.BlockSpec(memory_space=pl.ANY)
    vmem = pl.BlockSpec(memory_space=pltpu.VMEM)
    smem = pl.BlockSpec(memory_space=pltpu.SMEM)
    sem = pltpu.SemaphoreType.DMA
    handed = [
        pltpu.VMEM(x.shape, f32),
        pltpu.VMEM((tokens, width), f32),
        pltpu.VMEM((2, 2, quarter, width), bf16),
        pltpu.VMEM(out_weight.shape[1:], bf16),
        pltpu.VMEM(up_weight.shape[1:], bf16),
        pltpu.VMEM(down_weight.shape[1:], bf16),
    ]
    parts = pl.pallas_call(
        functools.partial(kernel, lax.axis_size("lat")),
        in_specs=[hbm, vmem, hbm, hbm, hbm, hbm, vmem, vmem, smem],
        out_specs=[vmem] * len(handed),
        out_shape=handed,
        scratch_shapes=[
            pltpu.VMEM((samples * wins, tokens, width), f32),
            pltpu.VMEM((samples, 2, blocks, quarter, width), bf16),
            pltpu.VMEM((samples, 2, blocks, quarter, width), bf16),
            pltpu.VMEM((samples, blocks, quarter, width), bf16),
            pltpu.VMEM((samples, 1, quarter, width), bf16),
            pltpu.VMEM((samples, blocks, quarter, width), bf16),
            pltpu.VMEM((samples, 1, quarter, width), bf16),
            pltpu.VMEM((wins, tokens, tokens + 3 * (width // logit_scale.shape[1] // 2)), f32),
            pltpu.VMEM((quarter, width), bf16),
            pltpu.VMEM((wins * tokens, width), bf16),
            pltpu.VMEM((2, width), f32),
            pltpu.VMEM(qkv_weight.shape, bf16),
            pltpu.VMEM(out_weight.shape[1:], bf16),
            pltpu.VMEM(up_weight.shape[1:], bf16),
            pltpu.VMEM(down_weight.shape[1:], bf16),
            sem((2, 4)),
            sem((samples, wins)),
            sem((samples, copies)),
            sem((samples, copies)),
            sem((samples, copies)),
            sem((samples, copies)),
            pltpu.VMEM(ids.shape, jnp.int32),
            sem((2,)),
        ],
        compiler_params=pltpu.CompilerParams(
            vmem_limit_bytes=VMEM_LIMIT, collective_id=0, has_side_effects=True
        ),
        name="both_layers",
    )(x, ids, qkv_weight, out_weight, up_weight, down_weight, norm_gain, norm_bias, logit_scale)
    y = pl.pallas_call(
        closing,
        in_specs=[vmem] * (len(handed) + 2),
        out_specs=hbm,
        out_shape=jax.ShapeDtypeStruct(x.shape, f32),
        scratch_shapes=[pltpu.VMEM((WIN_LAT,) + x.shape[2:], f32), sem((samples, wins))],
        compiler_params=pltpu.CompilerParams(vmem_limit_bytes=CLOSING_LIMIT),
        name="closing",
    )(*[pltpu.with_memory_space_constraint(part, pltpu.VMEM) for part in parts], norm_gain, norm_bias)
    return y.transpose(0, 3, 1, 2, 4)


def solution(mesh):
    in_specs = (P("ens", None, "lat", "lon", None), P("ens", "lat", "lon")) + (P(),) * 7
    out_specs = P("ens", None, "lat", "lon", None)
    return jax.shard_map(local, mesh=mesh, in_specs=in_specs, out_specs=out_specs, check_vma=False)
```

```python
import functools

import jax
import jax.numpy as jnp
from jax import lax
from jax.experimental import pallas as pl
from jax.experimental.pallas import tpu as pltpu
from jax.sharding import PartitionSpec as P

WIN_LAT = 6
WIN_LON = 12
HALF_LAT = WIN_LAT // 2
HALF_LON = WIN_LON // 2
LOG2E = 1.4426950408889634
VMEM_LIMIT = 51 * 1024 * 1024 + 512 * 1024
CLOSING_LIMIT = 40 * 1024 * 1024

f32 = jnp.float32
bf16 = jnp.bfloat16


MESH = pl.DeviceIdType.MESH


def mm(a, b):
    return jnp.dot(a, b, preferred_element_type=f32)


def head_blocks(group, head_dim):
    d0 = lax.broadcasted_iota(jnp.int32, (group, group), 0)
    d1 = lax.broadcasted_iota(jnp.int32, (group, group), 1)
    shift = head_dim.bit_length() - 1
    same_head = lax.shift_right_logical(d0, shift) == lax.shift_right_logical(d1, shift)
    return same_head.astype(f32).astype(bf16)


def when(condition):
    if isinstance(condition, bool):
        return (lambda run: run()) if condition else (lambda run: None)
    return pl.when(condition)


def project_windows(operand, qkv_weight, tokens, head_dim, joint):
    rows, width = operand.shape
    group = 4 * head_dim
    groups = width // group
    same_head = head_blocks(group, head_dim)

    def project(block, g):
        at = block * width + g * group
        return mm(operand, qkv_weight[:, at : at + group])

    def square(part):
        rounded = part.astype(bf16)
        return rounded * rounded

    raw = [(project(0, g), project(1, g)) for g in range(groups)]
    if joint:
        every = mm(jnp.concatenate([square(part) for g in range(groups) for part in raw[g]], axis=0), same_head)
        sums = [[every[(2 * g + n) * rows : (2 * g + n + 1) * rows] for n in range(2)] for g in range(groups)]
    else:
        sums = [[mm(square(part), same_head) for part in raw[g]] for g in range(groups)]
    value = [project(2, g).astype(bf16) for g in range(groups)]
    windows = []
    for at in range(0, rows, tokens):
        cut = slice(at, at + tokens)
        windows.append(
            (
                [[part[cut] for part in raw[g]] for g in range(groups)],
                [[part[cut] for part in sums[g]] for g in range(groups)],
                [part[cut] for part in value],
            )
        )
    return windows


def attend_window(projected, scale_row, bias_ref, head_dim, store, between=None):
    raw, sums, value = projected
    tokens = value[0].shape[0]
    width = sum(part.shape[1] for part in value)
    group = 4 * head_dim
    pair = 2 * head_dim
    rest = pair // 4
    main = tokens - rest
    last = (((1,), (1,)), ((), ()))
    groups = width // group

    def lanes(rows, cols, at, size):
        lane = lax.broadcasted_iota(jnp.int32, (rows, cols), 1)
        return ((lane >= at) & (lane < at + size)).astype(f32).astype(bf16)

    first_b = lanes(tokens, pair, 0, head_dim)
    second_b = lanes(tokens, pair, head_dim, head_dim)
    first = lax.broadcasted_iota(jnp.int32, (tokens, pair), 1) < head_dim

    def unit(part, total, scale):
        inv = lax.rsqrt(total + 1e-06)
        if scale is not None:
            inv = inv * scale
        return (part * inv).astype(bf16)

    def rest_shares(q, k):
        k_rest = jnp.concatenate(
            [k[main:] * lanes(rest, group, h * head_dim, head_dim) for h in range(4)], axis=0
        )
        score = lax.dot_general(q, k_rest, last, preferred_element_type=f32)
        if bias_ref is not None:
            score = score + bias_ref[:, main:]
        return jnp.exp2(score).astype(bf16)

    def rest_part(weights, v):
        columns = []
        for h in range(4):
            side = h % 2
            own, other = (first_b, second_b)[side][:rest], (second_b, first_b)[side][:rest]
            v_rest = v[main:, (h // 2) * pair : (h // 2 + 1) * pair] * own + other
            zero = jnp.zeros_like(v_rest)
            columns.append(jnp.concatenate([v_rest if i == h else zero for i in range(4)], axis=0))
        return mm(weights, jnp.concatenate(columns, axis=1))

    def main_share(q, k, h):
        cut = slice((h // 2) * pair, (h // 2 + 1) * pair)
        own = (first_b, second_b)[h % 2][:main]
        score = lax.dot_general(q[:, cut], k[:main, cut] * own, last, preferred_element_type=f32)
        if bias_ref is not None:
            score = score + bias_ref[:, :main]
        return jnp.exp2(score).astype(bf16)

    def main_part(share, v, h):
        cut = slice((h // 2) * pair, (h // 2 + 1) * pair)
        own, other = ((first_b, second_b), (second_b, first_b))[h % 2]
        return mm(share, v[:main, cut] * own[:main] + other[:main])

    def combine(g, p, even, odd):
        result = jnp.where(first, even, odd)
        total = pltpu.roll(jnp.where(first, odd, even), head_dim, 1)
        at = g * group + p * pair
        store(slice(at, at + pair), result / total)

    units = [None] * groups

    def scaled(g):
        at = g * group
        return (
            unit(raw[g][0], sums[g][0], scale_row[:, at : at + group]),
            unit(raw[g][1], sums[g][1], None),
        )

    units[0] = scaled(0)

    shares = [rest_shares(*units[0])] + [main_share(*units[0], h) for h in range(4)]
    for g in range(groups):
        following = g + 1 < groups
        if following:
            units[g + 1] = scaled(g + 1)
        ahead = []
        rest_out = rest_part(shares[0], value[g])
        if following:
            ahead.append(rest_shares(*units[g + 1]))
        elif between is not None and g > 0:
            between(g - 1)
        parts = []
        for h in range(4):
            parts.append(main_part(shares[1 + h], value[g], h) + rest_out[:, h * pair : (h + 1) * pair])
            if following:
                ahead.append(main_share(*units[g + 1], h))
            if h % 2 == 1:
                combine(g, h // 2, parts[h - 1], parts[h])
        shares = ahead


def scale_lanes(scale_ref, layer, width, heads):
    lane = lax.broadcasted_iota(jnp.int32, (1, width), 1)
    row = jnp.zeros((1, width), f32)
    for h in range(heads):
        row = jnp.where(lane >= h * (width // heads), scale_ref[layer, h] * LOG2E, row)
    return row


def norm_rows(values, gain_row, bias_row):
    average = jnp.mean(values, -1, keepdims=True)
    centred = values - average
    spread = jnp.mean(centred * centred, -1, keepdims=True)
    return centred * (lax.rsqrt(spread + 1e-05)) * gain_row + bias_row


def gelu_twice(x):
    c = 0.7978845608028654
    x = x.astype(bf16)
    one = jnp.ones((), bf16)
    inner = x * (jnp.asarray(c, bf16) + jnp.asarray(c * 0.044715, bf16) * (x * x))
    return x * (one + jnp.tanh(inner))


def finish_window(x, projected, up_ref, down_ref, gain, bias):
    after = x + norm_rows(projected, gain[0:1], bias[0:1])
    after_b = after.astype(bf16)
    ff = up_ref.shape[1]
    step = min(512, ff)
    hidden = [gelu_twice(mm(after_b, up_ref[:, at : at + step])) for at in range(0, ff, step)]
    total = mm(jnp.concatenate(hidden, axis=1), down_ref[...])
    return after + norm_rows(0.5 * total, gain[1:2], bias[1:2])


def window_keys(ids_ref, j, cols, main, rest, levels, base, lat_total):
    run = HALF_LON * levels
    quarter = HALF_LAT * run
    shape = (1, cols)
    at = lax.broadcasted_iota(jnp.int32, shape, 1)
    t = jnp.where(at < main, at, main + ((at - main) & (rest - 1))).astype(f32)

    def cut(value, by):
        return jnp.floor((value + 0.5) * (1.0 / by))

    q = cut(t, quarter)
    half = cut(q, 2)
    block = q - 2 * half
    inside = t - quarter * q
    r = cut(inside, run)
    column = half * HALF_LON + cut(inside - run * r, levels)
    row = base + block * HALF_LAT + r
    key = jnp.zeros(shape, f32)
    ids = ids_ref[j * WIN_LAT, 0:1, :].astype(f32)
    for c in range(WIN_LON):
        key = jnp.where(column == c, ids[:, c : c + 1], key)
    band = jnp.where(row >= lat_total - WIN_LAT, 1.0, 0.0) + jnp.where(row >= lat_total - HALF_LAT, 1.0, 0.0)
    return key * 3 + band


def order(samples, wins):
    plan = []
    for k in range(samples + 2):
        for s, kind in ((k, "f"), (k - 1, "S"), (k - 2, "l")):
            if 0 <= s < samples:
                if kind == "l" and s < samples - 1:
                    plan.append(("L", s))
                else:
                    plan += [(kind, s * wins + j) for j in range(wins)]
    plan[0] = ("a", 0)
    return plan[:-1]


def kernel(lat_size, x_hbm, ids_ref, qkv_hbm, out_hbm, up_hbm, down_hbm, gain_ref, bias_ref, scale_ref,
           x_s, first_o, att_o, out1_s, up1_s, down1_s, first_s, op_s, att_s, send_s, send_own, back_s, back_own, mask_s, keep_s, win_b,
           scale_s, qkv_s, out_s, up_s, down_s, w_sem, x_sem, send1, recv1, send2, recv2, ids_s, ids_sem):
    samples, lat_rows, lon_cols, levels, width = x_s.shape
    wins = lat_rows // WIN_LAT
    blocks = 2 * wins
    run = HALF_LON * levels
    quarter = HALF_LAT * run
    last_block = blocks - 1

    loads = [
        [
            pltpu.make_async_copy(src.at[layer], dst, w_sem.at[layer, k])
            for k, (src, dst) in enumerate(zip((qkv_hbm, out_hbm, up_hbm, down_hbm), targets))
        ]
        for layer, targets in enumerate(
            ((qkv_s.at[0], out_s, up_s, down_s), (qkv_s.at[1], out1_s, up1_s, down1_s))
        )
    ]

    def x_load(s, j):
        rows = pl.ds(j * WIN_LAT, WIN_LAT)
        return pltpu.make_async_copy(x_hbm.at[s, rows], x_s.at[s, rows], x_sem.at[s, j])

    x_load(0, 0).start()
    for copy in loads[0]:
        copy.start()
    for s in range(samples):
        for j in range(wins):
            if s + j > 0:
                x_load(s, j).start()
    for copy in loads[1]:
        copy.start()

    lon, lat = lax.axis_index("lon"), lax.axis_index("lat")
    lon_size = lax.axis_size("lon")
    west = lax.rem(lon + lon_size - 1, lon_size)
    east = lax.rem(lon + 1, lon_size)
    before = lax.rem(lat + lat_size - 1, lat_size)
    after = lax.rem(lat + 1, lat_size)

    barrier = pltpu.get_barrier_semaphore()
    peers = ((east, lat), (east, before), (lon, before), (lon, after), (west, lat), (west, after))
    for to_lon, to_lat in peers:
        pl.semaphore_signal(barrier, inc=1, device_id={"lon": to_lon, "lat": to_lat}, device_id_type=MESH)

    heads = scale_ref.shape[1]
    head_dim = width // heads
    rest = head_dim // 2
    tokens = 4 * quarter
    for layer in range(2):
        scale_s[layer : layer + 1, :] = scale_lanes(scale_ref, layer, width, heads)

    def remote(src, dst, send, recv, to_lon, to_lat):
        return pltpu.make_async_remote_copy(
            src_ref=src, dst_ref=dst, send_sem=send, recv_sem=recv,
            device_id={"lon": to_lon, "lat": to_lat}, device_id_type=MESH,
        )

    def ahead(s, k):
        if k == 0:
            return remote(send_s.at[s, pl.ds(1, 1)], op_s.at[s, 0, pl.ds(0, 1)], send1.at[s, k], recv1.at[s, k], east, lat)
        if k == 1:
            return remote(send_s.at[s, pl.ds(0, 1)], op_s.at[s, 0, pl.ds(last_block, 1)], send1.at[s, k], recv1.at[s, k], east, before)
        if k == 2:
            return remote(send_own.at[s], op_s.at[s, 1, pl.ds(last_block, 1)], send1.at[s, k], recv1.at[s, k], lon, before)
        j = k - 2
        return remote(send_s.at[s, pl.ds(2 * j, 2)], op_s.at[s, 0, pl.ds(2 * j - 1, 2)], send1.at[s, k], recv1.at[s, k], east, lat)

    def back(s, k):
        if k == 0:
            return remote(back_s.at[s, pl.ds(last_block - 1, 1)], att_s.at[s, 1, pl.ds(last_block, 1)], send2.at[s, k], recv2.at[s, k], west, lat)
        if k == 1:
            return remote(back_s.at[s, pl.ds(last_block, 1)], att_s.at[s, 1, pl.ds(0, 1)], send2.at[s, k], recv2.at[s, k], west, after)
        if k == 2:
            return remote(back_own.at[s], att_s.at[s, 0, pl.ds(0, 1)], send2.at[s, k], recv2.at[s, k], lon, after)
        j = k - 3
        return remote(back_s.at[s, pl.ds(2 * j, 2)], att_s.at[s, 1, pl.ds(2 * j + 1, 2)], send2.at[s, k], recv2.at[s, k], west, lat)

    def ids_copy():
        return remote(ids_ref, ids_s, ids_sem.at[0], ids_sem.at[1], east, lat)

    def make_masks():
        lat_total = lat_size * lat_rows
        cols = tokens + 3 * rest
        for j in range(wins):
            base = (lat * lat_rows + j * WIN_LAT).astype(f32)
            key = window_keys(ids_s, j, cols, tokens - rest, rest, levels, base, lat_total)
            kinds = lax.broadcasted_iota(jnp.int32, (16, cols), 0).astype(f32)
            member = (kinds == key).astype(f32).astype(bf16)
            same = lax.dot_general(member[:, :tokens], member, (((0,), (0,)), ((), ())), preferred_element_type=f32)
            mask_s[j] = (same - 1.0) * 1e30

    copies = 3 + wins - 1

    def layer_first(items, first):
        for i, s, j in items:
            x_load(s, j).wait()
        if first:
            loads[0][0].wait()

        for i, s, j in items:
            for half in range(2):
                for block in range(2):
                    for r in range(HALF_LAT):
                        row = (half * 2 + block) * quarter + r * run
                        part = x_s[s, j * WIN_LAT + block * HALF_LAT + r, half * HALF_LON : (half + 1) * HALF_LON]
                        first_s[i, row : row + run, :] = part.reshape(run, width)

        def residual():
            return jnp.concatenate([first_s[i] for i, _, _ in items], axis=0)

        rows = len(items) * tokens
        products = []

        def project(g):
            cut = slice(g * 4 * head_dim, (g + 1) * 4 * head_dim)
            products.append(mm(win_b[:rows, cut], out_s[cut, :]))

        windows = project_windows(residual().astype(bf16), qkv_s.at[0], tokens, head_dim, True)
        for n, window in enumerate(windows):

            def store(cut, value):
                win_b[n * tokens : (n + 1) * tokens, cut] = value.astype(bf16)

            attend_window(
                window,
                scale_s[0:1, :],
                None,
                head_dim,
                store,
                project if n == len(windows) - 1 and not first else None,
            )
        if first:
            for copy in loads[0][1:]:
                copy.wait()
        while len(products) * 4 * head_dim < width:
            project(len(products))
        total = products[0]
        for part in products[1:]:
            total = total + part
        result = finish_window(residual(), total, up_s, down_s, gain_ref[0], bias_ref[0])

        for n, (i, s, j) in enumerate(items):
            mine = result[n * tokens : (n + 1) * tokens]
            first_s[i] = mine

            def block_of(q):
                return mine[q * quarter : (q + 1) * quarter, :].astype(bf16)

            send_s[s, 2 * j] = block_of(2)
            send_s[s, 2 * j + 1] = block_of(3)
            op_s[s, 1, 2 * j] = block_of(1)
            if isinstance(j, int):
                if j == 0:
                    send_own[s, 0] = block_of(0)
                else:
                    op_s[s, 1, 2 * j - 1] = block_of(0)
            else:
                keep_s[...] = block_of(0)

        if first:
            pl.semaphore_wait(barrier, len(peers))
            ids_copy().start()

        for i, s, j in items:

            @when(j == 0)
            def _():
                if not isinstance(j, int):
                    send_own[s, 0] = keep_s[...]
                for k in range(3):
                    ahead(s, k).start()

            for jj in range(1, wins):

                @when(j == jj)
                def _():
                    if not isinstance(j, int):
                        op_s[s, 1, 2 * jj - 1] = keep_s[...]
                    ahead(s, 2 + jj).start()

    def opening(i):
        layer_first([(0, 0, 0)], True)

    def first_window(i):
        layer_first([(i, lax.div(i, wins), lax.rem(i, wins))], False)

    def first_sample(s):
        layer_first([(s * wins + j, s, j) for j in range(wins)], False)

    def shifted_attention(i):
        s, j = lax.div(i, wins), lax.rem(i, wins)

        @pl.when(j == 0)
        def _():
            ahead(s, 0).wait_recv()

        for jj in range(1, wins):

            @pl.when(j == jj - 1)
            def _():
                ahead(s, 2 + jj).wait_recv()

        @pl.when(j == wins - 1)
        def _():
            for k in (1, 2):
                ahead(s, k).wait_recv()

        @pl.when(i == 0)
        def _():
            loads[1][0].wait()
            ids_copy().wait_recv()
            make_masks()

        operand = jnp.concatenate(
            [op_s[s, half, 2 * j + block].astype(f32) for half in range(2) for block in range(2)], axis=0
        ).astype(bf16)

        def store(cut, value):
            parts = [value[q * quarter : (q + 1) * quarter, :].astype(bf16) for q in range(4)]
            back_s[s, 2 * j, :, cut] = parts[0]
            back_s[s, 2 * j + 1, :, cut] = parts[1]
            att_s[s, 0, 2 * j + 1, :, cut] = parts[2]
            keep_s[:, cut] = parts[3]

        window = project_windows(operand, qkv_s.at[1], tokens, head_dim, False)[0]
        attend_window(window, scale_s[1:2, :], mask_s.at[j], head_dim, store)

        @pl.when(j == wins - 1)
        def _():
            back_own[s, 0] = keep_s[...]
            for k in (1, 0, 2):
                back(s, k).start()

        for jj in range(wins - 1):

            @pl.when(j == jj)
            def _():
                att_s[s, 0, 2 * jj + 2] = keep_s[...]
                back(s, 3 + jj).start()

    def layer_last(items):
        for i, s, j in items:

            @when(j == 0)
            def _():
                for k in (1, 2):
                    back(s, k).wait_recv()

            for jj in range(wins - 1):

                @when(j == jj)
                def _():
                    back(s, 3 + jj).wait_recv()

            @when(j == wins - 1)
            def _():
                back(s, 0).wait_recv()

        @pl.when(items[0][0] == 0)
        def _():
            for copy in loads[1][1:]:
                copy.wait()

        attended = jnp.concatenate(
            [att_s[s, half, 2 * j + block].astype(f32) for _, s, j in items for half in range(2) for block in range(2)],
            axis=0,
        ).astype(bf16)
        result = finish_window(
            jnp.concatenate([first_s[i] for i, _, _ in items], axis=0),
            mm(attended, out1_s[...]), up1_s, down1_s, gain_ref[1], bias_ref[1],
        )
        for n, (_, s, j) in enumerate(items):
            for half in range(2):
                for block in range(2):
                    for r in range(HALF_LAT):
                        row = n * tokens + (half * 2 + block) * quarter + r * run
                        x_s[s, j * WIN_LAT + block * HALF_LAT + r, half * HALF_LON : (half + 1) * HALF_LON] = result[
                            row : row + run, :
                        ].reshape(HALF_LON, levels, width)

    def last_window(i):
        layer_last([(i, lax.div(i, wins), lax.rem(i, wins))])

    def last_sample(s):
        layer_last([(s * wins + j, s, j) for j in range(wins)])

    plan = order(samples, wins)
    steps = {"a": opening, "f": first_window, "F": first_sample, "S": shifted_attention, "l": last_window, "L": last_sample}
    kinds = [kind for kind in steps if any(kind == k for k, _ in plan)]

    def pick(t, values):
        value = jnp.int32(values[0])
        for n in range(1, len(values)):
            if values[n] != values[n - 1]:
                value = jnp.where(t >= n, jnp.int32(values[n]), value)
        return value

    def advance(t, carry):
        kind = pick(t, [kinds.index(k) for k, _ in plan])
        n = pick(t, [n for _, n in plan])
        for k, name in enumerate(kinds):

            @pl.when(kind == k)
            def _():
                steps[name](n)

        return carry

    lax.fori_loop(0, len(plan), advance, 0)

    if samples * wins == 1:
        for copy in loads[1][1:]:
            copy.wait()
    if wins == 1:
        for k in (1, 2):
            back(samples - 1, k).wait_recv()
    back(samples - 1, 0).wait_recv()
    first_o[...] = first_s[samples * wins - 1]
    for half in range(2):
        for block in range(2):
            att_o[half, block] = att_s[samples - 1, half, blocks - 2 + block]

    def drain(s, carry):
        for k in range(copies):
            ahead(s, k).wait_send()
            back(s, k).wait_send()
        return carry

    lax.fori_loop(0, samples, drain, 0)
    ids_copy().wait_send()


def closing(x_ref, first_ref, att_ref, out_ref, up_ref, down_ref, gain_ref, bias_ref, y_hbm, last_s, sems):
    samples, lat_rows, lon_cols, levels, width = x_ref.shape
    wins = lat_rows // WIN_LAT
    run = HALF_LON * levels
    quarter = HALF_LAT * run

    def store(src, s, j):
        return pltpu.make_async_copy(src, y_hbm.at[s, pl.ds(j * WIN_LAT, WIN_LAT)], sems.at[s, j])

    copies = [
        store(x_ref.at[s, pl.ds(j * WIN_LAT, WIN_LAT)], s, j)
        for s in range(samples)
        for j in range(wins)
        if s * wins + j < samples * wins - 1
    ]
    for copy in copies:
        copy.start()
    attended = jnp.concatenate(
        [att_ref[half, block].astype(f32) for half in range(2) for block in range(2)], axis=0
    ).astype(bf16)
    result = finish_window(
        first_ref[...], mm(attended, out_ref[...]), up_ref, down_ref, gain_ref[1], bias_ref[1]
    )
    for half in range(2):
        for block in range(2):
            for r in range(HALF_LAT):
                row = (half * 2 + block) * quarter + r * run
                last_s[block * HALF_LAT + r, half * HALF_LON : (half + 1) * HALF_LON] = result[
                    row : row + run, :
                ].reshape(HALF_LON, levels, width)
    copies.append(store(last_s, samples - 1, wins - 1))
    copies[-1].start()
    for copy in copies:
        copy.wait()


def local(stream, region_ids, qkv_weight, out_weight, up_weight, down_weight, norm_gain, norm_bias, logit_scale):
    samples, levels, lat_rows, lon_cols, width = stream.shape
    assert lon_cols == WIN_LON
    wins = lat_rows // WIN_LAT
    blocks = 2 * wins
    quarter = levels * HALF_LAT * HALF_LON
    tokens = 4 * quarter
    copies = 3 + wins - 1
    x = stream.transpose(0, 2, 3, 1, 4)
    ids = region_ids.transpose(1, 0, 2)
    hbm = pl.BlockSpec(memory_space=pl.ANY)
    vmem = pl.BlockSpec(memory_space=pltpu.VMEM)
    smem = pl.BlockSpec(memory_space=pltpu.SMEM)
    sem = pltpu.SemaphoreType.DMA
    handed = [
        pltpu.VMEM(x.shape, f32),
        pltpu.VMEM((tokens, width), f32),
        pltpu.VMEM((2, 2, quarter, width), bf16),
        pltpu.VMEM(out_weight.shape[1:], bf16),
        pltpu.VMEM(up_weight.shape[1:], bf16),
        pltpu.VMEM(down_weight.shape[1:], bf16),
    ]
    parts = pl.pallas_call(
        functools.partial(kernel, lax.axis_size("lat")),
        in_specs=[hbm, vmem, hbm, hbm, hbm, hbm, vmem, vmem, smem],
        out_specs=[vmem] * len(handed),
        out_shape=handed,
        scratch_shapes=[
            pltpu.VMEM((samples * wins, tokens, width), f32),
            pltpu.VMEM((samples, 2, blocks, quarter, width), bf16),
            pltpu.VMEM((samples, 2, blocks, quarter, width), bf16),
            pltpu.VMEM((samples, blocks, quarter, width), bf16),
            pltpu.VMEM((samples, 1, quarter, width), bf16),
            pltpu.VMEM((samples, blocks, quarter, width), bf16),
            pltpu.VMEM((samples, 1, quarter, width), bf16),
            pltpu.VMEM((wins, tokens, tokens + 3 * (width // logit_scale.shape[1] // 2)), f32),
            pltpu.VMEM((quarter, width), bf16),
            pltpu.VMEM((wins * tokens, width), bf16),
            pltpu.VMEM((2, width), f32),
            pltpu.VMEM(qkv_weight.shape, bf16),
            pltpu.VMEM(out_weight.shape[1:], bf16),
            pltpu.VMEM(up_weight.shape[1:], bf16),
            pltpu.VMEM(down_weight.shape[1:], bf16),
            sem((2, 4)),
            sem((samples, wins)),
            sem((samples, copies)),
            sem((samples, copies)),
            sem((samples, copies)),
            sem((samples, copies)),
            pltpu.VMEM(ids.shape, jnp.int32),
            sem((2,)),
        ],
        compiler_params=pltpu.CompilerParams(
            vmem_limit_bytes=VMEM_LIMIT, collective_id=0, has_side_effects=True
        ),
        name="both_layers",
    )(x, ids, qkv_weight, out_weight, up_weight, down_weight, norm_gain, norm_bias, logit_scale)
    y = pl.pallas_call(
        closing,
        in_specs=[vmem] * (len(handed) + 2),
        out_specs=hbm,
        out_shape=jax.ShapeDtypeStruct(x.shape, f32),
        scratch_shapes=[pltpu.VMEM((WIN_LAT,) + x.shape[2:], f32), sem((samples, wins))],
        compiler_params=pltpu.CompilerParams(vmem_limit_bytes=CLOSING_LIMIT),
        name="closing",
    )(*[pltpu.with_memory_space_constraint(part, pltpu.VMEM) for part in parts], norm_gain, norm_bias)
    return y.transpose(0, 3, 1, 2, 4)


def solution(mesh):
    in_specs = (P("ens", None, "lat", "lon", None), P("ens", "lat", "lon")) + (P(),) * 7
    out_specs = P("ens", None, "lat", "lon", None)
    return jax.shard_map(local, mesh=mesh, in_specs=in_specs, out_specs=out_specs, check_vma=False)
```
